32 devices in a mesh: dp: 16 (over z, y, core), tensor: 2 (over x).
Axes of the slice: x: 2, y: 2, z: 4, core: 2. Of those that a mesh axis runs over, the one named last changes fastest.
Arguments:
- tokens: bfloat16 [32768, 768], P(('dp', 'tensor')), may hold values from -6 to 6
- out_grad: bfloat16 [32768, 768], P(('dp', 'tensor')), may hold values from -6 to 6
- seq_lengths: int32 [48], replicated, may hold values from 1 to 1024, 32768 in all
- deal_order: int32 [48], replicated, may hold values from 0 to 47, each once
- input_weight: float32 [2, 3, 768, 768], P(None, None, 'dp', 'tensor'), may hold values from -0.21875 to 0.21875
- output_weight: float32 [2, 768, 768], P(None, 'tensor', 'dp'), may hold values from -0.21875 to 0.21875
- up_projection_weight: float32 [2, 768, 3072], P(None, 'dp', 'tensor'), may hold values from -0.21875 to 0.21875
- down_projection_weight: float32 [2, 3072, 768], P(None, 'tensor', 'dp'), may hold values from -0.109375 to 0.109375
- input_bias: float32 [2, 3, 768], replicated, may hold values from -2 to 2
- short_taps: float32 [2, 3, 3, 768], replicated, may hold values from -3 to 3
- filter_first: float32 [2, 33, 64], replicated, may hold values from -1 to 1
- filter_inner: float32 [2, 2, 64, 64], replicated, may hold values from -0.75 to 0.75
- filter_biases: float32 [2, 3, 64], replicated, may hold values from -3 to 3
- filter_rates: float32 [2, 3, 64], replicated, may hold values from 0.1 to 1.9
- filter_out: float32 [2, 64, 768], replicated, may hold values from -0.09375 to 0.09375
- conv_bias: float32 [2, 768], replicated, may hold values from -4 to 4
- norm_gains: float32 [2, 2, 768], replicated, may hold values from 0.5 to 1.5
- norm_biases: float32 [2, 2, 768], replicated, may hold values from -2 to 2
- output_biases: float32 [2, 2, 768], replicated, may hold values from -2 to 2
- up_projection_bias: float32 [2, 3072], replicated, may hold values from -2 to 2
Outputs:
- out_first: bfloat16 [32768, 768], P(('dp', 'tensor'))
- out_second: bfloat16 [32768, 768], P(('dp', 'tensor'))
- in_grad: bfloat16 [32768, 768], P(('dp', 'tensor'))
- in_weight_grad: float32 [2, 3, 768, 768], P(None, None, 'dp', 'tensor')
- out_weight_grad: float32 [2, 768, 768], P(None, 'tensor', 'dp')
- up_weight_grad: float32 [2, 768, 3072], P(None, 'dp', 'tensor')
- down_weight_grad: float32 [2, 3072, 768], P(None, 'tensor', 'dp')
- in_bias_grad: float32 [2, 3, 768], replicated
- short_taps_grad: float32 [2, 3, 3, 768], replicated
- filter_first_grad: float32 [2, 33, 64], replicated
- filter_inner_grad: float32 [2, 2, 64, 64], replicated
- filter_biases_grad: float32 [2, 3, 64], replicated
- filter_rates_grad: float32 [2, 3, 64], replicated
- filter_out_grad: float32 [2, 64, 768], replicated
- conv_bias_grad: float32 [2, 768], replicated
- norm_gains_grad: float32 [2, 2, 768], replicated
- norm_biases_grad: float32 [2, 2, 768], replicated
- out_biases_grad: float32 [2, 2, 768], replicated
- up_bias_grad: float32 [2, 3072], replicated
The draws below stay inside these ranges and needn't reach their ends.
Inputs may be any that keep to these rules, and one draw needn't show every extreme that they name: `seq_lengths`: lengths of the sequences in slot order; slot k belongs to index k // 3 of dp; they sum to 32768 and the largest is 1024. Slot k holds the sequence of input rank deal_order[k]; every rank once.
All inputs are finite; a program needn't handle non-finite values.
Results may differ from the reference program's by a relative error of at most 0.024.
Values may be sent and summed in bfloat16 or wider, within the bound.
No kernel may reach another device: no remote copies, remote signals or barrier semaphores. Data moves between devices by JAX's collectives and lax.ppermute only.
A program may use at most 576 MiB of HBM per device.

```python
import math
import jax
import jax.numpy as jnp
import numpy as np
from jax import lax

D = 768
FF = 3072
FILT = 64
EMB = 33
LAYERS = 2
LMAX = 1024
SEQ_DEV = 3
NSEQ = 48
TOKENS = 32768


def block_scale(key, extent, cuts, smallest, top_value):
    level = 1.0
    for dim, blocks in cuts:
        heights = jax.random.uniform(jax.random.fold_in(jax.random.fold_in(key, 6), dim), (blocks,), jnp.float32, smallest / len(cuts), top_value / len(cuts))
        level = level * jnp.repeat(jnp.exp(heights), extent[dim] // blocks).reshape((-1,) + (1,) * (len(extent) - 1 - dim))
    return level


def split_up(count, total, bound, lean):
    loads = [(1 << 20) // math.isqrt(standing ** lean) + 1 for standing in range(2, count + 1)]
    surplus, holding = total - bound - (count - 1), [1] * (count - 1)
    while surplus > 0:
        movable = [i for i in range(count - 1) if holding[i] < bound]
        mass, left = sum([loads[i] for i in movable]), surplus
        for i in movable:
            addition = min(bound - holding[i], max(1, left * loads[i] // mass), surplus)
            holding[i] = holding[i] + addition
            surplus = surplus - addition
    return np.array([bound] + holding)


def ragged(key, count, total, bound, lean):
    if count == 2:
        one = jax.random.randint(key, (), max(1, total - bound), min(bound, total - 1) + 1)
        return jnp.stack([one, total - one])
    lengths = jnp.asarray(split_up(count, total, bound, lean), jnp.int32)
    couples = (count - 1) // 2
    donor, sink = lengths[1:1 + 2 * couples:2], lengths[2:2 + 2 * couples:2]
    slack = jnp.minimum(donor - 1, bound - sink)
    shifted = jax.random.randint(jax.random.fold_in(key, 1), (couples,), 0, 1 << 20) % (slack + 1)
    lengths = lengths.at[1:1 + 2 * couples:2].set(donor - shifted).at[2:2 + 2 * couples:2].set(sink + shifted)
    return lengths[jax.random.permutation(jax.random.fold_in(key, 2), count)]


def scatter_about(own_key, dims, scale, reach, shards=(), held_as=jnp.bfloat16):
    entries = scale * jax.random.normal(own_key, dims, jnp.float32)
    if shards:
        entries = entries * block_scale(own_key, dims, shards, -0.22, 0.18)
    return jnp.clip(entries, -reach, reach).astype(held_as)


def setup_inputs(seed: int = 0) -> dict:
    streams_of = jax.random.split(jax.random.key(seed), 21)
    tokens = scatter_about(streams_of[0], (TOKENS, D), 1.0, 6.0, ((0, 32),))
    out_grad = scatter_about(streams_of[1], (TOKENS, D), 1.0, 6.0, ((0, 32),))
    seq_lengths = ragged(streams_of[2], NSEQ, TOKENS, LMAX, 2).astype(jnp.int32)
    deal_order = jax.random.permutation(streams_of[3], NSEQ).astype(jnp.int32)
    input_weight = scatter_about(streams_of[4], (LAYERS, 3, D, D), D ** -0.5, 0.21875, ((2, 16), (3, 2)), jnp.float32)
    output_weight = scatter_about(streams_of[5], (LAYERS, D, D), D ** -0.5, 0.21875, ((1, 2), (2, 16)), jnp.float32)
    up_projection_weight = scatter_about(streams_of[6], (LAYERS, D, FF), D ** -0.5, 0.21875, ((1, 16), (2, 2)), jnp.float32)
    down_projection_weight = scatter_about(streams_of[7], (LAYERS, FF, D), FF ** -0.5, 0.109375, ((1, 2), (2, 16)), jnp.float32)
    input_bias = scatter_about(streams_of[8], (LAYERS, 3, D), 0.3, 2.0, (), jnp.float32)
    short_taps = scatter_about(streams_of[9], (LAYERS, 3, 3, D), 0.5, 3.0, (), jnp.float32)
    filter_first = scatter_about(streams_of[10], (LAYERS, EMB, FILT), EMB ** -0.5, 1.0, (), jnp.float32)
    filter_inner = scatter_about(streams_of[11], (LAYERS, 2, FILT, FILT), FILT ** -0.5, 0.75, (), jnp.float32)
    filter_biases = scatter_about(streams_of[12], (LAYERS, 3, FILT), 0.5, 3.0, (), jnp.float32)
    filter_rates = jnp.clip(1.0 + 0.18 * jax.random.normal(streams_of[13], (LAYERS, 3, FILT), jnp.float32), 0.1, 1.9)
    filter_out = scatter_about(streams_of[14], (LAYERS, FILT, D), (FILT * 64) ** -0.5, 0.09375, (), jnp.float32)
    conv_bias = scatter_about(streams_of[15], (LAYERS, D), 1.0, 4.0, (), jnp.float32)
    norm_gains = jnp.clip(1.0 + 0.1 * jax.random.normal(streams_of[16], (LAYERS, 2, D), jnp.float32), 0.5, 1.5)
    norm_biases = scatter_about(streams_of[17], (LAYERS, 2, D), 0.3, 2.0, (), jnp.float32)
    output_biases = scatter_about(streams_of[18], (LAYERS, 2, D), 0.3, 2.0, (), jnp.float32)
    up_projection_bias = scatter_about(streams_of[19], (LAYERS, FF), 0.3, 2.0, (), jnp.float32)
    return dict(tokens=tokens, out_grad=out_grad, seq_lengths=seq_lengths, deal_order=deal_order, input_weight=input_weight, output_weight=output_weight, up_projection_weight=up_projection_weight, down_projection_weight=down_projection_weight, input_bias=input_bias, short_taps=short_taps, filter_first=filter_first, filter_inner=filter_inner, filter_biases=filter_biases, filter_rates=filter_rates, filter_out=filter_out, conv_bias=conv_bias, norm_gains=norm_gains, norm_biases=norm_biases, output_biases=output_biases, up_projection_bias=up_projection_bias)


@jax.custom_vjp
def lowered_copy(v):
    return lax.optimization_barrier(v.astype(jnp.bfloat16)).astype(jnp.float32)

@jax.custom_vjp
def lowered_backward(v):
    return v

def low_keep(v):
    return (lowered_copy(v), None)

def low_pass(kept, grad):
    return (grad,)

def back_keep(v):
    return (v, None)

def back_low(kept, grad):
    return (lowered_copy(grad),)
lowered_copy.defvjp(low_keep, low_pass)
lowered_backward.defvjp(back_keep, back_low)
highest_accuracy = lax.Precision.HIGHEST
epsilon = 1e-05
shift_value = 0.05

def layer_norm(values, gain, bias):
    middle_state = lax.optimization_barrier(jnp.mean(values, -1, keepdims=True))
    centered = values - middle_state
    spread = lax.optimization_barrier(jnp.mean(centered * centered, -1, keepdims=True))
    return centered * lax.rsqrt(spread + epsilon) * gain + bias

def positions_table(length):
    bands = (EMB - 1) // 2
    ramp = jnp.linspace(0.0, 1.0, length, dtype=jnp.float32)[:, None]
    places = jnp.arange(length, dtype=jnp.float32)[:, None] * (2.0 * math.pi / length)
    levels = jnp.linspace(0.0001, bands - 1, bands, dtype=jnp.float32)[None, :]
    return jnp.concatenate([ramp, jnp.cos(levels * places), -jnp.sin(levels * places)], axis=1)

def decay_table(length, channel_ids):
    ramp = jnp.linspace(0.0, 1.0, length, dtype=jnp.float32)[:, None]
    fastest = math.log(0.01) / 0.3
    slowest = math.log(0.01) / 1.5
    speeds = slowest + (fastest - slowest) * channel_ids.astype(jnp.float32) / (D - 1)
    return jnp.exp(-ramp * jnp.abs(speeds)[None, :]) + shift_value

def filter_hidden(positions, first_w, inner_w, bias_w, rate_w):
    inner = jnp.sin(rate_w[0] * (jnp.dot(positions, first_w, precision=highest_accuracy) + bias_w[0]))
    inner = jnp.sin(rate_w[1] * (jnp.dot(inner, inner_w[0], precision=highest_accuracy) + bias_w[1]))
    return jnp.sin(rate_w[2] * (jnp.dot(inner, inner_w[1], precision=highest_accuracy) + bias_w[2]))

def short_conv(signal, taps):
    once = jnp.pad(signal, ((0, 0), (1, 0), (0, 0)))[:, :-1]
    twice = jnp.pad(signal, ((0, 0), (2, 0), (0, 0)))[:, :-2]
    return taps[0] * signal + taps[1] * once + taps[2] * twice

def slot_starts(seq_lengths, deal_order):
    count = seq_lengths.shape[0]
    match = deal_order[:, None] == jnp.arange(count, dtype=jnp.int32)[None, :]
    by_input = lax.optimization_barrier(jnp.sum(jnp.where(match, seq_lengths[:, None], 0), axis=0)).astype(jnp.int32)
    starts = (jnp.cumsum(by_input) - by_input).astype(jnp.int32)
    return lax.optimization_barrier(jnp.sum(jnp.where(match, starts[None, :], 0), axis=1)).astype(jnp.int32)

def long_conv(signal, kernel):
    size = 2 * LMAX
    product = jnp.fft.rfft(signal, n=size, axis=1) * jnp.fft.rfft(kernel, n=size, axis=0)[None]
    return jnp.fft.irfft(product, n=size, axis=1)[:, :LMAX]

def layer_forward(hidden_state, parameters, residual_layer, kernel):
    slots, length = (hidden_state.shape[0], hidden_state.shape[1])
    normalized_rows = lowered_copy(layer_norm(hidden_state, parameters['norm_gains'][residual_layer, 0], parameters['norm_biases'][residual_layer, 0]))
    projected_rows = lowered_backward(jnp.einsum('wby,kya->wbka', normalized_rows, lowered_copy(parameters['in_weight'][residual_layer]), precision=highest_accuracy)) + parameters['in_bias'][residual_layer]
    mixed = short_conv(projected_rows.reshape(slots, length, 3 * D), parameters['short_taps'][residual_layer].reshape(3, 3 * D)).reshape(slots, length, 3, D)
    signal = mixed[:, :, 1] * mixed[:, :, 2]
    carried = long_conv(signal, kernel) + parameters['conv_bias'][residual_layer] * signal
    mixer_block = lowered_copy(mixed[:, :, 0] * carried)
    middle_state = hidden_state + (lowered_backward(jnp.einsum('jik,kb->jib', mixer_block, lowered_copy(parameters['out_weight'][residual_layer]), precision=highest_accuracy)) + parameters['out_biases'][residual_layer, 0])
    second_layer = lowered_copy(layer_norm(middle_state, parameters['norm_gains'][residual_layer, 1], parameters['norm_biases'][residual_layer, 1]))
    prior_input = lowered_backward(jnp.einsum('eni,iq->enq', second_layer, lowered_copy(parameters['up_weight'][residual_layer]), precision=highest_accuracy)) + parameters['up_bias'][residual_layer]
    gelu_applied = lowered_copy(jax.nn.gelu(prior_input, approximate=False))
    return middle_state + (lowered_backward(jnp.einsum('uiv,vj->uij', gelu_applied, lowered_copy(parameters['down_weight'][residual_layer]), precision=highest_accuracy)) + parameters['out_biases'][residual_layer, 1])

def reference(tokens, out_grad, seq_lengths, deal_order, input_weight, output_weight, up_projection_weight, down_projection_weight, input_bias, short_taps, filter_first, filter_inner, filter_biases, filter_rates, filter_out, conv_bias, norm_gains, norm_biases, output_biases, up_projection_bias):
    pairs = [('in_weight', input_weight), ('out_weight', output_weight), ('up_weight', up_projection_weight), ('down_weight', down_projection_weight), ('in_bias', input_bias), ('short_taps', short_taps), ('filter_first', filter_first), ('filter_inner', filter_inner), ('filter_biases', filter_biases), ('filter_rates', filter_rates), ('filter_out', filter_out), ('conv_bias', conv_bias), ('norm_gains', norm_gains), ('norm_biases', norm_biases), ('out_biases', output_biases), ('up_bias', up_projection_bias)]
    parameters = {}
    for label, value in pairs:
        parameters[label] = value.astype(jnp.float32)
    starts = slot_starts(seq_lengths, deal_order)
    offsets = jnp.arange(LMAX, dtype=jnp.int32)
    live = offsets[None, :] < seq_lengths[:, None]
    source = jnp.where(live, starts[:, None] + offsets[None, :], 0).reshape(-1).astype(jnp.int32)
    live = live.reshape(-1)
    token_ids = jnp.arange(TOKENS, dtype=jnp.int32)[:, None]
    inside = (token_ids >= starts[None, :]) & (token_ids < starts[None, :] + seq_lengths[None, :])
    slot_base = jnp.arange(NSEQ, dtype=jnp.int32)[None, :] * LMAX - starts[None, :]
    row_of = lax.optimization_barrier(jnp.sum(jnp.where(inside, slot_base + token_ids, 0), axis=1)).astype(jnp.int32)
    positions = positions_table(LMAX)
    modulation = decay_table(LMAX, jnp.arange(D, dtype=jnp.int32))

    def model(inputs, weights):
        slots = jnp.where(live[:, None], inputs[source], 0.0).reshape(NSEQ // SEQ_DEV, SEQ_DEV, LMAX, D)
        kernels = []
        for residual_layer in range(LAYERS):
            inner = filter_hidden(positions, weights['filter_first'][residual_layer], weights['filter_inner'][residual_layer], weights['filter_biases'][residual_layer], weights['filter_rates'][residual_layer])
            kernels.append(jnp.dot(inner, weights['filter_out'][residual_layer], precision=highest_accuracy) * modulation)

        def run(block):
            results = []
            hidden_state = block
            for residual_layer in range(LAYERS):
                hidden_state = layer_forward(hidden_state, weights, residual_layer, kernels[residual_layer])
                results.append(hidden_state)
            return (results[0], results[1])
        first, second_layer = lax.map(jax.checkpoint(run), slots)
        return (first.reshape(NSEQ * LMAX, D)[row_of], second_layer.reshape(NSEQ * LMAX, D)[row_of])
    (out_first, out_second), back = jax.vjp(model, tokens.astype(jnp.float32), parameters)
    in_grad, grads = back((jnp.zeros_like(out_first), out_grad.astype(jnp.float32)))
    return (out_first.astype(jnp.bfloat16), out_second.astype(jnp.bfloat16), in_grad.astype(jnp.bfloat16), grads['in_weight'], grads['out_weight'], grads['up_weight'], grads['down_weight'], grads['in_bias'], grads['short_taps'], grads['filter_first'], grads['filter_inner'], grads['filter_biases'], grads['filter_rates'], grads['filter_out'], grads['conv_bias'], grads['norm_gains'], grads['norm_biases'], grads['out_biases'], grads['up_bias'])
```

```python
import functools
import math

import jax
import jax.numpy as jnp
import numpy as np
from jax import lax
from jax.experimental import pallas as pl
from jax.experimental.pallas import tpu as pltpu
from jax.sharding import PartitionSpec as P

D = 768
FF = 3072
EMB = 33
LAYERS = 2
LMAX = 1024
BLK = 128
TAPS = LMAX // BLK
LANES = 384

highest = lax.Precision.HIGHEST
f32 = jnp.float32
bf16 = jnp.bfloat16
epsilon = 1e-05
shift_value = 0.05


def wave_tables():
    waves = (np.arange(BLK) + 0.5)[:, None] * (2.0 * math.pi / (2 * BLK))

    def spectrum(places):
        angle = waves * places[None, :]
        return np.concatenate([np.cos(angle), -np.sin(angle)], axis=0)

    causal = spectrum(np.arange(2 * BLK) - BLK)
    ahead = spectrum(np.arange(2 * BLK))
    single = spectrum(np.arange(BLK))
    back = spectrum(np.arange(BLK)).T / BLK
    return causal, ahead, single, back


def layer_norm_parts(values):
    centered = values - jnp.mean(values, -1, keepdims=True)
    rate = lax.rsqrt(jnp.mean(centered * centered, -1, keepdims=True) + epsilon)
    return centered * rate, rate


def layer_norm_back(grad, scaled, rate, gain):
    g = grad * gain
    return rate * (
        g - jnp.mean(g, -1, keepdims=True) - scaled * jnp.mean(g * scaled, -1, keepdims=True)
    )


def positions_table(length):
    bands = (EMB - 1) // 2
    ramp = jnp.linspace(0.0, 1.0, length, dtype=f32)[:, None]
    places = jnp.arange(length, dtype=f32)[:, None] * (2.0 * math.pi / length)
    levels = jnp.linspace(0.0001, bands - 1, bands, dtype=f32)[None, :]
    return jnp.concatenate([ramp, jnp.cos(levels * places), -jnp.sin(levels * places)], axis=1)


def decay_table(length):
    ramp = jnp.linspace(0.0, 1.0, length, dtype=f32)[:, None]
    fastest = math.log(0.01) / 0.3
    slowest = math.log(0.01) / 1.5
    speeds = slowest + (fastest - slowest) * jnp.arange(D, dtype=jnp.int32).astype(f32) / (D - 1)
    return jnp.exp(-ramp * jnp.abs(speeds)[None, :]) + shift_value


def filter_hidden(positions, first_w, inner_w, bias_w, rate_w):
    inner = jnp.sin(rate_w[0] * (jnp.dot(positions, first_w, precision=highest) + bias_w[0]))
    inner = jnp.sin(rate_w[1] * (jnp.dot(inner, inner_w[0], precision=highest) + bias_w[1]))
    return jnp.sin(rate_w[2] * (jnp.dot(inner, inner_w[1], precision=highest) + bias_w[2]))


def rows_mask(first, count, begin, end):
    rows = first + lax.broadcasted_iota(jnp.int32, (count, 1), 0)
    return (rows >= begin) & (rows < end)


def masked_spectrum(table, block, mask):
    kept = jnp.where(mask, block.astype(f32), 0.0).astype(bf16)
    return jnp.dot(table, kept, preferred_element_type=f32)


def multiply_add(carry, left_re, left_im, right_re, right_im, conj):
    re, im = carry
    if conj:
        return (
            re + (left_re * right_re + left_im * right_im),
            im + (left_re * right_im - left_im * right_re),
        )
    return (
        re + (left_re * right_re - left_im * right_im),
        im + (left_re * right_im + left_im * right_re),
    )


def conv_forward_body(own_block, table, window, kernel, causal, back, out, spectra, total):
    blocks = spectra.shape[0]
    lanes = out.shape[1]
    origin = table[2]

    def segment(n, _):
        begin = table[3 + n] - origin
        end = table[4 + n] - origin
        head = lax.div(begin, BLK)
        tail = jnp.minimum(lax.div(end - 1, BLK), blocks - 1)

        def transform(j, _):
            at = pl.multiple_of(j * BLK, BLK)
            mask = rows_mask(at - BLK, 2 * BLK, begin, end)
            spectra[j] = masked_spectrum(causal[...], window[pl.ds(at, 2 * BLK), :], mask)
            return 0

        lax.fori_loop(head, tail + 1, transform, 0)

        def produce(j, _):
            reach = jnp.minimum(j - head, TAPS - 1) + 1
            for lane in range(0, lanes, 128):
                part = slice(lane, lane + 128)

                def lag(b, carry):
                    return multiply_add(
                        carry,
                        kernel[b, :BLK, part],
                        kernel[b, BLK:, part],
                        spectra[j - b, :BLK, part],
                        spectra[j - b, BLK:, part],
                        False,
                    )

                zero = jnp.zeros((BLK, 128), f32)
                re, im = lax.fori_loop(0, reach, lag, (zero, zero))
                total[:BLK, part] = re.astype(bf16)
                total[BLK:, part] = im.astype(bf16)
            value = jnp.dot(back[...], total[...], preferred_element_type=f32)
            at = pl.multiple_of((j - own_block) * BLK, BLK)
            mask = rows_mask(j * BLK, BLK, begin, end)
            out[pl.ds(at, BLK), :] = jnp.where(mask, value, out[pl.ds(at, BLK), :])
            return 0

        lax.fori_loop(jnp.maximum(head, own_block), tail + 1, produce, 0)
        return 0

    lax.fori_loop(table[0], table[1] + 1, segment, 0)


def conv_backward_body(
    own_block,
    table,
    window,
    grads,
    kernel,
    causal,
    ahead,
    single,
    back,
    signal_grad,
    kernel_grad,
    spectra,
    grad_spectra,
    own_spectra,
    sums,
    total,
):
    blocks = spectra.shape[0]
    grad_blocks = grad_spectra.shape[0]
    own_blocks = own_spectra.shape[0]
    lanes = signal_grad.shape[1]
    origin = table[2]
    sums[...] = jnp.zeros_like(sums)

    def segment(n, _):
        begin = table[3 + n] - origin
        end = table[4 + n] - origin
        head = lax.div(begin, BLK)
        tail = jnp.minimum(lax.div(end - 1, BLK), blocks - 1)
        first = jnp.maximum(head, own_block)
        last = jnp.minimum(lax.div(end - 1, BLK), own_block + grad_blocks - 1)

        def transform(j, _):
            at = pl.multiple_of(j * BLK, BLK)
            mask = rows_mask(at - BLK, 2 * BLK, begin, end)
            spectra[j] = masked_spectrum(causal[...], window[pl.ds(at, 2 * BLK), :], mask)
            return 0

        lax.fori_loop(head, tail + 1, transform, 0)

        def transform_grad(j, _):
            at = pl.multiple_of((j - own_block) * BLK, BLK)
            mask = rows_mask(j * BLK, 2 * BLK, begin, end)
            grad_spectra[j - own_block] = masked_spectrum(
                ahead[...], grads[pl.ds(at, 2 * BLK), :], mask
            )
            return 0

        lax.fori_loop(first, last + 1, transform_grad, 0)

        def transform_own(j, _):
            at = pl.multiple_of((j - own_block) * BLK, BLK)
            mask = rows_mask(j * BLK, BLK, begin, end)
            own_spectra[j - own_block] = masked_spectrum(
                single[...], grads[pl.ds(at, BLK), :], mask
            )
            return 0

        lax.fori_loop(first, tail + 1, transform_own, 0)

        def produce(j, _):
            reach = jnp.minimum(last - j, TAPS - 1) + 1
            for lane in range(0, lanes, 128):
                part = slice(lane, lane + 128)

                def lag(b, carry):
                    at = j - own_block + b
                    return multiply_add(
                        carry,
                        kernel[b, :BLK, part],
                        kernel[b, BLK:, part],
                        grad_spectra[at, :BLK, part],
                        grad_spectra[at, BLK:, part],
                        True,
                    )

                zero = jnp.zeros((BLK, 128), f32)
                re, im = lax.fori_loop(0, reach, lag, (zero, zero))
                total[:BLK, part] = re.astype(bf16)
                total[BLK:, part] = im.astype(bf16)
            value = jnp.dot(back[...], total[...], preferred_element_type=f32)
            at = pl.multiple_of((j - own_block) * BLK, BLK)
            mask = rows_mask(j * BLK, BLK, begin, end)
            signal_grad[pl.ds(at, BLK), :] = jnp.where(
                mask, value, signal_grad[pl.ds(at, BLK), :]
            )
            return 0

        lax.fori_loop(first, tail + 1, produce, 0)

        def accumulate(b, _):
            for lane in range(0, lanes, 128):
                part = slice(lane, lane + 128)

                def at_block(j, carry):
                    return multiply_add(
                        carry,
                        spectra[j - b, :BLK, part],
                        spectra[j - b, BLK:, part],
                        own_spectra[j - own_block, :BLK, part],
                        own_spectra[j - own_block, BLK:, part],
                        True,
                    )

                re, im = lax.fori_loop(
                    jnp.maximum(first, head + b),
                    tail + 1,
                    at_block,
                    (sums[b, :BLK, part], sums[b, BLK:, part]),
                )
                sums[b, :BLK, part] = re
                sums[b, BLK:, part] = im
            return 0

        lax.fori_loop(0, jnp.minimum(tail - head, TAPS - 1) + 1, accumulate, 0)
        return 0

    lax.fori_loop(table[0], table[1] + 1, segment, 0)
    for b in range(TAPS):
        kernel_grad[b * BLK : (b + 1) * BLK, :] = jnp.dot(
            back[...], sums[b].astype(bf16), preferred_element_type=f32
        )


def fixed(shape):
    return pl.BlockSpec(shape, lambda c, table: (0,) * len(shape))


def by_lane(shape):
    return pl.BlockSpec(shape, lambda c, table: (0,) * (len(shape) - 1) + (c,))


def conv_forward(table, window, kernel, rows, tables):
    causal, _, _, back = tables
    wide = window.shape[0]
    blocks = wide // BLK - 1
    own_block = (wide - BLK - rows) // BLK
    return pl.pallas_call(
        functools.partial(conv_forward_body, own_block),
        out_shape=jax.ShapeDtypeStruct((rows, D), f32),
        grid_spec=pltpu.PrefetchScalarGridSpec(
            num_scalar_prefetch=1,
            grid=(D // LANES,),
            in_specs=[
                by_lane((wide, LANES)),
                by_lane((TAPS, 2 * BLK, LANES)),
                fixed((2 * BLK, 2 * BLK)),
                fixed((BLK, 2 * BLK)),
            ],
            out_specs=by_lane((rows, LANES)),
            scratch_shapes=[
                pltpu.VMEM((blocks, 2 * BLK, LANES), f32),
                pltpu.VMEM((2 * BLK, LANES), bf16),
            ],
        ),
        compiler_params=pltpu.CompilerParams(vmem_limit_bytes=40 << 20),
        cost_estimate=pl.CostEstimate(
            flops=4_000_000_000, bytes_accessed=20_000_000, transcendentals=0
        ),
        name="conv_forward",
    )(table, window, kernel, causal, back)


def conv_backward(table, window, grads, kernel, rows, tables):
    causal, ahead, single, back = tables
    wide = window.shape[0]
    blocks = wide // BLK - 1
    grad_blocks = grads.shape[0] // BLK - 1
    own_block = (wide - BLK - rows) // BLK
    return pl.pallas_call(
        functools.partial(conv_backward_body, own_block),
        out_shape=(
            jax.ShapeDtypeStruct((rows, D), f32),
            jax.ShapeDtypeStruct((LMAX, D), f32),
        ),
        grid_spec=pltpu.PrefetchScalarGridSpec(
            num_scalar_prefetch=1,
            grid=(D // LANES,),
            in_specs=[
                by_lane((wide, LANES)),
                by_lane((grads.shape[0], LANES)),
                by_lane((TAPS, 2 * BLK, LANES)),
                fixed((2 * BLK, 2 * BLK)),
                fixed((2 * BLK, 2 * BLK)),
                fixed((2 * BLK, BLK)),
                fixed((BLK, 2 * BLK)),
            ],
            out_specs=(by_lane((rows, LANES)), by_lane((LMAX, LANES))),
            scratch_shapes=[
                pltpu.VMEM((blocks, 2 * BLK, LANES), f32),
                pltpu.VMEM((grad_blocks, 2 * BLK, LANES), f32),
                pltpu.VMEM((rows // BLK, 2 * BLK, LANES), f32),
                pltpu.VMEM((TAPS, 2 * BLK, LANES), f32),
                pltpu.VMEM((2 * BLK, LANES), bf16),
            ],
        ),
        compiler_params=pltpu.CompilerParams(vmem_limit_bytes=50 << 20),
        cost_estimate=pl.CostEstimate(
            flops=8_000_000_000, bytes_accessed=30_000_000, transcendentals=0
        ),
        name="conv_backward",
    )(table, window, grads, kernel, causal, ahead, single, back)


def shards(
    tokens,
    out_grad,
    seq_lengths,
    deal_order,
    input_weight,
    output_weight,
    up_projection_weight,
    down_projection_weight,
    input_bias,
    short_taps,
    filter_first,
    filter_inner,
    filter_biases,
    filter_rates,
    filter_out,
    conv_bias,
    norm_gains,
    norm_biases,
    output_biases,
    up_projection_bias,
):
    tensor_count = lax.axis_size("tensor")
    group_count = lax.axis_size("dp")
    devices = tensor_count * group_count
    rank = lax.axis_index("dp") * tensor_count + lax.axis_index("tensor")
    rows = tokens.shape[0]
    width = input_weight.shape[3]
    hidden = up_projection_weight.shape[2]
    depth = input_weight.shape[2]
    columns = 4 * width + 2 * hidden
    count = seq_lengths.shape[0]
    everyone = ("dp", "tensor")
    owners = ("tensor", "dp")
    hops = -(-(LMAX - 1) // rows)

    def from_before(values, hop=1):
        return lax.ppermute(values, everyone, [(i, i + hop) for i in range(devices - hop)])

    def from_after(values, hop=1):
        return lax.ppermute(values, everyone, [(i + hop, i) for i in range(devices - hop)])

    held = [
        jnp.concatenate(
            [
                jnp.transpose(input_weight[layer].astype(bf16), (1, 0, 2)).reshape(
                    depth, 3 * width
                ),
                jnp.transpose(output_weight[layer].astype(bf16)),
                up_projection_weight[layer].astype(bf16),
                jnp.transpose(down_projection_weight[layer].astype(bf16)),
            ],
            axis=1,
        )
        for layer in range(LAYERS)
    ]
    gathered = [
        lax.all_gather(part, owners, axis=0, tiled=True).reshape(tensor_count, D, columns)
        for part in held
    ]

    def whole(layer, start, parts, size):
        piece = gathered[layer][:, :, start : start + parts * size]
        piece = piece.reshape(tensor_count, D, parts, size)
        return jnp.transpose(piece, (1, 2, 0, 3)).reshape(D, parts * tensor_count * size)

    numbers = jnp.arange(count, dtype=jnp.int32)
    match = deal_order[:, None] == numbers[None, :]
    lengths = jnp.sum(jnp.where(match, seq_lengths[:, None], 0), axis=0)
    ends = jnp.sum(jnp.where(numbers[:, None] <= numbers[None, :], lengths[:, None], 0), axis=0)
    starts = ends - lengths
    base = rank * rows
    first_segment = jnp.sum((starts <= base).astype(jnp.int32)) - 1
    last_segment = jnp.sum((starts < base + rows).astype(jnp.int32)) - 1
    table = jnp.concatenate(
        [
            jnp.stack([first_segment, last_segment, base - hops * rows]),
            starts,
            ends[count - 1 :],
        ]
    ).astype(jnp.int32)
    places = base + jnp.arange(rows + 2, dtype=jnp.int32)
    begun = jnp.max(jnp.where(starts[None, :] <= places[:, None], starts[None, :], 0), axis=1)
    age = places - begun
    after_one = (age >= 1).astype(f32)[:, None]
    after_two = (age >= 2).astype(f32)[:, None]

    causal, ahead, single, back = wave_tables()
    tables = tuple(jnp.asarray(t, f32).astype(bf16) for t in (causal, ahead, single, back))
    positions = positions_table(LMAX)
    modulation = decay_table(LMAX)
    blank = jnp.zeros((BLK, D), bf16)

    filters = []
    for layer in range(LAYERS):
        inner, filter_back = jax.vjp(
            lambda a, b, c, d: filter_hidden(positions, a, b, c, d),
            filter_first[layer],
            filter_inner[layer],
            filter_biases[layer],
            filter_rates[layer],
        )
        kernel = jnp.dot(inner, filter_out[layer], precision=highest) * modulation
        kernel_spectra = jnp.einsum(
            "kr,brc->bkc",
            tables[2],
            kernel.reshape(TAPS, BLK, D).astype(bf16),
            preferred_element_type=f32,
        )
        filters.append((inner, filter_back, kernel_spectra))

    state = tokens.astype(f32)
    kept = []
    outputs = []
    for layer in range(LAYERS):
        in_all = whole(layer, 0, 3, width)
        out_all = whole(layer, 3 * width, 1, width)
        up_all = whole(layer, 4 * width, 1, hidden)
        down_all = whole(layer, 4 * width + hidden, 1, hidden)
        gains, biases = norm_gains[layer], norm_biases[layer]
        before_state = from_before(state[rows - 8 :].astype(f32))
        joined = jnp.concatenate([before_state, state], axis=0)
        scaled, rate = layer_norm_parts(joined)
        normed = (scaled * gains[0] + biases[0]).astype(bf16)
        projected = jnp.dot(normed, in_all, preferred_element_type=f32) + input_bias[
            layer
        ].reshape(3 * D)
        taps = short_taps[layer].reshape(3, 3 * D)
        mixed = (
            taps[0] * projected[8:]
            + taps[1] * projected[7:-1] * after_one[:rows]
            + taps[2] * projected[6:-2] * after_two[:rows]
        )
        gate_out = mixed[:, :D]
        gate_in = mixed[:, D : 2 * D]
        values = mixed[:, 2 * D :]
        signal = gate_in * values
        signal_low = signal.astype(bf16)
        window = jnp.concatenate(
            [blank] + [from_before(signal_low, hop) for hop in range(hops, 0, -1)] + [signal_low]
        )
        carried = (
            conv_forward(table, window, filters[layer][2], rows, tables)
            + conv_bias[layer] * signal
        )
        mixer = (gate_out * carried).astype(bf16)
        middle = (
            state
            + jnp.einsum("rc,dc->rd", mixer, out_all, preferred_element_type=f32)
            + output_biases[layer, 0]
        )
        second_scaled, second_rate = layer_norm_parts(middle)
        second = (second_scaled * gains[1] + biases[1]).astype(bf16)
        before = (
            jnp.dot(second, up_all, preferred_element_type=f32) + up_projection_bias[layer]
        )
        cumulative = 0.5 * (1.0 + lax.erf(before * math.sqrt(0.5)))
        slope = (
            cumulative + before * jnp.exp(-0.5 * before * before) * (1.0 / math.sqrt(2 * math.pi))
        ).astype(bf16)
        activated = (before * cumulative).astype(bf16)
        new_state = (
            middle
            + jnp.einsum("rf,df->rd", activated, down_all, preferred_element_type=f32)
            + output_biases[layer, 1]
        )
        outputs.append(new_state.astype(bf16))
        kept.append(
            (
                in_all, out_all, up_all, down_all, scaled[8:], rate[8:], normed[8:], projected,
                gate_out, gate_in, values, signal, window, carried, mixer, second_scaled,
                second_rate, second, slope, activated,
            )
        )
        state = new_state

    def sum_rows(values):
        return jnp.sum(values, axis=0)

    grad = out_grad.astype(f32)
    owned = [None] * LAYERS
    small = [None] * LAYERS
    for layer in reversed(range(LAYERS)):
        (
            in_all, out_all, up_all, down_all, scaled, rate, normed, projected,
            gate_out, gate_in, values, signal, window, carried, mixer, second_scaled,
            second_rate, second, slope, activated,
        ) = kept[layer]
        gains = norm_gains[layer]
        inner, filter_back, kernel_spectra = filters[layer]
        down_bias_grad = sum_rows(grad)
        grad_low = grad.astype(bf16)
        down_grad = jnp.einsum("rd,rf->df", grad_low, activated, preferred_element_type=f32)
        before_grad = (
            jnp.dot(grad_low, down_all, preferred_element_type=f32) * slope.astype(f32)
        )
        up_bias_grad = sum_rows(before_grad)
        before_low = before_grad.astype(bf16)
        up_grad = jnp.einsum("rd,rf->df", second, before_low, preferred_element_type=f32)
        second_grad = jnp.einsum("rf,df->rd", before_low, up_all, preferred_element_type=f32)
        second_gain_grad = sum_rows(second_grad * second_scaled)
        second_bias_grad = sum_rows(second_grad)
        middle_grad = grad + layer_norm_back(second_grad, second_scaled, second_rate, gains[1])
        mixer_bias_grad = sum_rows(middle_grad)
        middle_low = middle_grad.astype(bf16)
        out_grad_part = jnp.einsum("rd,rc->dc", middle_low, mixer, preferred_element_type=f32)
        mixer_grad = jnp.dot(middle_low, out_all, preferred_element_type=f32)
        carried_grad = mixer_grad * gate_out
        carried_low = carried_grad.astype(bf16)
        grads_window = jnp.concatenate(
            [carried_low] + [from_after(carried_low, hop) for hop in range(1, hops + 1)] + [blank]
        )
        conv_bias_grad = sum_rows(carried_grad * signal)
        signal_grad, kernel_grad = conv_backward(
            table, window, grads_window, kernel_spectra, rows, tables
        )
        signal_grad = signal_grad + conv_bias[layer] * carried_grad
        mixed_grad = jnp.concatenate(
            [mixer_grad * carried, signal_grad * values, signal_grad * gate_in], axis=1
        )
        after = from_after(mixed_grad[:8])
        spread = jnp.concatenate([mixed_grad, after], axis=0)
        taps = short_taps[layer].reshape(3, 3 * D)
        projected_grad = (
            taps[0] * mixed_grad
            + taps[1] * spread[1 : rows + 1] * after_one[1 : rows + 1]
            + taps[2] * spread[2 : rows + 2] * after_two[2 : rows + 2]
        )
        taps_grad = jnp.stack(
            [
                sum_rows(mixed_grad * projected[8:]),
                sum_rows(mixed_grad * projected[7:-1] * after_one[:rows]),
                sum_rows(mixed_grad * projected[6:-2] * after_two[:rows]),
            ]
        )
        in_bias_grad = sum_rows(projected_grad)
        projected_low = projected_grad.astype(bf16)
        in_grad_part = jnp.einsum("rd,rc->dc", normed, projected_low, preferred_element_type=f32)
        first_grad = jnp.einsum("rc,dc->rd", projected_low, in_all, preferred_element_type=f32)
        first_gain_grad = sum_rows(first_grad * scaled)
        first_bias_grad = sum_rows(first_grad)
        grad = middle_grad + layer_norm_back(first_grad, scaled, rate, gains[0])

        def by_owner(whole_grad, parts):
            size = whole_grad.shape[1] // (parts * tensor_count)
            piece = whole_grad.astype(bf16).reshape(D, parts, tensor_count, size)
            return jnp.transpose(piece, (2, 0, 1, 3)).reshape(tensor_count, D, parts * size)

        stacked = jnp.concatenate(
            [
                by_owner(in_grad_part, 3),
                by_owner(out_grad_part, 1),
                by_owner(up_grad, 1),
                by_owner(down_grad, 1),
            ],
            axis=2,
        ).reshape(tensor_count * D, columns)
        owned[layer] = lax.psum_scatter(
            stacked, owners, scatter_dimension=0, tiled=True
        ).astype(f32)

        shaped = kernel_grad * modulation
        filter_out_grad = jnp.dot(jnp.transpose(inner), shaped, precision=highest)
        inner_grad = jnp.dot(shaped, jnp.transpose(filter_out[layer]), precision=highest)
        filter_grads = filter_back(inner_grad)
        small[layer] = (
            in_bias_grad.reshape(3, D),
            taps_grad.reshape(3, 3, D),
            *filter_grads,
            filter_out_grad,
            conv_bias_grad,
            jnp.stack([first_gain_grad, second_gain_grad]),
            jnp.stack([first_bias_grad, second_bias_grad]),
            jnp.stack([mixer_bias_grad, down_bias_grad]),
            up_bias_grad,
        )

    small_stacked = [
        jnp.stack([small[layer][index] for layer in range(LAYERS)])
        for index in range(len(small[0]))
    ]
    sizes = [part.size for part in small_stacked]
    flat = jnp.concatenate([part.reshape(-1) for part in small_stacked])
    unit = 1024
    padded = -(-flat.shape[0] // unit) * unit
    flat = jnp.pad(flat, (0, padded - flat.shape[0])).reshape(padded // 128, 128)
    step = 1
    while step < devices:
        low = flat.astype(bf16)
        other = lax.ppermute(low, everyone, [(i, i ^ step) for i in range(devices)])
        flat = low.astype(f32) + other.astype(f32)
        step *= 2
    flat = flat.reshape(-1)
    summed = []
    offset = 0
    for part, size in zip(small_stacked, sizes):
        summed.append(flat[offset : offset + size].reshape(part.shape))
        offset += size

    in_owned = jnp.stack(
        [
            jnp.transpose(owned[layer][:, : 3 * width].reshape(depth, 3, width), (1, 0, 2))
            for layer in range(LAYERS)
        ]
    )
    out_owned = jnp.stack(
        [jnp.transpose(owned[layer][:, 3 * width : 4 * width]) for layer in range(LAYERS)]
    )
    up_owned = jnp.stack(
        [owned[layer][:, 4 * width : 4 * width + hidden] for layer in range(LAYERS)]
    )
    down_owned = jnp.stack(
        [jnp.transpose(owned[layer][:, 4 * width + hidden :]) for layer in range(LAYERS)]
    )
    return (
        outputs[0],
        outputs[1],
        grad.astype(bf16),
        in_owned,
        out_owned,
        up_owned,
        down_owned,
        *summed,
    )


def solution(mesh):
    rows = P(("dp", "tensor"), None)
    weights = (
        P(None, None, "dp", "tensor"),
        P(None, "tensor", "dp"),
        P(None, "dp", "tensor"),
        P(None, "tensor", "dp"),
    )
    return jax.shard_map(
        shards,
        mesh=mesh,
        in_specs=(rows, rows, P(), P(), *weights) + (P(),) * 12,
        out_specs=(rows, rows, rows, *weights) + (P(),) * 12,
        check_vma=False,
    )
```

```python
import functools
import math

import jax
import jax.numpy as jnp
import numpy as np
from jax import lax
from jax.experimental import pallas as pl
from jax.experimental.pallas import tpu as pltpu
from jax.sharding import PartitionSpec as P

D = 768
FF = 3072
EMB = 33
LAYERS = 2
LMAX = 1024
BLK = 128
TAPS = LMAX // BLK
LANES = 384
HIDDEN = 768
HALO = 16
STRIP = 64

highest = lax.Precision.HIGHEST
f32 = jnp.float32
bf16 = jnp.bfloat16
epsilon = 1e-05
shift_value = 0.05


def wave_tables():
    waves = (np.arange(BLK) + 0.5)[:, None] * (2.0 * math.pi / (2 * BLK))

    def spectrum(places):
        angle = waves * places[None, :]
        return np.concatenate([np.cos(angle), -np.sin(angle)], axis=0)

    causal = spectrum(np.arange(2 * BLK) - BLK)
    ahead = spectrum(np.arange(2 * BLK))
    single = spectrum(np.arange(BLK))
    back = spectrum(np.arange(BLK)).T / BLK
    return causal, ahead, single, back


def positions_table(length):
    bands = (EMB - 1) // 2
    ramp = jnp.linspace(0.0, 1.0, length, dtype=f32)[:, None]
    places = jnp.arange(length, dtype=f32)[:, None] * (2.0 * math.pi / length)
    levels = jnp.linspace(0.0001, bands - 1, bands, dtype=f32)[None, :]
    return jnp.concatenate([ramp, jnp.cos(levels * places), -jnp.sin(levels * places)], axis=1)


def decay_table(length):
    ramp = jnp.linspace(0.0, 1.0, length, dtype=f32)[:, None]
    fastest = math.log(0.01) / 0.3
    slowest = math.log(0.01) / 1.5
    speeds = slowest + (fastest - slowest) * jnp.arange(D, dtype=jnp.int32).astype(f32) / (D - 1)
    return jnp.exp(-ramp * jnp.abs(speeds)[None, :]) + shift_value


def filter_hidden(positions, first_w, inner_w, bias_w, rate_w):
    inner = jnp.sin(rate_w[0] * (jnp.dot(positions, first_w, precision=highest) + bias_w[0]))
    inner = jnp.sin(rate_w[1] * (jnp.dot(inner, inner_w[0], precision=highest) + bias_w[1]))
    return jnp.sin(rate_w[2] * (jnp.dot(inner, inner_w[1], precision=highest) + bias_w[2]))


def rows_mask(first, count, begin, end):
    rows = first + lax.broadcasted_iota(jnp.int32, (count, 1), 0)
    return (rows >= begin) & (rows < end)


def masked_spectrum(table, block, mask):
    kept = jnp.where(mask, block.astype(f32), 0.0).astype(bf16)
    return jnp.dot(table, kept, preferred_element_type=f32)


def multiply_add(carry, left_re, left_im, right_re, right_im, conj):
    re, im = carry
    if conj:
        return (
            re + (left_re * right_re + left_im * right_im),
            im + (left_re * right_im - left_im * right_re),
        )
    return (
        re + (left_re * right_re - left_im * right_im),
        im + (left_re * right_im + left_im * right_re),
    )


def conv_forward_body(
    own_block, table, window, kernel, gate_out, bias, causal, back, carried, mixer, out, spectra, total
):
    blocks = spectra.shape[0]
    width = out.shape[1]
    origin = table[2]

    def segment(n, _):
        begin = table[3 + n] - origin
        end = table[4 + n] - origin
        head = lax.div(begin, BLK)
        tail = jnp.minimum(lax.div(end - 1, BLK), blocks - 1)

        def transform(j, _):
            at = pl.multiple_of(j * BLK, BLK)
            mask = rows_mask(at - BLK, 2 * BLK, begin, end)
            spectra[j] = masked_spectrum(causal[...], window[pl.ds(at, 2 * BLK), :], mask)
            return 0

        lax.fori_loop(head, tail + 1, transform, 0)

        def produce(j, _):
            reach = jnp.minimum(j - head, TAPS - 1) + 1
            for lane in range(0, width, 128):
                part = slice(lane, lane + 128)

                def lag(b, carry):
                    return multiply_add(
                        carry,
                        kernel[b, :BLK, part],
                        kernel[b, BLK:, part],
                        spectra[j - b, :BLK, part],
                        spectra[j - b, BLK:, part],
                        False,
                    )

                zero = jnp.zeros((BLK, 128), f32)
                re, im = lax.fori_loop(0, reach, lag, (zero, zero))
                total[:BLK, part] = re.astype(bf16)
                total[BLK:, part] = im.astype(bf16)
            value = jnp.dot(back[...], total[...], preferred_element_type=f32)
            at = pl.multiple_of((j - own_block) * BLK, BLK)
            mask = rows_mask(j * BLK, BLK, begin, end)
            out[pl.ds(at, BLK), :] = jnp.where(mask, value, out[pl.ds(at, BLK), :])
            return 0

        lax.fori_loop(jnp.maximum(head, own_block), tail + 1, produce, 0)
        return 0

    lax.fori_loop(table[0], table[1] + 1, segment, 0)
    own = window.shape[0] - out.shape[0]

    def strip(at):
        for part in lanes(width):
            value = out[pl.ds(at, STRIP), part] + bias[0, :, part] * window[
                pl.ds(own + at, STRIP), part
            ].astype(f32)
            carried[pl.ds(at, STRIP), part] = value.astype(bf16)
            mixer[pl.ds(at, STRIP), part] = (
                value * gate_out[pl.ds(at, STRIP), part].astype(f32)
            ).astype(bf16)

    each_strip(out.shape[0], STRIP, strip)


def signal_backward_body(
    own_block, table, grads, kernel, values, gate_in, bias, ahead, back,
    gate_in_grad, values_grad, signal_grad, spectra, total,
):
    blocks = spectra.shape[0]
    own_blocks = signal_grad.shape[0] // BLK
    width = signal_grad.shape[1]
    origin = table[2] + own_block * BLK

    def segment(n, _):
        begin = table[3 + n] - origin
        end = table[4 + n] - origin
        first = lax.div(jnp.maximum(begin, 0), BLK)
        tail = jnp.minimum(lax.div(end - 1, BLK), own_blocks - 1)
        last = jnp.minimum(lax.div(end - 1, BLK), blocks - 1)

        def transform(j, _):
            at = pl.multiple_of(j * BLK, BLK)
            mask = rows_mask(at, 2 * BLK, begin, end)
            spectra[j] = masked_spectrum(ahead[...], grads[pl.ds(at, 2 * BLK), :], mask)
            return 0

        lax.fori_loop(first, last + 1, transform, 0)

        def produce(j, _):
            reach = jnp.minimum(last - j, TAPS - 1) + 1
            for part in lanes(width):

                def lag(b, carry):
                    return multiply_add(
                        carry,
                        kernel[b, :BLK, part],
                        kernel[b, BLK:, part],
                        spectra[j + b, :BLK, part],
                        spectra[j + b, BLK:, part],
                        True,
                    )

                zero = jnp.zeros((BLK, 128), f32)
                re, im = lax.fori_loop(0, reach, lag, (zero, zero))
                total[:BLK, part] = re.astype(bf16)
                total[BLK:, part] = im.astype(bf16)
            value = jnp.dot(back[...], total[...], preferred_element_type=f32)
            at = pl.multiple_of(j * BLK, BLK)
            mask = rows_mask(at, BLK, begin, end)
            signal_grad[pl.ds(at, BLK), :] = jnp.where(
                mask, value, signal_grad[pl.ds(at, BLK), :]
            )
            return 0

        lax.fori_loop(first, tail + 1, produce, 0)
        return 0

    lax.fori_loop(table[0], table[1] + 1, segment, 0)

    def strip(at):
        for part in lanes(width):
            where = (pl.ds(at, STRIP), part)
            value = signal_grad[where] + bias[0, :, part] * grads[where].astype(f32)
            gate_in_grad[where] = (value * values[where].astype(f32)).astype(bf16)
            values_grad[where] = (value * gate_in[where].astype(f32)).astype(bf16)

    each_strip(signal_grad.shape[0], STRIP, strip)


def kernel_backward_body(
    own_block, table, window, grads, causal, single, back, kernel_grad, spectra, own_spectra, sums
):
    blocks = spectra.shape[0]
    width = kernel_grad.shape[1]
    origin = table[2]
    sums[...] = jnp.zeros_like(sums)

    def segment(n, _):
        begin = table[3 + n] - origin
        end = table[4 + n] - origin
        head = lax.div(begin, BLK)
        tail = jnp.minimum(lax.div(end - 1, BLK), blocks - 1)
        first = jnp.maximum(head, own_block)

        def transform(j, _):
            at = pl.multiple_of(j * BLK, BLK)
            mask = rows_mask(at - BLK, 2 * BLK, begin, end)
            spectra[j] = masked_spectrum(causal[...], window[pl.ds(at, 2 * BLK), :], mask)
            return 0

        lax.fori_loop(head, tail + 1, transform, 0)

        def transform_own(j, _):
            at = pl.multiple_of((j - own_block) * BLK, BLK)
            mask = rows_mask(j * BLK, BLK, begin, end)
            own_spectra[j - own_block] = masked_spectrum(
                single[...], grads[pl.ds(at, BLK), :], mask
            )
            return 0

        lax.fori_loop(first, tail + 1, transform_own, 0)

        def accumulate(b, _):
            for part in lanes(width):

                def at_block(j, carry):
                    return multiply_add(
                        carry,
                        spectra[j - b, :BLK, part],
                        spectra[j - b, BLK:, part],
                        own_spectra[j - own_block, :BLK, part],
                        own_spectra[j - own_block, BLK:, part],
                        True,
                    )

                re, im = lax.fori_loop(
                    jnp.maximum(first, head + b),
                    tail + 1,
                    at_block,
                    (sums[b, :BLK, part], sums[b, BLK:, part]),
                )
                sums[b, :BLK, part] = re
                sums[b, BLK:, part] = im
            return 0

        lax.fori_loop(0, jnp.minimum(tail - head, TAPS - 1) + 1, accumulate, 0)
        return 0

    lax.fori_loop(table[0], table[1] + 1, segment, 0)
    for b in range(TAPS):
        kernel_grad[b * BLK : (b + 1) * BLK, :] = jnp.dot(
            back[...], sums[b].astype(bf16), preferred_element_type=f32
        )


def norm_rows(values):
    centered = values - jnp.mean(values, -1, keepdims=True)
    rate = lax.rsqrt(jnp.mean(centered * centered, -1, keepdims=True) + epsilon)
    return centered * rate, rate


def norm_rows_back(grad, scaled, rate, gain):
    g = grad * gain
    return rate * (
        g - jnp.mean(g, -1, keepdims=True) - scaled * jnp.mean(g * scaled, -1, keepdims=True)
    )


def fold(values):
    return jnp.sum(values.reshape(values.shape[0] // 8, 8, values.shape[1]), axis=0)


def lanes(count):
    return [slice(q, q + 128) for q in range(0, count, 128)]


def dot(left, right):
    return jnp.dot(left, right, preferred_element_type=f32)


def dot_rows(left, right):
    return lax.dot_general(left, right, (((1,), (1,)), ((), ())), preferred_element_type=f32)


def each_strip(rows, step, body, copies=1):
    while rows % (step * copies):
        copies //= 2

    def run(c, _):
        for k in range(copies):
            body(pl.multiple_of((c * copies + k) * step, step))
        return 0

    lax.fori_loop(0, rows // (step * copies), run, 0)


def sum_strips(rows, step, body, zeros, copies=1):
    while rows % (step * copies):
        copies //= 2

    def run(c, totals):
        for k in range(copies):
            parts = body(pl.multiple_of((c * copies + k) * step, step))
            totals = tuple(total + part for total, part in zip(totals, parts))
        return totals

    return lax.fori_loop(0, rows // (step * copies), run, zeros)


def turn_into(target, chunk, at, order):
    turned = chunk.astype(bf16).T
    for first, size, place in order:
        target[pl.ds(place, size), at : at + chunk.shape[0]] = turned[first : first + size, :]


def in_forward_body(
    state, halo, norm, weight, bias, taps, age, normed, projected, gate_out, gate_in, values,
    signal, low, wide,
):
    rows = state.shape[0]

    @pl.when(pl.program_id(0) == 0)
    def _():
        gain, shift = norm[0:1, :], norm[1:2, :]
        low[:HALO, :] = (norm_rows(halo[...].astype(f32))[0] * gain + shift).astype(bf16)

        def strip(at):
            part = norm_rows(state[pl.ds(at, 32), :].astype(f32))[0] * gain + shift
            low[pl.ds(at + HALO, 32), :] = part.astype(bf16)
            normed[pl.ds(at, 32), :] = part.astype(bf16)

        each_strip(rows, 32, strip, 4)

    chunk = max(c for c in range(16, 273, 16) if (rows + HALO) % c == 0)

    def product(at):
        wide[pl.ds(at, chunk), :] = (
            dot(low[pl.ds(at, chunk), :], weight[0, :, : 3 * LANES]) + bias[0]
        )

    each_strip(rows + HALO, chunk, product)
    for part in range(3):
        projected[part, :HALO, :] = wide[:HALO, part * LANES : (part + 1) * LANES].astype(bf16)

    def strip(at):
        old = age[pl.ds(at, STRIP), :]
        for lane in lanes(LANES):
            mixed = []
            for part in range(3):
                cols = slice(part * LANES + lane.start, part * LANES + lane.stop)
                block = wide[pl.ds(at + HALO - 8, STRIP + 8), cols]
                now, once, twice = block[8:], block[7:-1], block[6:-2]
                projected[part, pl.ds(at + HALO, STRIP), lane] = now.astype(bf16)
                mixed.append(
                    taps[0, 0:1, cols] * now
                    + jnp.where(old >= 1, taps[0, 1:2, cols] * once, 0.0)
                    + jnp.where(old >= 2, taps[0, 2:3, cols] * twice, 0.0)
                )
            gate_out[pl.ds(at, STRIP), lane] = mixed[0].astype(bf16)
            gate_in[pl.ds(at, STRIP), lane] = mixed[1].astype(bf16)
            values[pl.ds(at, STRIP), lane] = mixed[2].astype(bf16)
            signal[pl.ds(at, STRIP), lane] = (mixed[1] * mixed[2]).astype(bf16)

    each_strip(rows, STRIP, strip)


def ff_forward_body(
    out_blocks, mixer, state, norm, shifts, weight, bias, *refs
):
    outs = refs[:out_blocks]
    middle, second, activated, slope, result, result_low, hidden = refs[out_blocks:]
    rows = state.shape[0]
    chunk = min(256, rows)

    @pl.when(pl.program_id(0) == 0)
    def _():
        def product(at):
            total = state[pl.ds(at, chunk), :].astype(f32) + shifts[0:1, :]
            for n, out in enumerate(outs):
                total += dot_rows(
                    mixer[pl.ds(at, chunk), n * LANES : (n + 1) * LANES], out[0]
                )
            middle[pl.ds(at, chunk), :] = total

        each_strip(rows, chunk, product)

        def strip(at):
            part = middle[pl.ds(at, 32), :]
            result[pl.ds(at, 32), :] = part + shifts[1:2, :]
            second[pl.ds(at, 32), :] = (
                norm_rows(part)[0] * norm[0:1, :] + norm[1:2, :]
            ).astype(bf16)

        each_strip(rows, 32, strip, 4)

    def product(at):
        hidden[...] = dot(second[pl.ds(at, chunk), :], weight[0, :, :HIDDEN]) + bias[0]

        def strip(inner):
            for lane in lanes(HIDDEN):
                before = hidden[pl.ds(inner, STRIP), lane]
                cumulative = 0.5 + 0.5 * lax.erf(before * math.sqrt(0.5))
                bell = jnp.exp(-0.5 * before * before) * (1.0 / math.sqrt(2 * math.pi))
                activated[pl.ds(at + inner, STRIP), lane] = (before * cumulative).astype(bf16)
                slope[pl.ds(at + inner, STRIP), lane] = (cumulative + before * bell).astype(bf16)

        each_strip(chunk, STRIP, strip)
        result[pl.ds(at, chunk), :] += dot_rows(
            activated[pl.ds(at, chunk), :], weight[0, :, HIDDEN:]
        )

    each_strip(rows, chunk, product)

    @pl.when(pl.program_id(0) == pl.num_programs(0) - 1)
    def _():
        def strip(at):
            result_low[pl.ds(at, STRIP), :] = result[pl.ds(at, STRIP), :].astype(bf16)

        each_strip(rows, STRIP, strip, 2)


def row_order(split, mine, size):
    if not split:
        return [(0, D, 0)]
    runs = []
    for run in range(D // size):
        slot = (run % 2) ^ mine
        place = pl.multiple_of(slot * (D // 2) + run // 2 * size, 16)
        runs.append((run * size, size, place))
    return runs


def ff_backward_body(
    split, place, grad, second, middle, norm, activated, slope, weight,
    middle_grad, middle_low, weight_grad, bias_grad, sums,
    grad_low, grad_turned, second_turned, hidden, hidden_low,
):
    rows = grad.shape[0]
    chunk = min(256, rows)
    order = row_order(split, place[0], 0 if not split else split)

    @pl.when(pl.program_id(0) == 0)
    def _():
        for at in range(0, rows, chunk):
            turn_into(grad_turned, grad[at : at + chunk, :], at, order)
            turn_into(second_turned, second[at : at + chunk, :], at, order)

        def strip(at):
            grad_low[pl.ds(at, 32), :] = grad[pl.ds(at, 32), :].astype(bf16)
            middle_grad[pl.ds(at, 32), :] = jnp.zeros((32, D), f32)

        each_strip(rows, 32, strip, 4)
        sums[...] = jnp.zeros_like(sums)
    bias_grad[...] = jnp.zeros_like(bias_grad)

    def product(at):
        hidden[...] = dot(grad_low[pl.ds(at, chunk), :], weight[0, :, HIDDEN:])

        def strip(inner):
            totals = []
            for lane in lanes(HIDDEN):
                part = hidden[pl.ds(inner, STRIP), lane] * slope[
                    pl.ds(at + inner, STRIP), lane
                ].astype(f32)
                hidden_low[pl.ds(at + inner, STRIP), lane] = part.astype(bf16)
                totals.append(fold(part))
            return totals

        zero = jnp.zeros((8, 128), f32)
        totals = sum_strips(chunk, STRIP, strip, (zero,) * (HIDDEN // 128))
        for lane, total in zip(lanes(HIDDEN), totals):
            bias_grad[0, :, lane] += jnp.sum(total, axis=0, keepdims=True)
        middle_grad[pl.ds(at, chunk), :] += dot_rows(
            hidden_low[pl.ds(at, chunk), :], weight[0, :, :HIDDEN]
        )

    each_strip(rows, chunk, product)

    def product_weight(at):
        weight_grad[0, pl.ds(at, 256), :HIDDEN] = dot(
            second_turned[pl.ds(at, 256), :], hidden_low[...]
        ).astype(bf16)
        weight_grad[0, pl.ds(at, 256), HIDDEN:] = dot(
            grad_turned[pl.ds(at, 256), :], activated[...]
        ).astype(bf16)

    each_strip(D, 256, product_weight)

    @pl.when(pl.program_id(0) == pl.num_programs(0) - 1)
    def _():
        def strip(at):
            above = grad[pl.ds(at, 16), :].astype(f32)
            inner = middle_grad[pl.ds(at, 16), :]
            scaled, rate = norm_rows(middle[pl.ds(at, 16), :])
            total = above + norm_rows_back(inner, scaled, rate, norm[0:1, :])
            middle_grad[pl.ds(at, 16), :] = total
            middle_low[pl.ds(at, 16), :] = total.astype(bf16)
            for k, part in enumerate((above, inner * scaled, inner, total)):
                sums[k] += fold(part)

        each_strip(rows, 16, strip, 4)


def gates_backward_body(
    middle_low, weight, gate_out, carried, signal, carried_grad, gate_grad, bias_grad, product_ref
):
    rows = middle_low.shape[0]
    chunk = min(256, rows)
    bias_grad[...] = jnp.zeros_like(bias_grad)

    def product(at):
        product_ref[...] = dot(middle_low[pl.ds(at, chunk), :], weight[0])

        def strip(inner):
            totals = []
            for lane in lanes(LANES):
                part = product_ref[pl.ds(inner, STRIP), lane]
                where = (pl.ds(at + inner, STRIP), lane)
                grown = part * gate_out[where].astype(f32)
                carried_grad[where] = grown.astype(bf16)
                gate_grad[where] = (part * carried[where].astype(f32)).astype(bf16)
                totals.append(fold(grown * signal[where].astype(f32)))
            return totals

        zero = jnp.zeros((8, 128), f32)
        totals = sum_strips(chunk, STRIP, strip, (zero,) * (LANES // 128))
        for lane, total in zip(lanes(LANES), totals):
            bias_grad[0, :, lane] += jnp.sum(total, axis=0, keepdims=True)

    each_strip(rows, chunk, product)


def in_backward_body(
    split, place, first_grad, second_grad, third_grad, halo, age, projected, taps, normed,
    middle_low, mixer, weight, state, middle_grad, norm,
    grad, grad_out, weight_grad, bias_grad, taps_grad, sums,
    normed_turned, middle_turned, spread, low,
):
    rows = normed.shape[0]
    chunk = min(256, rows)
    order = row_order(split, place[0], 0 if not split else split)

    @pl.when(pl.program_id(0) == 0)
    def _():
        for at in range(0, rows, chunk):
            turn_into(normed_turned, normed[at : at + chunk, :], at, order)
            turn_into(middle_turned, middle_low[at : at + chunk, :], at, order)
        sums[...] = jnp.zeros_like(sums)

        def strip(at):
            grad[pl.ds(at, 32), :] = jnp.zeros((32, D), f32)

        each_strip(rows, 32, strip, 4)

    for part, ref in enumerate((first_grad, second_grad, third_grad)):
        cols = slice(part * LANES, (part + 1) * LANES)

        def strip(at):
            spread[pl.ds(at, STRIP), cols] = ref[pl.ds(at, STRIP), :]

        each_strip(rows, STRIP, strip)
        spread[rows:, cols] = halo[part]

    for part in range(3):

        def strip(at):
            old = age[pl.ds(at, STRIP + HALO), :]
            mine, after_one, after_two = old[:STRIP], old[1 : STRIP + 1], old[2 : STRIP + 2]
            totals = []
            for lane in lanes(LANES):
                cols = slice(part * LANES + lane.start, part * LANES + lane.stop)
                block = spread[pl.ds(at, STRIP + HALO), cols].astype(f32)
                source = projected[part, pl.ds(at, STRIP + HALO), lane].astype(f32)
                now = block[:STRIP]
                total = (
                    taps[0, 0:1, cols] * now
                    + jnp.where(after_one >= 1, taps[0, 1:2, cols] * block[1 : STRIP + 1], 0.0)
                    + jnp.where(after_two >= 2, taps[0, 2:3, cols] * block[2 : STRIP + 2], 0.0)
                )
                low[pl.ds(at, STRIP), cols] = total.astype(bf16)
                totals += [
                    fold(now * source[HALO:]),
                    fold(jnp.where(mine >= 1, now * source[HALO - 1 : -1], 0.0)),
                    fold(jnp.where(mine >= 2, now * source[HALO - 2 : -2], 0.0)),
                    fold(total),
                ]
            return totals

        zero = jnp.zeros((8, 128), f32)
        totals = sum_strips(rows, STRIP, strip, (zero,) * (4 * LANES // 128))
        for q, lane in enumerate(lanes(LANES)):
            cols = slice(part * LANES + lane.start, part * LANES + lane.stop)
            for tap in range(3):
                taps_grad[0, tap : tap + 1, cols] = jnp.sum(
                    totals[4 * q + tap], axis=0, keepdims=True
                )
            bias_grad[0, :, cols] = jnp.sum(totals[4 * q + 3], axis=0, keepdims=True)

    def product(at):
        grad[pl.ds(at, chunk), :] += dot_rows(
            low[pl.ds(at, chunk), :], weight[0, :, : 3 * LANES]
        )

    each_strip(rows, chunk, product)

    def product_weight(at):
        weight_grad[0, pl.ds(at, 256), : 3 * LANES] = dot(
            normed_turned[pl.ds(at, 256), :], low[...]
        ).astype(bf16)
        weight_grad[0, pl.ds(at, 256), 3 * LANES :] = dot(
            middle_turned[pl.ds(at, 256), :], mixer[...]
        ).astype(bf16)

    each_strip(D, 256, product_weight)

    @pl.when(pl.program_id(0) == pl.num_programs(0) - 1)
    def _():
        def strip(at):
            inner = grad[pl.ds(at, 16), :]
            scaled, rate = norm_rows(state[pl.ds(at, 16), :].astype(f32))
            total = middle_grad[pl.ds(at, 16), :] + norm_rows_back(
                inner, scaled, rate, norm[0:1, :]
            )
            grad[pl.ds(at, 16), :] = total
            grad_out[pl.ds(at, 16), :] = total.astype(bf16)
            for k, part in enumerate((inner * scaled, inner)):
                sums[k] += fold(part)

        each_strip(rows, 16, strip, 4)


def whole(shape):
    return pl.BlockSpec(
        shape, lambda i, *_: (0,) * len(shape), pipeline_mode=pl.Buffered(1)
    )


def by_lane(shape):
    return pl.BlockSpec(shape, lambda i, *_: (0,) * (len(shape) - 1) + (i,))


def by_first(shape):
    return pl.BlockSpec(shape, lambda i, *_: (i,) + (0,) * (len(shape) - 1))


def weight_block(wide, per, first=0, stride=1):
    return pl.BlockSpec(
        (1, D, wide), lambda i, *_: (i // per, 0, first + stride * (i % per))
    )


def run(body, name, grid, scalars, ins, outs, scratch, flops, moved, limit=48):
    arrays, in_specs = zip(*ins)
    shapes, out_specs = zip(*outs)
    return pl.pallas_call(
        body,
        out_shape=shapes,
        grid_spec=pltpu.PrefetchScalarGridSpec(
            num_scalar_prefetch=len(scalars),
            grid=(grid,),
            in_specs=in_specs,
            out_specs=out_specs,
            scratch_shapes=scratch,
        ),
        compiler_params=pltpu.CompilerParams(vmem_limit_bytes=limit << 20),
        cost_estimate=pl.CostEstimate(flops=flops, bytes_accessed=moved, transcendentals=0),
        name=name,
    )(*scalars, *arrays)


def shape_of(dims, kind):
    return jax.ShapeDtypeStruct(dims, kind)


def in_forward(state, halo, norm, weights, first, per, bias, taps, age):
    rows = state.shape[0]
    blocks = D // LANES
    low = (shape_of((rows, D), bf16), by_lane((rows, LANES)))
    return run(
        in_forward_body, "in_forward", blocks, (),
        [
            (state, whole((rows, D))), (halo, whole((HALO, D))), (norm, whole((2, D))),
            (weights, weight_block(4 * LANES, per, first)),
            (bias, by_first((1, 1, 3 * LANES))), (taps, by_first((1, 3, 3 * LANES))),
            (age, whole(age.shape)),
        ],
        [
            (shape_of((rows, D), bf16), whole((rows, D))),
            (shape_of((3, rows + HALO, D), bf16), by_lane((3, rows + HALO, LANES))),
            low, low, low, low,
        ],
        [pltpu.VMEM((rows + HALO, D), bf16), pltpu.VMEM((rows + HALO, 3 * LANES), f32)],
        2 * rows * D * 3 * D, 20_000_000, 30,
    )


def ff_forward(mixer, state, norm, shifts, weights, per, hidden_per, bias, mix, first):
    rows = state.shape[0]
    hidden_blocks = FF // HIDDEN
    row = (rows, D)
    tall = (shape_of((rows, FF), bf16), by_lane((rows, HIDDEN)))
    out_specs = [
        pl.BlockSpec(
            (1, D, LANES), lambda i, *_, n=n: (n // per, 0, 4 * (first + n % per) + 3)
        )
        for n in range(D // LANES)
    ]
    return run(
        functools.partial(ff_forward_body, D // LANES), "ff_forward", hidden_blocks, (),
        [
            (mixer, whole(row)), (state, whole(row)), (norm, whole((2, D))),
            (shifts, whole((2, D))),
            (weights, weight_block(2 * HIDDEN, hidden_per)),
            (bias, by_first((1, 1, HIDDEN))),
        ]
        + [(mix, spec) for spec in out_specs],
        [
            (shape_of(row, f32), whole(row)), (shape_of(row, bf16), whole(row)), tall, tall,
            (shape_of(row, f32), whole(row)), (shape_of(row, bf16), whole(row)),
        ],
        [pltpu.VMEM((min(256, rows), HIDDEN), f32)],
        2 * rows * D * (2 * FF + D), 40_000_000, 32,
    )


def ff_backward(split, place, grad, second, middle, norm, activated, slope, weights, hidden_per):
    rows = grad.shape[0]
    row = (rows, D)
    halves = weights.shape[0]
    hidden_blocks = FF // HIDDEN
    grads = shape_of((halves, D, 2 * FF // halves), bf16)
    return run(
        functools.partial(ff_backward_body, split), "ff_backward", hidden_blocks, (place,),
        [
            (grad, whole(row)), (second, whole(row)), (middle, whole(row)), (norm, whole((2, D))),
            (activated, by_lane((rows, HIDDEN))), (slope, by_lane((rows, HIDDEN))),
            (weights, weight_block(2 * HIDDEN, hidden_per)),
        ],
        [
            (shape_of(row, f32), whole(row)), (shape_of(row, bf16), whole(row)),
            (grads, weight_block(2 * HIDDEN, hidden_per)),
            (shape_of((hidden_blocks, 1, HIDDEN), f32), by_first((1, 1, HIDDEN))),
            (shape_of((4, 8, D), f32), whole((4, 8, D))),
        ],
        [
            pltpu.VMEM(row, bf16), pltpu.VMEM((D, rows), bf16), pltpu.VMEM((D, rows), bf16),
            pltpu.VMEM((min(256, rows), HIDDEN), f32), pltpu.VMEM((rows, HIDDEN), bf16),
        ],
        8 * rows * D * FF, 50_000_000, 40,
    )


def gates_backward(middle_low, weights, first, per, gate_out, carried, signal):
    rows = middle_low.shape[0]
    block = (rows, LANES)
    low = (shape_of((rows, D), bf16), by_lane(block))
    return run(
        gates_backward_body, "gates_backward", D // LANES, (),
        [
            (middle_low, whole((rows, D))), (weights, weight_block(LANES, per, 4 * first + 3, 4)),
            (gate_out, by_lane(block)), (carried, by_lane(block)), (signal, by_lane(block)),
        ],
        [
            low, low,
            (shape_of((D // LANES, 1, LANES), f32), by_first((1, 1, LANES))),
        ],
        [pltpu.VMEM((min(256, rows), LANES), f32)],
        2 * rows * D * D, 10_000_000, 20,
    )


def in_backward(
    split, place, mixed_grads, halo, age, projected, taps, normed, middle_low, mixer, weights,
    first, per, state, middle_grad, norm,
):
    rows = normed.shape[0]
    row, block = (rows, D), (rows, LANES)
    blocks = D // LANES
    grads = shape_of((weights.shape[0], D, 4 * per * LANES), bf16)
    return run(
        functools.partial(in_backward_body, split), "in_backward", blocks, (place,),
        [(part, by_lane(block)) for part in mixed_grads]
        + [
            (halo, by_lane((3, HALO, LANES))), (age, whole(age.shape)),
            (projected, by_lane((3, rows + HALO, LANES))), (taps, by_first((1, 3, 3 * LANES))),
            (normed, whole(row)), (middle_low, whole(row)), (mixer, by_lane(block)),
            (weights, weight_block(4 * LANES, per, first)), (state, whole(row)),
            (middle_grad, whole(row)), (norm, whole((2, D))),
        ],
        [
            (shape_of(row, f32), whole(row)), (shape_of(row, bf16), whole(row)),
            (grads, weight_block(4 * LANES, per)),
            (shape_of((blocks, 1, 3 * LANES), f32), by_first((1, 1, 3 * LANES))),
            (shape_of((blocks, 3, 3 * LANES), f32), by_first((1, 3, 3 * LANES))),
            (shape_of((2, 8, D), f32), whole((2, 8, D))),
        ],
        [
            pltpu.VMEM((D, rows), bf16), pltpu.VMEM((D, rows), bf16),
            pltpu.VMEM((rows + HALO, 3 * LANES), bf16), pltpu.VMEM((rows, 3 * LANES), bf16),
        ],
        2 * rows * D * 7 * D, 40_000_000, 46,
    )


def conv_forward(table, window, kernel, gate_out, bias, rows, tables):
    causal, _, _, back = tables
    wide = window.shape[0]
    blocks = wide // BLK - 1
    own_block = (wide - BLK - rows) // BLK
    low = (shape_of((rows, D), bf16), by_lane((rows, LANES)))
    return run(
        functools.partial(conv_forward_body, own_block), "conv_forward", D // LANES, (table,),
        [
            (window, by_lane((wide, LANES))), (kernel, by_lane((TAPS, 2 * BLK, LANES))),
            (gate_out, by_lane((rows, LANES))), (bias, by_first((1, 1, LANES))),
            (causal, whole((2 * BLK, 2 * BLK))), (back, whole((BLK, 2 * BLK))),
        ],
        [low, low],
        [
            pltpu.VMEM((rows, LANES), f32),
            pltpu.VMEM((blocks, 2 * BLK, LANES), f32),
            pltpu.VMEM((2 * BLK, LANES), bf16),
        ],
        20_000_000_000, 20_000_000, 28,
    )


def signal_backward(table, grads, kernel, values, gate_in, bias, rows, hops, tables):
    _, ahead, _, back = tables
    wide = grads.shape[0]
    low = (shape_of((rows, D), bf16), by_lane((rows, LANES)))
    return run(
        functools.partial(signal_backward_body, hops * rows // BLK), "signal_backward",
        D // LANES, (table,),
        [
            (grads, by_lane((wide, LANES))),
            (kernel, by_lane((TAPS, 2 * BLK, LANES))), (values, by_lane((rows, LANES))),
            (gate_in, by_lane((rows, LANES))), (bias, by_first((1, 1, LANES))),
            (ahead, whole((2 * BLK, 2 * BLK))), (back, whole((BLK, 2 * BLK))),
        ],
        [low, low],
        [
            pltpu.VMEM((rows, LANES), f32),
            pltpu.VMEM((wide // BLK - 1, 2 * BLK, LANES), f32),
            pltpu.VMEM((2 * BLK, LANES), bf16),
        ],
        20_000_000_000, 20_000_000, 32,
    )


def kernel_backward(table, window, grads, rows, tables):
    causal, _, single, back = tables
    wide = window.shape[0]
    blocks = wide // BLK - 1
    own_block = (wide - BLK - rows) // BLK
    return run(
        functools.partial(kernel_backward_body, own_block), "kernel_backward",
        D // LANES, (table,),
        [
            (window, by_lane((wide, LANES))), (grads, by_lane((rows, LANES))),
            (causal, whole((2 * BLK, 2 * BLK))), (single, whole((2 * BLK, BLK))),
            (back, whole((BLK, 2 * BLK))),
        ],
        [(shape_of((LMAX, D), f32), by_lane((LMAX, LANES)))],
        [
            pltpu.VMEM((blocks, 2 * BLK, LANES), f32),
            pltpu.VMEM((rows // BLK, 2 * BLK, LANES), f32),
            pltpu.VMEM((TAPS, 2 * BLK, LANES), f32),
        ],
        20_000_000_000, 20_000_000, 32,
    )[0]


def shards(
    tokens,
    out_grad,
    seq_lengths,
    deal_order,
    input_weight,
    output_weight,
    up_projection_weight,
    down_projection_weight,
    input_bias,
    short_taps,
    filter_first,
    filter_inner,
    filter_biases,
    filter_rates,
    filter_out,
    conv_bias,
    norm_gains,
    norm_biases,
    output_biases,
    up_projection_bias,
):
    tensor_count = lax.axis_size("tensor")
    chips = lax.axis_size("chip")
    cores = lax.axis_size("core")
    devices = tensor_count * chips * cores
    core = lax.axis_index("core")
    rank = (lax.axis_index("chip") * cores + core) * tensor_count + lax.axis_index("tensor")
    rows = tokens.shape[0]
    width = input_weight.shape[3]
    hidden = up_projection_weight.shape[2]
    depth = input_weight.shape[2]
    count = seq_lengths.shape[0]
    everyone = ("chip", "core", "tensor")
    owners = ("tensor", "chip", "core")
    hops = -(-(LMAX - 1) // rows)
    direct = width % LANES == 0 and hidden % HIDDEN == 0
    per = width // LANES if direct else D // LANES
    hidden_per = hidden // HIDDEN if direct else FF // HIDDEN
    halves = tensor_count if direct else 1
    paired = (
        direct and depth % 16 == 0 and cores == 2 and tensor_count == 2
        and chips > 1 and chips & (chips - 1) == 0
    )
    split = depth if paired else 0
    chip, side = lax.axis_index("chip"), lax.axis_index("tensor")
    plane, row, planes = chip // 2, chip % 2, chips // 2

    def swap(values, mask):
        pairs = [(i, i ^ mask) for i in range(chips * tensor_count)]
        return lax.ppermute(values, ("chip", "tensor"), pairs)

    def swap_core(values):
        return lax.ppermute(values, "core", [(0, 1), (1, 0)])

    def pick(values, index, axis=0):
        return lax.dynamic_index_in_dim(values, index, axis, False)

    def gather_pairs(values):
        n = values.shape[-1]
        parts = jnp.stack([values] + [swap(values, k << 2) for k in range(1, planes)])
        values = jnp.stack([pick(parts, k ^ plane) for k in range(planes)])
        parts = jnp.stack([values] + [swap(values, k) for k in range(1, 4)])
        mine = row * 2 + side
        values = jnp.stack(
            [
                jnp.stack([pick(parts, (2 * r + s) ^ mine) for r in range(2)], axis=1)
                for s in range(2)
            ]
        )
        other = swap_core(values)
        values = jnp.stack(
            [jnp.where(core == 0, values, other), jnp.where(core == 0, other, values)], axis=3
        )
        return values.reshape(2, D, n)

    def scatter_pairs(values):
        half = D // 2
        other = swap_core(values[:, half:])
        total = (values[:, :half].astype(f32) + other.astype(f32)).astype(bf16)
        total = total.reshape(2, planes, 2, depth, -1)

        def block(s, r):
            return pick(pick(total, s), r, 1)

        parts = [swap(block(side ^ (k % 2), row ^ (k // 2)), k) for k in range(1, 4)]
        total = block(side, row).astype(f32)
        for part in parts:
            total += part.astype(f32)
        low = total.astype(bf16)
        parts = [swap(pick(low, plane ^ k), k << 2) for k in range(1, planes)]
        total = pick(total, plane)
        for part in parts:
            total += part.astype(f32)
        return total

    def from_before(values, hop=1):
        return lax.ppermute(values, everyone, [(i, i + hop) for i in range(devices - hop)])

    def from_after(values, hop=1):
        return lax.ppermute(values, everyone, [(i + hop, i) for i in range(devices - hop)])

    def join_columns(ins, out, up, down, mix_blocks, ff_blocks):
        lead = out.shape[:-1]
        mix = jnp.stack(
            [part.reshape(*lead, mix_blocks, -1) for part in (*ins, out)], axis=-2
        ).reshape(*lead, -1)
        ff = jnp.stack(
            [part.reshape(*lead, ff_blocks, -1) for part in (up, down)], axis=-2
        ).reshape(*lead, -1)
        return mix, ff

    def part_columns(mix, ff, mix_blocks, ff_blocks):
        lead = mix.shape[:-1]
        mix = mix.reshape(*lead, mix_blocks, 4, -1)
        ff = ff.reshape(*lead, ff_blocks, 2, -1)
        parts = [mix[..., k, :].reshape(*lead, -1) for k in range(4)]
        return parts[:3], parts[3], *[ff[..., k, :].reshape(*lead, -1) for k in range(2)]

    local_mix = per if direct else 1
    local_ff = hidden_per if direct else 1
    local = []
    for layer in range(LAYERS):
        local.append(
            join_columns(
                [input_weight[layer, k].astype(bf16) for k in range(3)],
                jnp.transpose(output_weight[layer].astype(bf16)),
                up_projection_weight[layer].astype(bf16),
                jnp.transpose(down_projection_weight[layer].astype(bf16)),
                local_mix,
                local_ff,
            )
        )

    def gather(part):
        return lax.all_gather(part, owners, axis=0, tiled=True).reshape(tensor_count, D, -1)

    gathered = []
    if paired:
        shared = gather(jnp.concatenate([local[0][1], local[1][0]], axis=1))
        last = gather(local[1][1])
        gathered.append((gather_pairs(local[0][0]), 0, shared))
        gathered.append((shared, 2 * hidden // (4 * LANES), last))
    else:
        for mix, ff in local:
            mix, ff = gather(mix), gather(ff)
            if not direct:
                ins, out, up, down = part_columns(mix, ff, local_mix, local_ff)

                def full(piece):
                    return jnp.transpose(piece, (1, 0, 2)).reshape(1, D, -1)

                mix, ff = join_columns(
                    [full(k) for k in ins], full(out), full(up), full(down), per, hidden_per
                )
            gathered.append((mix, 0, ff))

    numbers = jnp.arange(count, dtype=jnp.int32)
    match = deal_order[:, None] == numbers[None, :]
    lengths = jnp.sum(jnp.where(match, seq_lengths[:, None], 0), axis=0)
    ends = jnp.sum(jnp.where(numbers[:, None] <= numbers[None, :], lengths[:, None], 0), axis=0)
    starts = ends - lengths
    base = rank * rows
    first_segment = jnp.sum((starts <= base).astype(jnp.int32)) - 1
    last_segment = jnp.sum((starts < base + rows).astype(jnp.int32)) - 1
    table = jnp.concatenate(
        [
            jnp.stack([first_segment, last_segment, base - hops * rows]),
            starts,
            ends[count - 1 :],
        ]
    ).astype(jnp.int32)
    places = base + jnp.arange(rows + HALO, dtype=jnp.int32)
    begun = jnp.max(jnp.where(starts[None, :] <= places[:, None], starts[None, :], 0), axis=1)
    age = jnp.broadcast_to((places - begun)[:, None], (rows + HALO, 128))
    place = core.astype(jnp.int32).reshape(1)

    tables = tuple(jnp.asarray(t, f32).astype(bf16) for t in wave_tables())
    positions = positions_table(LMAX)
    modulation = decay_table(LMAX)
    blank = jnp.zeros((BLK, D), bf16)

    filters = []
    for layer in range(LAYERS):
        inner, filter_back = jax.vjp(
            lambda a, b, c, d: filter_hidden(positions, a, b, c, d),
            filter_first[layer],
            filter_inner[layer],
            filter_biases[layer],
            filter_rates[layer],
        )
        kernel = jnp.dot(inner, filter_out[layer], precision=highest) * modulation
        kernel_spectra = jnp.einsum(
            "kr,brc->bkc",
            tables[2],
            kernel.reshape(TAPS, BLK, D).astype(bf16),
            preferred_element_type=f32,
        )
        filters.append((inner, filter_back, kernel_spectra))

    def by_block(values):
        lead = values.shape[:-2]
        split_up = values.reshape(*lead, 3, D // LANES, LANES)
        return jnp.moveaxis(split_up, -2, 0).reshape(D // LANES, *lead, 3 * LANES)

    def from_block(values):
        lead = values.shape[1:-1]
        split_up = values.reshape(D // LANES, *lead, 3, LANES)
        return jnp.moveaxis(split_up, 0, -2).reshape(*lead, 3, D)

    state = tokens
    kept = []
    outputs = []
    for layer in range(LAYERS):
        mix_weights, first, ff_weights = gathered[layer]
        first_norm = jnp.stack([norm_gains[layer, 0], norm_biases[layer, 0]])
        second_norm = jnp.stack([norm_gains[layer, 1], norm_biases[layer, 1]])
        taps = by_block(short_taps[layer])
        lane_bias = conv_bias[layer].reshape(D // LANES, 1, LANES)
        normed, projected, gate_out, gate_in, values, signal = in_forward(
            state,
            from_before(state[rows - HALO :]),
            first_norm,
            mix_weights,
            first,
            per,
            by_block(input_bias[layer][None]),
            taps,
            age,
        )
        window = jnp.concatenate(
            [blank] + [from_before(signal, hop) for hop in range(hops, 0, -1)] + [signal]
        )
        carried, mixer = conv_forward(
            table, window, filters[layer][2], gate_out, lane_bias, rows, tables
        )
        middle, second, activated, slope, result, result_low = ff_forward(
            mixer, state, second_norm, output_biases[layer], ff_weights, per, hidden_per,
            up_projection_bias[layer].reshape(FF // HIDDEN, 1, HIDDEN), mix_weights, first,
        )
        outputs.append(result_low)
        kept.append(
            (
                state, first_norm, second_norm, taps, lane_bias, normed, projected, gate_out,
                gate_in, values, signal, window, carried, mixer, middle, second, activated, slope,
            )
        )
        state = result

    grad = out_grad
    owned, owned_ff = {}, {}
    small = [None] * LAYERS
    for layer in reversed(range(LAYERS)):
        (
            state, first_norm, second_norm, taps, lane_bias, normed, projected, gate_out,
            gate_in, values, signal, window, carried, mixer, middle, second, activated, slope,
        ) = kept[layer]
        mix_weights, first, ff_weights = gathered[layer]
        inner, filter_back, kernel_spectra = filters[layer]
        middle_grad, middle_low, ff_grad, up_bias_grad, ff_sums = ff_backward(
            0, place, grad, second, middle, second_norm, activated, slope, ff_weights, hidden_per
        )
        carried_grad, gate_grad, conv_bias_grad = gates_backward(
            middle_low, mix_weights, first, per, gate_out, carried, signal
        )
        ahead = [from_after(carried_grad, hop) for hop in range(1, hops + 1)]
        kernel_grad = kernel_backward(table, window, carried_grad, rows, tables)
        shaped = kernel_grad * modulation
        filter_out_grad = jnp.dot(jnp.transpose(inner), shaped, precision=highest)
        inner_grad = jnp.dot(shaped, jnp.transpose(filter_out[layer]), precision=highest)
        filter_grads = filter_back(inner_grad)
        ahead, filter_grads, filter_out_grad, owned = lax.optimization_barrier(
            (ahead, filter_grads, filter_out_grad, owned)
        )
        grads_window = jnp.concatenate([carried_grad] + ahead + [blank])
        gate_in_grad, values_grad = signal_backward(
            table, grads_window, kernel_spectra, values, gate_in, lane_bias, rows, hops, tables
        )
        mixed_grads = (gate_grad, gate_in_grad, values_grad)
        after = from_after(jnp.stack([part[:HALO] for part in mixed_grads]))
        grad, grad_low, mix_grad, in_bias_grad, taps_grad, in_sums = in_backward(
            split, place, mixed_grads, after, age, projected, taps, normed, middle_low, mixer,
            mix_weights, first, per, state, middle_grad, first_norm,
        )

        if not direct:
            ins, out, up, down = part_columns(mix_grad, ff_grad, per, hidden_per)

            def by_owner(piece):
                piece = piece.reshape(D, tensor_count, -1)
                return jnp.transpose(piece, (1, 0, 2))

            mix_grad, ff_grad = join_columns(
                [by_owner(k) for k in ins], by_owner(out), by_owner(up), by_owner(down), 1, 1
            )

        def share(part):
            return lax.psum_scatter(
                part.reshape(tensor_count * D, -1), owners, scatter_dimension=0, tiled=True
            )

        owned[layer] = (scatter_pairs(mix_grad) if paired else share(mix_grad)).astype(f32)
        owned_ff[layer] = share(ff_grad).astype(f32)
        ff_sums = jnp.sum(ff_sums, axis=1)
        in_sums = jnp.sum(in_sums, axis=1)
        small[layer] = (
            from_block(in_bias_grad)[0],
            from_block(taps_grad),
            *filter_grads,
            filter_out_grad,
            conv_bias_grad.reshape(D),
            jnp.stack([in_sums[0], ff_sums[1]]),
            jnp.stack([in_sums[1], ff_sums[2]]),
            jnp.stack([ff_sums[3], ff_sums[0]]),
            up_bias_grad.reshape(FF),
        )

    small_stacked = [
        jnp.stack([small[layer][index] for layer in range(LAYERS)])
        for index in range(len(small[0]))
    ]
    sizes = [part.size for part in small_stacked]
    flat = jnp.concatenate([part.reshape(-1) for part in small_stacked])
    unit = 1024
    padded = -(-flat.shape[0] // unit) * unit
    flat = jnp.pad(flat, (0, padded - flat.shape[0])).reshape(padded // 128, 128)
    step = 1
    while step < devices:
        low = flat.astype(bf16)
        other = lax.ppermute(low, everyone, [(i, i ^ step) for i in range(devices)])
        flat = low.astype(f32) + other.astype(f32)
        step *= 2
    flat = flat.reshape(-1)
    summed = []
    offset = 0
    for part, size in zip(small_stacked, sizes):
        summed.append(flat[offset : offset + size].reshape(part.shape))
        offset += size

    in_owned, out_owned, up_owned, down_owned = [], [], [], []
    for layer in range(LAYERS):
        ins, out, up, down = part_columns(owned[layer], owned_ff[layer], local_mix, local_ff)
        in_owned.append(jnp.stack(ins))
        out_owned.append(jnp.transpose(out))
        up_owned.append(up)
        down_owned.append(jnp.transpose(down))
    return (
        outputs[0],
        outputs[1],
        grad_low,
        jnp.stack(in_owned),
        jnp.stack(out_owned),
        jnp.stack(up_owned),
        jnp.stack(down_owned),
        *summed,
    )


def solution(mesh):
    groups, tensors = mesh.shape["dp"], mesh.shape["tensor"]
    cores = 2 if groups % 2 == 0 else 1
    fine = jax.sharding.Mesh(
        mesh.devices.reshape(groups // cores, cores, tensors), ("chip", "core", "tensor")
    )
    dp = ("chip", "core")
    rows = P(("chip", "core", "tensor"), None)
    weights = (
        P(None, None, dp, "tensor"),
        P(None, "tensor", dp),
        P(None, dp, "tensor"),
        P(None, "tensor", dp),
    )
    return jax.shard_map(
        shards,
        mesh=fine,
        in_specs=(rows, rows, P(), P(), *weights) + (P(),) * 12,
        out_specs=(rows, rows, rows, *weights) + (P(),) * 12,
        check_vma=False,
    )
```

```python
import functools
import math

import jax
import jax.numpy as jnp
import numpy as np
from jax import lax
from jax.experimental import pallas as pl
from jax.experimental.pallas import tpu as pltpu
from jax.sharding import PartitionSpec as P

D = 768
FF = 3072
EMB = 33
LAYERS = 2
LMAX = 1024
BLK = 128
TAPS = LMAX // BLK
LANES = 384
CONV_LANES = 768
STEP = 1
GROUP = 16
HIDDEN = 768
HALO = 16
STRIP = 64

highest = lax.Precision.HIGHEST
f32 = jnp.float32
bf16 = jnp.bfloat16
epsilon = 1e-05
shift_value = 0.05


def wave_tables():
    waves = (np.arange(BLK) + 0.5)[:, None] * (2.0 * math.pi / (2 * BLK))

    def spectrum(places):
        angle = waves * places[None, :]
        return np.concatenate([np.cos(angle), -np.sin(angle)], axis=0)

    causal = spectrum(np.arange(2 * BLK) - BLK)
    ahead = spectrum(np.arange(2 * BLK))
    single = spectrum(np.arange(BLK))
    back = spectrum(np.arange(BLK)).T / BLK
    return causal, ahead, single, back


def positions_table(length):
    bands = (EMB - 1) // 2
    ramp = jnp.linspace(0.0, 1.0, length, dtype=f32)[:, None]
    places = jnp.arange(length, dtype=f32)[:, None] * (2.0 * math.pi / length)
    levels = jnp.linspace(0.0001, bands - 1, bands, dtype=f32)[None, :]
    return jnp.concatenate([ramp, jnp.cos(levels * places), -jnp.sin(levels * places)], axis=1)


def decay_table(length):
    ramp = jnp.linspace(0.0, 1.0, length, dtype=f32)[:, None]
    fastest = math.log(0.01) / 0.3
    slowest = math.log(0.01) / 1.5
    speeds = slowest + (fastest - slowest) * jnp.arange(D, dtype=jnp.int32).astype(f32) / (D - 1)
    return jnp.exp(-ramp * jnp.abs(speeds)[None, :]) + shift_value


def filter_hidden(positions, first_w, inner_w, bias_w, rate_w):
    inner = jnp.sin(rate_w[0] * (jnp.dot(positions, first_w, precision=highest) + bias_w[0]))
    inner = jnp.sin(rate_w[1] * (jnp.dot(inner, inner_w[0], precision=highest) + bias_w[1]))
    return jnp.sin(rate_w[2] * (jnp.dot(inner, inner_w[1], precision=highest) + bias_w[2]))


def rows_mask(first, count, begin, end):
    rows = first + lax.broadcasted_iota(jnp.int32, (count, 1), 0)
    return (rows >= begin) & (rows < end)


def masked_spectrum(table, block, mask):
    kept = jnp.where(mask, block.astype(f32), 0.0).astype(bf16)
    return jnp.dot(table, kept, preferred_element_type=f32)


def groups():
    return [(slice(f, f + GROUP), slice(BLK + f, BLK + f + GROUP)) for f in range(0, BLK, GROUP)]


def no_sums():
    return tuple(jnp.zeros((GROUP, 128), f32) for _ in range(2 * BLK // GROUP))


def multiply_add(carry, left, a, right, b, part, conj):
    result = []
    for k, (up, down) in enumerate(groups()):
        left_re, left_im = left[a, up, part], left[a, down, part]
        right_re, right_im = right[b, up, part], right[b, down, part]
        if conj:
            re = left_re * right_re + left_im * right_im
            im = left_re * right_im - left_im * right_re
        else:
            re = left_re * right_re - left_im * right_im
            im = left_re * right_im + left_im * right_re
        result += [carry[2 * k] + re, carry[2 * k + 1] + im]
    return tuple(result)


def conv_forward_body(
    own_block, table, window, kernel, gate_out, bias, causal, back, carried, mixer, out, spectra, total
):
    blocks = spectra.shape[0] - STEP + 1
    width = out.shape[1]
    origin = table[2]

    def segment(n, _):
        begin = table[3 + n] - origin
        end = table[4 + n] - origin
        head = lax.div(begin, BLK)
        tail = jnp.minimum(lax.div(end - 1, BLK), blocks - 1)

        for k in range(STEP - 1):
            spectra[head + k] = jnp.zeros(spectra.shape[1:], f32)

        def transform(j, _):
            at = pl.multiple_of(j * BLK, BLK)
            mask = rows_mask(at - BLK, 2 * BLK, begin, end)
            spectra[j + STEP - 1] = masked_spectrum(
                causal[...], window[pl.ds(at, 2 * BLK), :], mask
            )
            return 0

        lax.fori_loop(head, tail + 1, transform, 0)

        def produce(j, _):
            reach = lax.div(jnp.minimum(j - head, TAPS - 1) + STEP, STEP)
            for lane in range(0, width, 128):
                part = slice(lane, lane + 128)

                def lag(c, carry):
                    for k in range(STEP):
                        b = c * STEP + k
                        at = j - b + STEP - 1
                        carry = multiply_add(carry, kernel, b, spectra, at, part, False)
                    return carry

                held = lax.fori_loop(0, reach, lag, no_sums())
                for k, pair in enumerate(groups()):
                    total[pair[0], part] = held[2 * k].astype(bf16)
                    total[pair[1], part] = held[2 * k + 1].astype(bf16)
            value = jnp.dot(back[...], total[...], preferred_element_type=f32)
            at = pl.multiple_of((j - own_block) * BLK, BLK)
            mask = rows_mask(j * BLK, BLK, begin, end)
            out[pl.ds(at, BLK), :] = jnp.where(mask, value, out[pl.ds(at, BLK), :])
            return 0

        lax.fori_loop(jnp.maximum(head, own_block), tail + 1, produce, 0)
        return 0

    lax.fori_loop(table[0], table[1] + 1, segment, 0)
    own = window.shape[0] - out.shape[0]

    def strip(at):
        for part in lanes(width):
            value = out[pl.ds(at, STRIP), part] + bias[0, :, part] * window[
                pl.ds(own + at, STRIP), part
            ].astype(f32)
            carried[pl.ds(at, STRIP), part] = value.astype(bf16)
            mixer[pl.ds(at, STRIP), part] = (
                value * gate_out[pl.ds(at, STRIP), part].astype(f32)
            ).astype(bf16)

    each_strip(out.shape[0], STRIP, strip)


def signal_backward_body(
    own_block, table, grads, kernel, values, gate_in, bias, ahead, back,
    gate_in_grad, values_grad, signal_grad, spectra, total,
):
    blocks = spectra.shape[0] - STEP + 1
    own_blocks = signal_grad.shape[0] // BLK
    width = signal_grad.shape[1]
    origin = table[2] + own_block * BLK

    def segment(n, _):
        begin = table[3 + n] - origin
        end = table[4 + n] - origin
        first = lax.div(jnp.maximum(begin, 0), BLK)
        tail = jnp.minimum(lax.div(end - 1, BLK), own_blocks - 1)
        last = jnp.minimum(lax.div(end - 1, BLK), blocks - 1)

        def transform(j, _):
            at = pl.multiple_of(j * BLK, BLK)
            mask = rows_mask(at, 2 * BLK, begin, end)
            spectra[j] = masked_spectrum(ahead[...], grads[pl.ds(at, 2 * BLK), :], mask)
            return 0

        lax.fori_loop(first, last + 1, transform, 0)
        for k in range(1, STEP):
            spectra[last + k] = jnp.zeros(spectra.shape[1:], f32)

        def produce(j, _):
            reach = lax.div(jnp.minimum(last - j, TAPS - 1) + STEP, STEP)
            for part in lanes(width):

                def lag(c, carry):
                    for k in range(STEP):
                        b = c * STEP + k
                        carry = multiply_add(carry, kernel, b, spectra, j + b, part, True)
                    return carry

                held = lax.fori_loop(0, reach, lag, no_sums())
                for k, pair in enumerate(groups()):
                    total[pair[0], part] = held[2 * k].astype(bf16)
                    total[pair[1], part] = held[2 * k + 1].astype(bf16)
            value = jnp.dot(back[...], total[...], preferred_element_type=f32)
            at = pl.multiple_of(j * BLK, BLK)
            mask = rows_mask(at, BLK, begin, end)
            signal_grad[pl.ds(at, BLK), :] = jnp.where(
                mask, value, signal_grad[pl.ds(at, BLK), :]
            )
            return 0

        lax.fori_loop(first, tail + 1, produce, 0)
        return 0

    lax.fori_loop(table[0], table[1] + 1, segment, 0)

    def strip(at):
        for part in lanes(width):
            where = (pl.ds(at, STRIP), part)
            value = signal_grad[where] + bias[0, :, part] * grads[where].astype(f32)
            gate_in_grad[where] = (value * values[where].astype(f32)).astype(bf16)
            values_grad[where] = (value * gate_in[where].astype(f32)).astype(bf16)

    each_strip(signal_grad.shape[0], STRIP, strip)


def kernel_backward_body(
    own_block, table, window, grads, causal, single, back, kernel_grad, spectra, own_spectra, sums
):
    blocks = spectra.shape[0] - STEP + 1
    width = kernel_grad.shape[1]
    origin = table[2]
    sums[...] = jnp.zeros_like(sums)

    def segment(n, _):
        begin = table[3 + n] - origin
        end = table[4 + n] - origin
        head = lax.div(begin, BLK)
        tail = jnp.minimum(lax.div(end - 1, BLK), blocks - 1)
        first = jnp.maximum(head, own_block)

        def transform(j, _):
            at = pl.multiple_of(j * BLK, BLK)
            mask = rows_mask(at - BLK, 2 * BLK, begin, end)
            spectra[j] = masked_spectrum(causal[...], window[pl.ds(at, 2 * BLK), :], mask)
            return 0

        lax.fori_loop(head, tail + 1, transform, 0)

        def transform_own(j, _):
            at = pl.multiple_of((j - own_block) * BLK, BLK)
            mask = rows_mask(j * BLK, BLK, begin, end)
            own_spectra[j - own_block] = masked_spectrum(
                single[...], grads[pl.ds(at, BLK), :], mask
            )
            return 0

        lax.fori_loop(first, tail + 1, transform_own, 0)
        for k in range(1, STEP):
            spectra[tail + k] = jnp.zeros(spectra.shape[1:], f32)
            own_spectra[tail - own_block + k] = jnp.zeros(own_spectra.shape[1:], f32)

        def accumulate(b, _):
            begin_at = jnp.maximum(first, head + b)
            for part in lanes(width):

                def at_blocks(c, carry):
                    for k in range(STEP):
                        j = begin_at + c * STEP + k
                        carry = multiply_add(
                            carry, spectra, j - b, own_spectra, j - own_block, part, True
                        )
                    return carry

                held = [sums[b, rows, part] for pair in groups() for rows in pair]
                count = lax.div(tail - begin_at + STEP, STEP)
                held = lax.fori_loop(0, count, at_blocks, tuple(held))
                for k, pair in enumerate(groups()):
                    sums[b, pair[0], part] = held[2 * k]
                    sums[b, pair[1], part] = held[2 * k + 1]
            return 0

        lax.fori_loop(0, jnp.minimum(tail - head, TAPS - 1) + 1, accumulate, 0)
        return 0

    lax.fori_loop(table[0], table[1] + 1, segment, 0)
    for b in range(TAPS):
        kernel_grad[b * BLK : (b + 1) * BLK, :] = jnp.dot(
            back[...], sums[b].astype(bf16), preferred_element_type=f32
        )


def norm_rows(values):
    centered = values - jnp.mean(values, -1, keepdims=True)
    rate = lax.rsqrt(jnp.mean(centered * centered, -1, keepdims=True) + epsilon)
    return centered * rate, rate


def norm_rows_back(grad, scaled, rate, gain):
    g = grad * gain
    return rate * (
        g - jnp.mean(g, -1, keepdims=True) - scaled * jnp.mean(g * scaled, -1, keepdims=True)
    )


def fold(values):
    return jnp.sum(values.reshape(values.shape[0] // 8, 8, values.shape[1]), axis=0)


def lanes(count):
    return [slice(q, q + 128) for q in range(0, count, 128)]


def dot(left, right):
    return jnp.dot(left, right, preferred_element_type=f32)


def dot_rows(left, right):
    return lax.dot_general(left, right, (((1,), (1,)), ((), ())), preferred_element_type=f32)


def each_strip(rows, step, body, copies=1):
    while rows % (step * copies):
        copies //= 2

    def run(c, _):
        for k in range(copies):
            body(pl.multiple_of((c * copies + k) * step, step))
        return 0

    lax.fori_loop(0, rows // (step * copies), run, 0)


def sum_strips(rows, step, body, zeros, copies=1):
    while rows % (step * copies):
        copies //= 2

    def run(c, totals):
        for k in range(copies):
            parts = body(pl.multiple_of((c * copies + k) * step, step))
            totals = tuple(total + part for total, part in zip(totals, parts))
        return totals

    return lax.fori_loop(0, rows // (step * copies), run, zeros)


def turn_into(target, chunk, at, order):
    turned = chunk.astype(bf16).T
    for first, size, place in order:
        target[pl.ds(place, size), at : at + chunk.shape[0]] = turned[first : first + size, :]


def in_forward_body(state, halo, norm, weight, bias, taps, age, *refs):
    normed, projected, gate_out, gate_in, values, signal, low, wide = refs
    rows = state.shape[0]

    @pl.when(pl.program_id(0) == 0)
    def _():
        gain, shift = norm[0:1, :], norm[1:2, :]
        low[:HALO, :] = (norm_rows(halo[...].astype(f32))[0] * gain + shift).astype(bf16)

        def strip(at):
            part = norm_rows(state[pl.ds(at, 32), :].astype(f32))[0] * gain + shift
            low[pl.ds(at + HALO, 32), :] = part.astype(bf16)
            normed[pl.ds(at, 32), :] = part.astype(bf16)

        each_strip(rows, 32, strip, 4)

    chunk = max(c for c in range(16, 273, 16) if (rows + HALO) % c == 0)

    def product(at):
        wide[pl.ds(at, chunk), :] = (
            dot(low[pl.ds(at, chunk), :], weight[0, :, : 3 * LANES]) + bias[0]
        )

    each_strip(rows + HALO, chunk, product)
    for part in range(3):
        projected[part, :HALO, :] = wide[:HALO, part * LANES : (part + 1) * LANES].astype(bf16)

    def strip(at):
        old = age[pl.ds(at, STRIP), :]
        for lane in lanes(LANES):
            mixed = []
            for part in range(3):
                cols = slice(part * LANES + lane.start, part * LANES + lane.stop)
                block = wide[pl.ds(at + HALO - 8, STRIP + 8), cols]
                now, once, twice = block[8:], block[7:-1], block[6:-2]
                projected[part, pl.ds(at + HALO, STRIP), lane] = now.astype(bf16)
                mixed.append(
                    taps[0, 0:1, cols] * now
                    + jnp.where(old >= 1, taps[0, 1:2, cols] * once, 0.0)
                    + jnp.where(old >= 2, taps[0, 2:3, cols] * twice, 0.0)
                )
            for ref, value in zip((gate_out, gate_in, values), mixed):
                ref[pl.ds(at, STRIP), lane] = value.astype(bf16)
            signal[pl.ds(at, STRIP), lane] = (mixed[1] * mixed[2]).astype(bf16)

    each_strip(rows, STRIP, strip)


def ff_forward_body(
    out_blocks, mixer, state, norm, shifts, weight, bias, *refs
):
    outs = refs[:out_blocks]
    middle, second, activated, slope, result, result_low, hidden = refs[out_blocks:]
    rows = state.shape[0]
    chunk = min(512, rows)

    @pl.when(pl.program_id(0) == 0)
    def _():
        def product(at):
            total = state[pl.ds(at, chunk), :].astype(f32) + shifts[0:1, :]
            for n, out in enumerate(outs):
                total += dot_rows(
                    mixer[pl.ds(at, chunk), n * LANES : (n + 1) * LANES], out[0]
                )
            middle[pl.ds(at, chunk), :] = total

        each_strip(rows, chunk, product)

        def strip(at):
            part = middle[pl.ds(at, 64), :]
            result[pl.ds(at, 64), :] = part + shifts[1:2, :]
            second[pl.ds(at, 64), :] = (
                norm_rows(part)[0] * norm[0:1, :] + norm[1:2, :]
            ).astype(bf16)

        each_strip(rows, 64, strip, 2)

    def product(at):
        hidden[...] = dot(second[pl.ds(at, chunk), :], weight[0, :, :HIDDEN]) + bias[0]

        def strip(inner):
            for lane in lanes(HIDDEN):
                before = hidden[pl.ds(inner, STRIP), lane]
                cumulative = 0.5 + 0.5 * lax.erf(before * math.sqrt(0.5))
                bell = jnp.exp(-0.5 * before * before) * (1.0 / math.sqrt(2 * math.pi))
                activated[pl.ds(at + inner, STRIP), lane] = (before * cumulative).astype(bf16)
                slope[pl.ds(at + inner, STRIP), lane] = (cumulative + before * bell).astype(bf16)

        each_strip(chunk, STRIP, strip)
        result[pl.ds(at, chunk), :] += dot_rows(
            activated[pl.ds(at, chunk), :], weight[0, :, HIDDEN:]
        )

    each_strip(rows, chunk, product)

    @pl.when(pl.program_id(0) == pl.num_programs(0) - 1)
    def _():
        def strip(at):
            result_low[pl.ds(at, STRIP), :] = result[pl.ds(at, STRIP), :].astype(bf16)

        each_strip(rows, STRIP, strip, 2)


def row_order(split, mine, size):
    if not split:
        return [(0, D, 0)]
    runs = []
    for run in range(D // size):
        slot = (run % 2) ^ mine
        place = pl.multiple_of(slot * (D // 2) + run // 2 * size, 16)
        runs.append((run * size, size, place))
    return runs


def ff_backward_body(
    split, place, grad, second, middle, norm, activated, slope, weight, *refs
):
    middle_grad, middle_low, weight_grad, bias_grad, sums = refs[-10:-5]
    grad_low, grad_turned, second_turned, hidden, hidden_low = refs[-5:]
    rows = grad.shape[0]
    chunk = min(512, rows)
    order = row_order(split, place[0], 0 if not split else split)

    @pl.when(pl.program_id(0) == 0)
    def _():
        for at in range(0, rows, chunk):
            turn_into(grad_turned, grad[at : at + chunk, :], at, order)
            turn_into(second_turned, second[at : at + chunk, :], at, order)

        def strip(at):
            grad_low[pl.ds(at, 32), :] = grad[pl.ds(at, 32), :].astype(bf16)
            middle_grad[pl.ds(at, 32), :] = jnp.zeros((32, D), f32)

        each_strip(rows, 32, strip, 4)
        sums[...] = jnp.zeros_like(sums)
    bias_grad[...] = jnp.zeros_like(bias_grad)

    def product(at):
        hidden[...] = dot(grad_low[pl.ds(at, chunk), :], weight[0, :, HIDDEN:])

        def strip(inner):
            totals = []
            for lane in lanes(HIDDEN):
                part = hidden[pl.ds(inner, STRIP), lane] * slope[
                    pl.ds(at + inner, STRIP), lane
                ].astype(f32)
                hidden_low[pl.ds(at + inner, STRIP), lane] = part.astype(bf16)
                totals.append(fold(part))
            return totals

        zero = jnp.zeros((8, 128), f32)
        totals = sum_strips(chunk, STRIP, strip, (zero,) * (HIDDEN // 128))
        for lane, total in zip(lanes(HIDDEN), totals):
            bias_grad[0, :, lane] += jnp.sum(total, axis=0, keepdims=True)
        middle_grad[pl.ds(at, chunk), :] += dot_rows(
            hidden_low[pl.ds(at, chunk), :], weight[0, :, :HIDDEN]
        )

    each_strip(rows, chunk, product)

    def product_weight(at):
        weight_grad[0, pl.ds(at, 256), :HIDDEN] = dot(
            second_turned[pl.ds(at, 256), :], hidden_low[...]
        ).astype(bf16)
        weight_grad[0, pl.ds(at, 256), HIDDEN:] = dot(
            grad_turned[pl.ds(at, 256), :], activated[...]
        ).astype(bf16)

    each_strip(D, 256, product_weight)

    @pl.when(pl.program_id(0) == pl.num_programs(0) - 1)
    def _():
        def strip(at):
            above = grad[pl.ds(at, 128), :].astype(f32)
            inner = middle_grad[pl.ds(at, 128), :]
            scaled, rate = norm_rows(middle[pl.ds(at, 128), :])
            total = above + norm_rows_back(inner, scaled, rate, norm[0:1, :])
            middle_grad[pl.ds(at, 128), :] = total
            middle_low[pl.ds(at, 128), :] = total.astype(bf16)
            for k, part in enumerate((above, inner * scaled, inner, total)):
                sums[k] += fold(part)

        each_strip(rows, 128, strip)


def gates_backward_body(
    middle_low, weight, gate_out, carried, signal, carried_grad, gate_grad, bias_grad, product_ref
):
    rows = middle_low.shape[0]
    chunk = min(512, rows)
    bias_grad[...] = jnp.zeros_like(bias_grad)

    def product(at):
        product_ref[...] = dot(middle_low[pl.ds(at, chunk), :], weight[0])

        def strip(inner):
            totals = []
            for lane in lanes(LANES):
                part = product_ref[pl.ds(inner, STRIP), lane]
                where = (pl.ds(at + inner, STRIP), lane)
                grown = part * gate_out[where].astype(f32)
                carried_grad[where] = grown.astype(bf16)
                gate_grad[where] = (part * carried[where].astype(f32)).astype(bf16)
                totals.append(fold(grown * signal[where].astype(f32)))
            return totals

        zero = jnp.zeros((8, 128), f32)
        totals = sum_strips(chunk, STRIP, strip, (zero,) * (LANES // 128))
        for lane, total in zip(lanes(LANES), totals):
            bias_grad[0, :, lane] += jnp.sum(total, axis=0, keepdims=True)

    each_strip(rows, chunk, product)


def in_backward_body(
    split, place, first_grad, second_grad, third_grad, halo, age, projected, taps, normed,
    middle_low, mixer, weight, state, middle_grad, norm,
    grad, grad_out, bias_grad, taps_grad, sums, *refs
):
    normed_turned, middle_turned, spread, low = refs[-4:]
    weight_grads = refs[:-4]
    rows = normed.shape[0]
    chunk = min(512, rows)
    order = row_order(split, place[0], 0 if not split else split)

    @pl.when(pl.program_id(0) == 0)
    def _():
        for at in range(0, rows, chunk):
            turn_into(normed_turned, normed[at : at + chunk, :], at, order)
            turn_into(middle_turned, middle_low[at : at + chunk, :], at, order)
        sums[...] = jnp.zeros_like(sums)

        def strip(at):
            grad[pl.ds(at, 32), :] = jnp.zeros((32, D), f32)

        each_strip(rows, 32, strip, 4)

    for part, ref in enumerate((first_grad, second_grad, third_grad)):
        cols = slice(part * LANES, (part + 1) * LANES)

        def strip(at):
            spread[pl.ds(at, STRIP), cols] = ref[pl.ds(at, STRIP), :]

        each_strip(rows, STRIP, strip)
        spread[rows:, cols] = halo[part]

    for part in range(3):

        def strip(at):
            old = age[pl.ds(at, STRIP + HALO), :]
            mine, after_one, after_two = old[:STRIP], old[1 : STRIP + 1], old[2 : STRIP + 2]
            totals = []
            for lane in lanes(LANES):
                cols = slice(part * LANES + lane.start, part * LANES + lane.stop)
                block = spread[pl.ds(at, STRIP + HALO), cols].astype(f32)
                source = projected[part, pl.ds(at, STRIP + HALO), lane].astype(f32)
                now = block[:STRIP]
                total = (
                    taps[0, 0:1, cols] * now
                    + jnp.where(after_one >= 1, taps[0, 1:2, cols] * block[1 : STRIP + 1], 0.0)
                    + jnp.where(after_two >= 2, taps[0, 2:3, cols] * block[2 : STRIP + 2], 0.0)
                )
                low[pl.ds(at, STRIP), cols] = total.astype(bf16)
                totals += [
                    fold(now * source[HALO:]),
                    fold(jnp.where(mine >= 1, now * source[HALO - 1 : -1], 0.0)),
                    fold(jnp.where(mine >= 2, now * source[HALO - 2 : -2], 0.0)),
                    fold(total),
                ]
            return totals

        zero = jnp.zeros((8, 128), f32)
        totals = sum_strips(rows, STRIP, strip, (zero,) * (4 * LANES // 128))
        for q, lane in enumerate(lanes(LANES)):
            cols = slice(part * LANES + lane.start, part * LANES + lane.stop)
            for tap in range(3):
                taps_grad[0, tap : tap + 1, cols] = jnp.sum(
                    totals[4 * q + tap], axis=0, keepdims=True
                )
            bias_grad[0, :, cols] = jnp.sum(totals[4 * q + 3], axis=0, keepdims=True)

    def product(at):
        grad[pl.ds(at, chunk), :] += dot_rows(
            low[pl.ds(at, chunk), :], weight[0, :, : 3 * LANES]
        )

    each_strip(rows, chunk, product)

    size = D // len(weight_grads)
    for k, weight_grad in enumerate(weight_grads):

        def product_weight(at):
            source = pl.ds(k * size + at, 192)
            weight_grad[0, pl.ds(at, 192), : 3 * LANES] = dot(
                normed_turned[source, :], low[...]
            ).astype(bf16)
            weight_grad[0, pl.ds(at, 192), 3 * LANES :] = dot(
                middle_turned[source, :], mixer[...]
            ).astype(bf16)

        each_strip(size, 192, product_weight)

    @pl.when(pl.program_id(0) == pl.num_programs(0) - 1)
    def _():
        def strip(at):
            inner = grad[pl.ds(at, 128), :]
            scaled, rate = norm_rows(state[pl.ds(at, 128), :].astype(f32))
            total = middle_grad[pl.ds(at, 128), :] + norm_rows_back(
                inner, scaled, rate, norm[0:1, :]
            )
            grad[pl.ds(at, 128), :] = total
            grad_out[pl.ds(at, 128), :] = total.astype(bf16)
            for k, part in enumerate((inner * scaled, inner)):
                sums[k] += fold(part)

        each_strip(rows, 128, strip)


def whole(shape):
    return pl.BlockSpec(
        shape, lambda i, *_: (0,) * len(shape), pipeline_mode=pl.Buffered(1)
    )


def by_lane(shape):
    return pl.BlockSpec(shape, lambda i, *_: (0,) * (len(shape) - 1) + (i,))


def by_first(shape):
    return pl.BlockSpec(shape, lambda i, *_: (i,) + (0,) * (len(shape) - 1))


def weight_block(wide, per, first=0, stride=1, depth=D):
    return pl.BlockSpec(
        (1, depth, wide), lambda i, *_: (i // per, 0, first + stride * (i % per))
    )


def run(body, name, grid, scalars, ins, outs, scratch, flops, moved, limit=48, aliases={}):
    arrays, in_specs = zip(*ins)
    shapes, out_specs = zip(*outs)
    return pl.pallas_call(
        body,
        out_shape=shapes,
        grid_spec=pltpu.PrefetchScalarGridSpec(
            num_scalar_prefetch=len(scalars),
            grid=(grid,),
            in_specs=in_specs,
            out_specs=out_specs,
            scratch_shapes=scratch,
        ),
        compiler_params=pltpu.CompilerParams(vmem_limit_bytes=limit << 20),
        input_output_aliases=aliases,
        cost_estimate=pl.CostEstimate(flops=flops, bytes_accessed=moved, transcendentals=0),
        name=name,
    )(*scalars, *arrays)


def shape_of(dims, kind):
    return jax.ShapeDtypeStruct(dims, kind)


def in_forward(state, halo, norm, weights, first, per, bias, taps, age):
    rows = state.shape[0]
    blocks = D // LANES
    low = (shape_of((rows, D), bf16), by_lane((rows, LANES)))
    return run(
        in_forward_body, "in_forward", blocks, (),
        [
            (state, whole((rows, D))), (halo, whole((HALO, D))), (norm, whole((2, D))),
            (weights, weight_block(4 * LANES, per, first)),
            (bias, by_first((1, 1, 3 * LANES))), (taps, by_first((1, 3, 3 * LANES))),
            (age, whole(age.shape)),
        ],
        [
            (shape_of((rows, D), bf16), whole((rows, D))),
            (shape_of((3, rows + HALO, D), bf16), by_lane((3, rows + HALO, LANES))),
            low, low, low, low,
        ],
        [pltpu.VMEM((rows + HALO, D), bf16), pltpu.VMEM((rows + HALO, 3 * LANES), f32)],
        2 * rows * D * 3 * D, 20_000_000, 30,
    )


def ff_forward(mixer, state, norm, shifts, weights, per, hidden_per, bias, mix, first):
    rows = state.shape[0]
    hidden_blocks = FF // HIDDEN
    row = (rows, D)
    tall = (shape_of((rows, FF), bf16), by_lane((rows, HIDDEN)))
    out_specs = [
        pl.BlockSpec(
            (1, D, LANES), lambda i, *_, n=n: (n // per, 0, 4 * (first + n % per) + 3)
        )
        for n in range(D // LANES)
    ]
    return run(
        functools.partial(ff_forward_body, D // LANES), "ff_forward", hidden_blocks, (),
        [
            (mixer, whole(row)), (state, whole(row)), (norm, whole((2, D))),
            (shifts, whole((2, D))),
            (weights, weight_block(2 * HIDDEN, hidden_per)),
            (bias, by_first((1, 1, HIDDEN))),
        ]
        + [(mix, spec) for spec in out_specs],
        [
            (shape_of(row, f32), whole(row)), (shape_of(row, bf16), whole(row)), tall, tall,
            (shape_of(row, f32), whole(row)), (shape_of(row, bf16), whole(row)),
        ],
        [pltpu.VMEM((min(512, rows), HIDDEN), f32)],
        2 * rows * D * (2 * FF + D), 40_000_000, 32,
    )


def ff_backward(
    split, place, grad, second, middle, norm, activated, slope, weights, hidden_per, shared
):
    rows = grad.shape[0]
    row = (rows, D)
    hidden_blocks = FF // HIDDEN
    halves = weights.shape[0]
    grads = shape_of((halves, D, 2 * FF // halves) if shared is None else shared.shape, bf16)
    base = [] if shared is None else [(shared, pl.BlockSpec(memory_space=pl.ANY))]
    return run(
        functools.partial(ff_backward_body, split), "ff_backward", hidden_blocks, (place,),
        [
            (grad, whole(row)), (second, whole(row)), (middle, whole(row)), (norm, whole((2, D))),
            (activated, by_lane((rows, HIDDEN))), (slope, by_lane((rows, HIDDEN))),
            (weights, weight_block(2 * HIDDEN, hidden_per)),
        ]
        + base,
        [
            (shape_of(row, f32), whole(row)), (shape_of(row, bf16), whole(row)),
            (grads, weight_block(2 * HIDDEN, hidden_per)),
            (shape_of((hidden_blocks, 1, HIDDEN), f32), by_first((1, 1, HIDDEN))),
            (shape_of((4, 8, D), f32), whole((4, 8, D))),
        ],
        [
            pltpu.VMEM(row, bf16), pltpu.VMEM((D, rows), bf16), pltpu.VMEM((D, rows), bf16),
            pltpu.VMEM((min(512, rows), HIDDEN), f32), pltpu.VMEM((rows, HIDDEN), bf16),
        ],
        8 * rows * D * FF, 50_000_000, 40, {8: 2} if base else {},
    )


def gates_backward(middle_low, weights, first, per, gate_out, carried, signal):
    rows = middle_low.shape[0]
    block = (rows, LANES)
    low = (shape_of((rows, D), bf16), by_lane(block))
    return run(
        gates_backward_body, "gates_backward", D // LANES, (),
        [
            (middle_low, whole((rows, D))), (weights, weight_block(LANES, per, 4 * first + 3, 4)),
            (gate_out, by_lane(block)), (carried, by_lane(block)), (signal, by_lane(block)),
        ],
        [
            low, low,
            (shape_of((D // LANES, 1, LANES), f32), by_first((1, 1, LANES))),
        ],
        [pltpu.VMEM((min(512, rows), LANES), f32)],
        2 * rows * D * D, 10_000_000, 20,
    )


def in_backward(
    split, place, mixed_grads, halo, age, projected, taps, normed, middle_low, mixer, weights,
    first, per, state, middle_grad, norm, columns, grad_first,
):
    rows = normed.shape[0]
    row, block = (rows, D), (rows, LANES)
    blocks = D // LANES
    count = 2 if split else 1
    grads = (
        shape_of((weights.shape[0], D // count, columns), bf16),
        weight_block(4 * LANES, per, grad_first, depth=D // count),
    )
    return run(
        functools.partial(in_backward_body, split), "in_backward", blocks, (place,),
        [(part, by_lane(block)) for part in mixed_grads]
        + [
            (halo, by_lane((3, HALO, LANES))), (age, whole(age.shape)),
            (projected, by_lane((3, rows + HALO, LANES))), (taps, by_first((1, 3, 3 * LANES))),
            (normed, whole(row)), (middle_low, whole(row)), (mixer, by_lane(block)),
            (weights, weight_block(4 * LANES, per, first)), (state, whole(row)),
            (middle_grad, whole(row)), (norm, whole((2, D))),
        ],
        [
            (shape_of(row, f32), whole(row)), (shape_of(row, bf16), whole(row)),
            (shape_of((blocks, 1, 3 * LANES), f32), by_first((1, 1, 3 * LANES))),
            (shape_of((blocks, 3, 3 * LANES), f32), by_first((1, 3, 3 * LANES))),
            (shape_of((2, 8, D), f32), whole((2, 8, D))),
        ]
        + [grads] * count,
        [
            pltpu.VMEM((D, rows), bf16), pltpu.VMEM((D, rows), bf16),
            pltpu.VMEM((rows + HALO, 3 * LANES), bf16), pltpu.VMEM((rows, 3 * LANES), bf16),
        ],
        2 * rows * D * 7 * D, 40_000_000, 46,
    )


def conv_forward(table, window, kernel, gate_out, bias, rows, tables):
    causal, _, _, back = tables
    wide = window.shape[0]
    blocks = wide // BLK - 1
    own_block = (wide - BLK - rows) // BLK
    low = (shape_of((rows, D), bf16), by_lane((rows, CONV_LANES)))
    return run(
        functools.partial(conv_forward_body, own_block), "conv_forward", D // CONV_LANES, (table,),
        [
            (window, by_lane((wide, CONV_LANES))), (kernel, by_lane((TAPS, 2 * BLK, CONV_LANES))),
            (gate_out, by_lane((rows, CONV_LANES))), (bias, by_first((1, 1, CONV_LANES))),
            (causal, whole((2 * BLK, 2 * BLK))), (back, whole((BLK, 2 * BLK))),
        ],
        [low, low],
        [
            pltpu.VMEM((rows, CONV_LANES), f32),
            pltpu.VMEM((blocks + STEP - 1, 2 * BLK, CONV_LANES), f32),
            pltpu.VMEM((2 * BLK, CONV_LANES), bf16),
        ],
        20_000_000_000, 20_000_000, 28,
    )


def signal_backward(table, grads, kernel, values, gate_in, bias, rows, hops, tables):
    _, ahead, _, back = tables
    wide = grads.shape[0]
    low = (shape_of((rows, D), bf16), by_lane((rows, CONV_LANES)))
    return run(
        functools.partial(signal_backward_body, hops * rows // BLK), "signal_backward",
        D // CONV_LANES, (table,),
        [
            (grads, by_lane((wide, CONV_LANES))),
            (kernel, by_lane((TAPS, 2 * BLK, CONV_LANES))), (values, by_lane((rows, CONV_LANES))),
            (gate_in, by_lane((rows, CONV_LANES))), (bias, by_first((1, 1, CONV_LANES))),
            (ahead, whole((2 * BLK, 2 * BLK))), (back, whole((BLK, 2 * BLK))),
        ],
        [low, low],
        [
            pltpu.VMEM((rows, CONV_LANES), f32),
            pltpu.VMEM((wide // BLK + STEP - 2, 2 * BLK, CONV_LANES), f32),
            pltpu.VMEM((2 * BLK, CONV_LANES), bf16),
        ],
        20_000_000_000, 20_000_000, 32,
    )


def kernel_backward(table, window, grads, rows, tables):
    causal, _, single, back = tables
    wide = window.shape[0]
    blocks = wide // BLK - 1
    own_block = (wide - BLK - rows) // BLK
    return run(
        functools.partial(kernel_backward_body, own_block), "kernel_backward",
        D // CONV_LANES, (table,),
        [
            (window, by_lane((wide, CONV_LANES))), (grads, by_lane((rows, CONV_LANES))),
            (causal, whole((2 * BLK, 2 * BLK))), (single, whole((2 * BLK, BLK))),
            (back, whole((BLK, 2 * BLK))),
        ],
        [(shape_of((LMAX, D), f32), by_lane((LMAX, CONV_LANES)))],
        [
            pltpu.VMEM((blocks + STEP - 1, 2 * BLK, CONV_LANES), f32),
            pltpu.VMEM((rows // BLK + STEP - 1, 2 * BLK, CONV_LANES), f32),
            pltpu.VMEM((TAPS, 2 * BLK, CONV_LANES), f32),
        ],
        20_000_000_000, 20_000_000, 32,
    )[0]


def shards(
    tokens,
    out_grad,
    seq_lengths,
    deal_order,
    input_weight,
    output_weight,
    up_projection_weight,
    down_projection_weight,
    input_bias,
    short_taps,
    filter_first,
    filter_inner,
    filter_biases,
    filter_rates,
    filter_out,
    conv_bias,
    norm_gains,
    norm_biases,
    output_biases,
    up_projection_bias,
):
    tensor_count = lax.axis_size("tensor")
    chips = lax.axis_size("chip")
    cores = lax.axis_size("core")
    devices = tensor_count * chips * cores
    core = lax.axis_index("core")
    rank = (lax.axis_index("chip") * cores + core) * tensor_count + lax.axis_index("tensor")
    rows = tokens.shape[0]
    width = input_weight.shape[3]
    hidden = up_projection_weight.shape[2]
    depth = input_weight.shape[2]
    count = seq_lengths.shape[0]
    everyone = ("chip", "core", "tensor")
    owners = ("tensor", "chip", "core")
    hops = -(-(LMAX - 1) // rows)
    direct = width % LANES == 0 and hidden % HIDDEN == 0
    per = width // LANES if direct else D // LANES
    hidden_per = hidden // HIDDEN if direct else FF // HIDDEN
    halves = tensor_count if direct else 1
    paired = (
        direct and depth % 16 == 0 and cores == 2 and tensor_count == 2
        and chips > 1 and chips & (chips - 1) == 0
    )
    split = depth if paired else 0
    chip, side = lax.axis_index("chip"), lax.axis_index("tensor")
    plane, row, planes = chip // 2, chip % 2, chips // 2

    def swap(values, mask):
        pairs = [(i, i ^ mask) for i in range(chips * tensor_count)]
        return lax.ppermute(values, ("chip", "tensor"), pairs)

    def swap_core(values):
        return lax.ppermute(values, "core", [(0, 1), (1, 0)])

    def pick(values, index, axis=0):
        return lax.dynamic_index_in_dim(values, index, axis, False)

    def gather_pairs(values, beside):
        n = values.shape[-1]
        parts = jnp.stack([values] + [swap(values, k << 2) for k in range(1, planes)])
        values = jnp.stack([pick(parts, k ^ plane) for k in range(planes)])
        parts = jnp.stack([values] + [swap(values, k) for k in range(1, 4)])
        mine = row * 2 + side
        values = jnp.stack(
            [
                jnp.stack([pick(parts, (2 * r + s) ^ mine) for r in range(2)], axis=1)
                for s in range(2)
            ]
        )
        values, beside = lax.optimization_barrier((values, beside))
        other = swap_core(values)
        values = jnp.stack(
            [jnp.where(core == 0, values, other), jnp.where(core == 0, other, values)], axis=3
        )
        return values.reshape(2, D, n), beside

    def total_of(parts, mine):
        held = jnp.stack(parts)
        total = pick(held, mine).astype(f32)
        for k in range(1, len(parts)):
            total += pick(held, k ^ mine).astype(f32)
        return total

    def reduce_plane(total):
        total = total.reshape(2, planes, 2, depth, -1)

        def block(s, r):
            return pick(pick(total, s), r, 1)

        parts = [swap(block(side ^ (k % 2), row ^ (k // 2)), k) for k in range(1, 4)]
        total = block(side, row).astype(f32)
        for part in parts:
            total += part.astype(f32)
        low = total.astype(bf16)
        parts = [swap(pick(low, plane ^ k), k << 2) for k in range(1, planes)]
        total = pick(total, plane)
        for part in parts:
            total += part.astype(f32)
        return total

    def reduce_all(extra):
        def rounded(values):
            return lax.optimization_barrier(values.astype(bf16))

        if paired:
            low = rounded(extra)
            low = rounded(low.astype(f32) + swap_core(low).astype(f32))
            parts = [low] + [swap(low, k) for k in range(1, 4)]
            extra = total_of(parts, row * 2 + side)
            for k in range((planes - 1).bit_length()):
                low = rounded(extra)
                extra = low.astype(f32) + swap(low, 4 << k).astype(f32)
            return extra
        step = 1
        while step < devices:
            low = rounded(extra)
            other = lax.ppermute(low, everyone, [(i, i ^ step) for i in range(devices)])
            extra = low.astype(f32) + other.astype(f32)
            step *= 2
        return extra

    def from_before(values, hop=1):
        return lax.ppermute(values, everyone, [(i, i + hop) for i in range(devices - hop)])

    def from_after(values, hop=1):
        return lax.ppermute(values, everyone, [(i + hop, i) for i in range(devices - hop)])

    def join_columns(ins, out, up, down, mix_blocks, ff_blocks):
        lead = out.shape[:-1]
        mix = jnp.stack(
            [part.reshape(*lead, mix_blocks, -1) for part in (*ins, out)], axis=-2
        ).reshape(*lead, -1)
        ff = jnp.stack(
            [part.reshape(*lead, ff_blocks, -1) for part in (up, down)], axis=-2
        ).reshape(*lead, -1)
        return mix, ff

    def part_columns(mix, ff, mix_blocks, ff_blocks):
        def strided(values, blocks, kinds, k):
            size = values.shape[-1] // (blocks * kinds)
            starts = [(kinds * b + k) * size for b in range(blocks)]
            return jnp.concatenate([values[..., at : at + size] for at in starts], axis=-1)

        mixes = [strided(mix, mix_blocks, 4, k) for k in range(4)]
        return mixes[:3], mixes[3], *[strided(ff, ff_blocks, 2, k) for k in range(2)]

    local_mix = per if direct else 1
    local_ff = hidden_per if direct else 1
    local = []
    for layer in range(LAYERS):
        local.append(
            join_columns(
                [input_weight[layer, k].astype(bf16) for k in range(3)],
                jnp.transpose(output_weight[layer].astype(bf16)),
                up_projection_weight[layer].astype(bf16),
                jnp.transpose(down_projection_weight[layer].astype(bf16)),
                local_mix,
                local_ff,
            )
        )

    def gather(part):
        return lax.all_gather(part, owners, axis=0, tiled=True).reshape(tensor_count, D, -1)

    tables = tuple(jnp.asarray(t, f32).astype(bf16) for t in wave_tables())
    positions = positions_table(LMAX)
    modulation = decay_table(LMAX)
    blank = jnp.zeros((BLK, D), bf16)

    filters = []
    for layer in range(LAYERS):
        inner, filter_back = jax.vjp(
            lambda a, b, c, d: filter_hidden(positions, a, b, c, d),
            filter_first[layer],
            filter_inner[layer],
            filter_biases[layer],
            filter_rates[layer],
        )
        kernel = jnp.dot(inner, filter_out[layer], precision=highest) * modulation
        kernel_spectra = jnp.einsum(
            "kr,brc->bkc",
            tables[2],
            kernel.reshape(TAPS, BLK, D).astype(bf16),
            preferred_element_type=f32,
        )
        filters.append((inner, filter_back, kernel_spectra))

    gathered = []
    if paired:
        shared = gather(jnp.concatenate([local[0][1], local[1][0]], axis=1))
        last = gather(local[1][1])
        inner, filter_back, kernel_spectra = filters[0]
        mix, kernel_spectra = gather_pairs(local[0][0], kernel_spectra)
        filters[0] = (inner, filter_back, kernel_spectra)
        gathered.append((mix, 0, shared))
        gathered.append((shared[:, :, 2 * hidden :], 0, last))
    else:
        for mix, ff in local:
            mix, ff = gather(mix), gather(ff)
            if not direct:
                ins, out, up, down = part_columns(mix, ff, local_mix, local_ff)

                def full(piece):
                    return jnp.transpose(piece, (1, 0, 2)).reshape(1, D, -1)

                mix, ff = join_columns(
                    [full(k) for k in ins], full(out), full(up), full(down), per, hidden_per
                )
            gathered.append((mix, 0, ff))

    numbers = jnp.arange(count, dtype=jnp.int32)
    match = deal_order[:, None] == numbers[None, :]
    lengths = jnp.sum(jnp.where(match, seq_lengths[:, None], 0), axis=0)
    ends = jnp.sum(jnp.where(numbers[:, None] <= numbers[None, :], lengths[:, None], 0), axis=0)
    starts = ends - lengths
    base = rank * rows
    first_segment = jnp.sum((starts <= base).astype(jnp.int32)) - 1
    last_segment = jnp.sum((starts < base + rows).astype(jnp.int32)) - 1
    table = jnp.concatenate(
        [
            jnp.stack([first_segment, last_segment, base - hops * rows]),
            starts,
            ends[count - 1 :],
        ]
    ).astype(jnp.int32)

    def ages(places):
        begun = jnp.max(jnp.where(starts[None, :] <= places[:, None], starts[None, :], 0), axis=1)
        return jnp.broadcast_to((places - begun)[:, None], (places.shape[0], 128))

    age = ages(base + jnp.arange(rows + HALO, dtype=jnp.int32))
    place = core.astype(jnp.int32).reshape(1)

    def by_block(values):
        lead = values.shape[:-2]
        split_up = values.reshape(*lead, 3, D // LANES, LANES)
        return jnp.moveaxis(split_up, -2, 0).reshape(D // LANES, *lead, 3 * LANES)

    def from_block(values):
        lead = values.shape[1:-1]
        split_up = values.reshape(D // LANES, *lead, 3, LANES)
        return jnp.moveaxis(split_up, 0, -2).reshape(*lead, 3, D)

    state = tokens
    kept = []
    outputs = []
    for layer in range(LAYERS):
        mix_weights, first, ff_weights = gathered[layer]
        first_norm = jnp.stack([norm_gains[layer, 0], norm_biases[layer, 0]])
        second_norm = jnp.stack([norm_gains[layer, 1], norm_biases[layer, 1]])
        taps = by_block(short_taps[layer])
        lane_bias = conv_bias[layer].reshape(D // CONV_LANES, 1, CONV_LANES)
        shared_in = (
            first_norm, mix_weights, first, per, by_block(input_bias[layer][None]), taps
        )
        near = from_before(state[rows - HALO :])
        normed, projected, gate_out, gate_in, values, signal = in_forward(
            state, near, *shared_in, age
        )
        before = [from_before(signal, hop) for hop in range(hops, 0, -1)]
        window = jnp.concatenate([blank, *before, signal])
        carried, mixer = conv_forward(
            table, window, filters[layer][2], gate_out, lane_bias, rows, tables
        )
        middle, second, activated, slope, result, result_low = ff_forward(
            mixer, state, second_norm, output_biases[layer], ff_weights, per, hidden_per,
            up_projection_bias[layer].reshape(FF // HIDDEN, 1, HIDDEN), mix_weights, first,
        )
        outputs.append(result_low)
        kept.append(
            (
                state, first_norm, second_norm, taps, lane_bias, normed, projected, gate_out,
                gate_in, values, signal, window, carried, mixer, middle, second, activated, slope,
            )
        )
        state = result

    grad = out_grad
    owned, owned_ff = {}, {}
    ff_columns = 2 * FF // halves
    shared = None
    small = [None] * LAYERS

    def share(part):
        return lax.psum_scatter(
            part.reshape(tensor_count * D, -1), owners, scatter_dimension=0, tiled=True
        )

    for layer in reversed(range(LAYERS)):
        joint = paired and layer == LAYERS - 1
        mix_columns = 4 * D // halves + (ff_columns if joint else 0)
        mix_first = ff_columns // (4 * LANES) if joint else 0
        (
            state, first_norm, second_norm, taps, lane_bias, normed, projected, gate_out,
            gate_in, values, signal, window, carried, mixer, middle, second, activated, slope,
        ) = kept[layer]
        mix_weights, first, ff_weights = gathered[layer]
        inner, filter_back, kernel_spectra = filters[layer]
        middle_grad, middle_low, ff_grad, up_bias_grad, ff_sums = ff_backward(
            0, place, grad, second, middle, second_norm, activated, slope, ff_weights, hidden_per,
            shared,
        )
        carried_grad, gate_grad, conv_bias_grad = gates_backward(
            middle_low, mix_weights, first, per, gate_out, carried, signal
        )
        ahead = [from_after(carried_grad, hop) for hop in range(1, hops + 1)]
        kernel_grad = kernel_backward(table, window, carried_grad, rows, tables)
        shaped = kernel_grad * modulation
        filter_out_grad = jnp.dot(jnp.transpose(inner), shaped, precision=highest)
        inner_grad = jnp.dot(shaped, jnp.transpose(filter_out[layer]), precision=highest)
        filter_grads = filter_back(inner_grad)
        ahead, filter_grads, filter_out_grad = lax.optimization_barrier(
            (ahead, filter_grads, filter_out_grad)
        )
        grads_window = jnp.concatenate([carried_grad] + ahead + [blank])
        gate_in_grad, values_grad = signal_backward(
            table, grads_window, kernel_spectra, values, gate_in, lane_bias, rows, hops, tables
        )
        mixed_grads = (gate_grad, gate_in_grad, values_grad)
        after = from_after(jnp.stack([part[:HALO] for part in mixed_grads]))
        grad, grad_low, in_bias_grad, taps_grad, in_sums, *mix_grad = in_backward(
            0 if joint else split, place, mixed_grads, after, age, projected, taps, normed, middle_low, mixer,
            mix_weights, first, per, state, middle_grad, first_norm, mix_columns, mix_first,
        )

        if len(mix_grad) == 1:
            mix_grad = mix_grad[0]
        if not direct:
            ins, out, up, down = part_columns(mix_grad, ff_grad, per, hidden_per)

            def by_owner(piece):
                piece = piece.reshape(D, tensor_count, -1)
                return jnp.transpose(piece, (1, 0, 2))

            mix_grad, ff_grad = join_columns(
                [by_owner(k) for k in ins], by_owner(out), by_owner(up), by_owner(down), 1, 1
            )

        if not paired:
            owned[layer], owned_ff[layer] = share(mix_grad), share(ff_grad)
        elif layer == LAYERS - 1:
            owned_ff[layer] = share(ff_grad)
            shared = mix_grad
        else:
            both = share(ff_grad)
            owned_ff[layer] = both[:, :ff_columns]
            owned[layer + 1] = both[:, ff_columns:]
            last_grads = mix_grad

        ff_sums = jnp.sum(ff_sums, axis=1)
        in_sums = jnp.sum(in_sums, axis=1)
        small[layer] = (
            from_block(in_bias_grad)[0],
            from_block(taps_grad),
            *filter_grads,
            filter_out_grad,
            conv_bias_grad.reshape(D),
            jnp.stack([in_sums[0], ff_sums[1]]),
            jnp.stack([in_sums[1], ff_sums[2]]),
            jnp.stack([ff_sums[3], ff_sums[0]]),
            up_bias_grad.reshape(FF),
        )

    narrow = range(2, 6)
    filter_size = filter_first.shape[2]

    def as_rows(layer):
        thin = jnp.concatenate([small[layer][k].reshape(-1, filter_size) for k in narrow])
        thin = jnp.pad(thin, ((0, -thin.shape[0] % (D // filter_size)), (0, 0)))
        wide = [small[layer][k].reshape(-1, D) for k in range(12) if k not in narrow]
        return wide + [thin.reshape(-1, D)]

    blocks = [as_rows(layer) for layer in range(LAYERS)]
    flat = jnp.concatenate([block.astype(bf16) for part in blocks for block in part])
    filled = flat.shape[0]
    flat = jnp.pad(flat, ((0, -filled % 16), (0, 0)))
    if paired:
        keep, send = last_grads
        total = (keep.astype(f32) + swap_core(send).astype(f32)).astype(bf16)
        flat, _ = lax.optimization_barrier((flat, total))
        owned[0] = reduce_plane(total)
    flat = reduce_all(flat)
    found = [[None] * 12 for _ in range(LAYERS)]
    offset = 0
    for layer in range(LAYERS):
        pieces = []
        for block in blocks[layer]:
            pieces.append(flat[offset : offset + block.shape[0]])
            offset += block.shape[0]
        thin = pieces[-1].reshape(-1, filter_size)
        at = 0
        for k in range(12):
            like = small[layer][k]
            if k in narrow:
                count = like.size // filter_size
                found[layer][k] = thin[at : at + count].reshape(like.shape)
                at += count
            else:
                found[layer][k] = pieces[k if k < 2 else k - 4].reshape(like.shape)
    summed = [jnp.stack([found[layer][k] for layer in range(LAYERS)]) for k in range(12)]

    in_owned, out_owned, up_owned, down_owned = [], [], [], []
    for layer in range(LAYERS):
        ins, out, up, down = part_columns(
            owned[layer].astype(f32), owned_ff[layer].astype(f32), local_mix, local_ff
        )
        in_owned.append(jnp.stack(ins))
        out_owned.append(jnp.transpose(out))
        up_owned.append(up)
        down_owned.append(jnp.transpose(down))
    return (
        outputs[0],
        outputs[1],
        grad_low,
        jnp.stack(in_owned),
        jnp.stack(out_owned),
        jnp.stack(up_owned),
        jnp.stack(down_owned),
        *summed,
    )


def solution(mesh):
    groups, tensors = mesh.shape["dp"], mesh.shape["tensor"]
    cores = 2 if groups % 2 == 0 else 1
    fine = jax.sharding.Mesh(
        mesh.devices.reshape(groups // cores, cores, tensors), ("chip", "core", "tensor")
    )
    dp = ("chip", "core")
    rows = P(("chip", "core", "tensor"), None)
    weights = (
        P(None, None, dp, "tensor"),
        P(None, "tensor", dp),
        P(None, dp, "tensor"),
        P(None, "tensor", dp),
    )
    return jax.shard_map(
        shards,
        mesh=fine,
        in_specs=(rows, rows, P(), P(), *weights) + (P(),) * 12,
        out_specs=(rows, rows, rows, *weights) + (P(),) * 12,
        check_vma=False,
    )
```

```python
import functools
import math

import jax
import jax.numpy as jnp
import numpy as np
from jax import lax
from jax.experimental import pallas as pl
from jax.experimental.pallas import tpu as pltpu
from jax.sharding import PartitionSpec as P

D = 768
FF = 3072
EMB = 33
LAYERS = 2
LMAX = 1024
BLK = 128
TAPS = LMAX // BLK
LANES = 384
CONV_LANES = 768
STEP = 1
GROUP = 16
HIDDEN = 768
HALO = 16
STRIP = 64

highest = lax.Precision.HIGHEST
f32 = jnp.float32
bf16 = jnp.bfloat16
epsilon = 1e-05
shift_value = 0.05


def wave_tables():
    waves = (np.arange(BLK) + 0.5)[:, None] * (2.0 * math.pi / (2 * BLK))

    def spectrum(places):
        angle = waves * places[None, :]
        return np.concatenate([np.cos(angle), -np.sin(angle)], axis=0)

    causal = spectrum(np.arange(2 * BLK) - BLK)
    ahead = spectrum(np.arange(2 * BLK))
    single = spectrum(np.arange(BLK))
    back = spectrum(np.arange(BLK)).T / BLK
    return causal, ahead, single, back


def positions_table(length):
    bands = (EMB - 1) // 2
    ramp = jnp.linspace(0.0, 1.0, length, dtype=f32)[:, None]
    places = jnp.arange(length, dtype=f32)[:, None] * (2.0 * math.pi / length)
    levels = jnp.linspace(0.0001, bands - 1, bands, dtype=f32)[None, :]
    return jnp.concatenate([ramp, jnp.cos(levels * places), -jnp.sin(levels * places)], axis=1)


def decay_table(length):
    ramp = jnp.linspace(0.0, 1.0, length, dtype=f32)[:, None]
    fastest = math.log(0.01) / 0.3
    slowest = math.log(0.01) / 1.5
    speeds = slowest + (fastest - slowest) * jnp.arange(D, dtype=jnp.int32).astype(f32) / (D - 1)
    return jnp.exp(-ramp * jnp.abs(speeds)[None, :]) + shift_value


def filter_hidden(positions, first_w, inner_w, bias_w, rate_w):
    inner = jnp.sin(rate_w[0] * (jnp.dot(positions, first_w, precision=highest) + bias_w[0]))
    inner = jnp.sin(rate_w[1] * (jnp.dot(inner, inner_w[0], precision=highest) + bias_w[1]))
    return jnp.sin(rate_w[2] * (jnp.dot(inner, inner_w[1], precision=highest) + bias_w[2]))


def rows_mask(first, count, begin, end):
    rows = first + lax.broadcasted_iota(jnp.int32, (count, 1), 0)
    return (rows >= begin) & (rows < end)


def masked_spectrum(table, block, mask):
    kept = jnp.where(mask, block.astype(f32), 0.0).astype(bf16)
    return jnp.dot(table, kept, preferred_element_type=f32)


def groups():
    return [(slice(f, f + GROUP), slice(BLK + f, BLK + f + GROUP)) for f in range(0, BLK, GROUP)]


def no_sums():
    return tuple(jnp.zeros((GROUP, 128), f32) for _ in range(2 * BLK // GROUP))


def multiply_add(carry, left, a, right, b, part, conj):
    result = []
    for k, (up, down) in enumerate(groups()):
        left_re, left_im = left[a, up, part], left[a, down, part]
        right_re, right_im = right[b, up, part], right[b, down, part]
        if conj:
            re = left_re * right_re + left_im * right_im
            im = left_re * right_im - left_im * right_re
        else:
            re = left_re * right_re - left_im * right_im
            im = left_re * right_im + left_im * right_re
        result += [carry[2 * k] + re, carry[2 * k + 1] + im]
    return tuple(result)


def conv_forward_body(
    own_block, table, window, kernel, gate_out, bias, causal, back, carried, mixer, out, spectra, total
):
    blocks = spectra.shape[0] - STEP + 1
    width = out.shape[1]
    origin = table[2]

    def segment(n, _):
        begin = table[3 + n] - origin
        end = table[4 + n] - origin
        head = lax.div(begin, BLK)
        tail = jnp.minimum(lax.div(end - 1, BLK), blocks - 1)

        for k in range(STEP - 1):
            spectra[head + k] = jnp.zeros(spectra.shape[1:], f32)

        def transform(j, _):
            at = pl.multiple_of(j * BLK, BLK)
            mask = rows_mask(at - BLK, 2 * BLK, begin, end)
            spectra[j + STEP - 1] = masked_spectrum(
                causal[...], window[pl.ds(at, 2 * BLK), :], mask
            )
            return 0

        lax.fori_loop(head, tail + 1, transform, 0)

        def produce(j, _):
            reach = lax.div(jnp.minimum(j - head, TAPS - 1) + STEP, STEP)
            for lane in range(0, width, 128):
                part = slice(lane, lane + 128)

                def lag(c, carry):
                    for k in range(STEP):
                        b = c * STEP + k
                        at = j - b + STEP - 1
                        carry = multiply_add(carry, kernel, b, spectra, at, part, False)
                    return carry

                held = lax.fori_loop(0, reach, lag, no_sums())
                for k, pair in enumerate(groups()):
                    total[pair[0], part] = held[2 * k].astype(bf16)
                    total[pair[1], part] = held[2 * k + 1].astype(bf16)
            value = jnp.dot(back[...], total[...], preferred_element_type=f32)
            at = pl.multiple_of((j - own_block) * BLK, BLK)
            mask = rows_mask(j * BLK, BLK, begin, end)
            out[pl.ds(at, BLK), :] = jnp.where(mask, value, out[pl.ds(at, BLK), :])
            return 0

        lax.fori_loop(jnp.maximum(head, own_block), tail + 1, produce, 0)
        return 0

    lax.fori_loop(table[0], table[1] + 1, segment, 0)
    own = window.shape[0] - out.shape[0]

    def strip(at):
        for part in lanes(width):
            value = out[pl.ds(at, STRIP), part] + bias[0, :, part] * window[
                pl.ds(own + at, STRIP), part
            ].astype(f32)
            carried[pl.ds(at, STRIP), part] = value.astype(bf16)
            mixer[pl.ds(at, STRIP), part] = (
                value * gate_out[pl.ds(at, STRIP), part].astype(f32)
            ).astype(bf16)

    each_strip(out.shape[0], STRIP, strip)


def signal_backward_body(
    own_block, table, grads, kernel, values, gate_in, bias, ahead, back,
    gate_in_grad, values_grad, signal_grad, spectra, total,
):
    blocks = spectra.shape[0] - STEP + 1
    own_blocks = signal_grad.shape[0] // BLK
    width = signal_grad.shape[1]
    origin = table[2] + own_block * BLK

    def segment(n, _):
        begin = table[3 + n] - origin
        end = table[4 + n] - origin
        first = lax.div(jnp.maximum(begin, 0), BLK)
        tail = jnp.minimum(lax.div(end - 1, BLK), own_blocks - 1)
        last = jnp.minimum(lax.div(end - 1, BLK), blocks - 1)

        def transform(j, _):
            at = pl.multiple_of(j * BLK, BLK)
            mask = rows_mask(at, 2 * BLK, begin, end)
            spectra[j] = masked_spectrum(ahead[...], grads[pl.ds(at, 2 * BLK), :], mask)
            return 0

        lax.fori_loop(first, last + 1, transform, 0)
        for k in range(1, STEP):
            spectra[last + k] = jnp.zeros(spectra.shape[1:], f32)

        def produce(j, _):
            reach = lax.div(jnp.minimum(last - j, TAPS - 1) + STEP, STEP)
            for part in lanes(width):

                def lag(c, carry):
                    for k in range(STEP):
                        b = c * STEP + k
                        carry = multiply_add(carry, kernel, b, spectra, j + b, part, True)
                    return carry

                held = lax.fori_loop(0, reach, lag, no_sums())
                for k, pair in enumerate(groups()):
                    total[pair[0], part] = held[2 * k].astype(bf16)
                    total[pair[1], part] = held[2 * k + 1].astype(bf16)
            value = jnp.dot(back[...], total[...], preferred_element_type=f32)
            at = pl.multiple_of(j * BLK, BLK)
            mask = rows_mask(at, BLK, begin, end)
            signal_grad[pl.ds(at, BLK), :] = jnp.where(
                mask, value, signal_grad[pl.ds(at, BLK), :]
            )
            return 0

        lax.fori_loop(first, tail + 1, produce, 0)
        return 0

    lax.fori_loop(table[0], table[1] + 1, segment, 0)

    def strip(at):
        for part in lanes(width):
            where = (pl.ds(at, STRIP), part)
            value = signal_grad[where] + bias[0, :, part] * grads[where].astype(f32)
            gate_in_grad[where] = (value * values[where].astype(f32)).astype(bf16)
            values_grad[where] = (value * gate_in[where].astype(f32)).astype(bf16)

    each_strip(signal_grad.shape[0], STRIP, strip)


def kernel_backward_body(
    own_block, table, window, grads, causal, single, back, kernel_grad, spectra, own_spectra, sums
):
    blocks = spectra.shape[0] - STEP + 1
    width = kernel_grad.shape[1]
    origin = table[2]
    sums[...] = jnp.zeros_like(sums)

    def segment(n, _):
        begin = table[3 + n] - origin
        end = table[4 + n] - origin
        head = lax.div(begin, BLK)
        tail = jnp.minimum(lax.div(end - 1, BLK), blocks - 1)
        first = jnp.maximum(head, own_block)

        def transform(j, _):
            at = pl.multiple_of(j * BLK, BLK)
            mask = rows_mask(at - BLK, 2 * BLK, begin, end)
            spectra[j] = masked_spectrum(causal[...], window[pl.ds(at, 2 * BLK), :], mask)
            return 0

        lax.fori_loop(head, tail + 1, transform, 0)

        def transform_own(j, _):
            at = pl.multiple_of((j - own_block) * BLK, BLK)
            mask = rows_mask(j * BLK, BLK, begin, end)
            own_spectra[j - own_block] = masked_spectrum(
                single[...], grads[pl.ds(at, BLK), :], mask
            )
            return 0

        lax.fori_loop(first, tail + 1, transform_own, 0)
        for k in range(1, STEP):
            spectra[tail + k] = jnp.zeros(spectra.shape[1:], f32)
            own_spectra[tail - own_block + k] = jnp.zeros(own_spectra.shape[1:], f32)

        def accumulate(b, _):
            begin_at = jnp.maximum(first, head + b)
            for part in lanes(width):

                def at_blocks(c, carry):
                    for k in range(STEP):
                        j = begin_at + c * STEP + k
                        carry = multiply_add(
                            carry, spectra, j - b, own_spectra, j - own_block, part, True
                        )
                    return carry

                held = [sums[b, rows, part] for pair in groups() for rows in pair]
                count = lax.div(tail - begin_at + STEP, STEP)
                held = lax.fori_loop(0, count, at_blocks, tuple(held))
                for k, pair in enumerate(groups()):
                    sums[b, pair[0], part] = held[2 * k]
                    sums[b, pair[1], part] = held[2 * k + 1]
            return 0

        lax.fori_loop(0, jnp.minimum(tail - head, TAPS - 1) + 1, accumulate, 0)
        return 0

    lax.fori_loop(table[0], table[1] + 1, segment, 0)
    for b in range(TAPS):
        kernel_grad[b * BLK : (b + 1) * BLK, :] = jnp.dot(
            back[...], sums[b].astype(bf16), preferred_element_type=f32
        )


def norm_rows(values):
    centered = values - jnp.mean(values, -1, keepdims=True)
    rate = lax.rsqrt(jnp.mean(centered * centered, -1, keepdims=True) + epsilon)
    return centered * rate, rate


def norm_rows_back(grad, scaled, rate, gain):
    g = grad * gain
    return rate * (
        g - jnp.mean(g, -1, keepdims=True) - scaled * jnp.mean(g * scaled, -1, keepdims=True)
    )


def fold(values):
    return jnp.sum(values.reshape(values.shape[0] // 8, 8, values.shape[1]), axis=0)


def lanes(count):
    return [slice(q, q + 128) for q in range(0, count, 128)]


def dot(left, right):
    return jnp.dot(left, right, preferred_element_type=f32)


def dot_rows(left, right):
    return lax.dot_general(left, right, (((1,), (1,)), ((), ())), preferred_element_type=f32)


def each_strip(rows, step, body, copies=1):
    while rows % (step * copies):
        copies //= 2

    def run(c, _):
        for k in range(copies):
            body(pl.multiple_of((c * copies + k) * step, step))
        return 0

    lax.fori_loop(0, rows // (step * copies), run, 0)


def sum_strips(rows, step, body, zeros, copies=1):
    while rows % (step * copies):
        copies //= 2

    def run(c, totals):
        for k in range(copies):
            parts = body(pl.multiple_of((c * copies + k) * step, step))
            totals = tuple(total + part for total, part in zip(totals, parts))
        return totals

    return lax.fori_loop(0, rows // (step * copies), run, zeros)


def turn_into(target, chunk, at, order):
    turned = chunk.astype(bf16).T
    for first, size, place in order:
        target[pl.ds(place, size), at : at + chunk.shape[0]] = turned[first : first + size, :]


def in_forward_body(state, halo, norm, weight, bias, taps, age, *refs):
    normed, projected, gate_out, gate_in, values, signal, low, wide = refs
    rows = state.shape[0]

    @pl.when(pl.program_id(0) == 0)
    def _():
        gain, shift = norm[0:1, :], norm[1:2, :]
        low[:HALO, :] = (norm_rows(halo[...].astype(f32))[0] * gain + shift).astype(bf16)

        def strip(at):
            part = norm_rows(state[pl.ds(at, 32), :].astype(f32))[0] * gain + shift
            low[pl.ds(at + HALO, 32), :] = part.astype(bf16)
            normed[pl.ds(at, 32), :] = part.astype(bf16)

        each_strip(rows, 32, strip, 4)

    chunk = max(c for c in range(16, 273, 16) if (rows + HALO) % c == 0)

    def product(at):
        wide[pl.ds(at, chunk), :] = (
            dot(low[pl.ds(at, chunk), :], weight[0, :, : 3 * LANES]) + bias[0]
        )

    each_strip(rows + HALO, chunk, product)
    for part in range(3):
        projected[part, :HALO, :] = wide[:HALO, part * LANES : (part + 1) * LANES].astype(bf16)

    def strip(at):
        old = age[pl.ds(at, STRIP), :]
        for lane in lanes(LANES):
            mixed = []
            for part in range(3):
                cols = slice(part * LANES + lane.start, part * LANES + lane.stop)
                block = wide[pl.ds(at + HALO - 8, STRIP + 8), cols]
                now, once, twice = block[8:], block[7:-1], block[6:-2]
                projected[part, pl.ds(at + HALO, STRIP), lane] = now.astype(bf16)
                mixed.append(
                    taps[0, 0:1, cols] * now
                    + jnp.where(old >= 1, taps[0, 1:2, cols] * once, 0.0)
                    + jnp.where(old >= 2, taps[0, 2:3, cols] * twice, 0.0)
                )
            for ref, value in zip((gate_out, gate_in, values), mixed):
                ref[pl.ds(at, STRIP), lane] = value.astype(bf16)
            signal[pl.ds(at, STRIP), lane] = (mixed[1] * mixed[2]).astype(bf16)

    each_strip(rows, STRIP, strip)


def ff_forward_body(
    out_blocks, mixer, state, norm, shifts, weight, bias, *refs
):
    outs = refs[:out_blocks]
    middle, second, activated, slope, result, result_low, hidden = refs[out_blocks:]
    rows = state.shape[0]
    chunk = min(512, rows)

    @pl.when(pl.program_id(0) == 0)
    def _():
        def product(at):
            total = state[pl.ds(at, chunk), :].astype(f32) + shifts[0:1, :]
            for n, out in enumerate(outs):
                total += dot_rows(
                    mixer[pl.ds(at, chunk), n * LANES : (n + 1) * LANES], out[0]
                )
            middle[pl.ds(at, chunk), :] = total

        each_strip(rows, chunk, product)

        def strip(at):
            part = middle[pl.ds(at, 64), :]
            result[pl.ds(at, 64), :] = part + shifts[1:2, :]
            second[pl.ds(at, 64), :] = (
                norm_rows(part)[0] * norm[0:1, :] + norm[1:2, :]
            ).astype(bf16)

        each_strip(rows, 64, strip, 2)

    def product(at):
        hidden[...] = dot(second[pl.ds(at, chunk), :], weight[0, :, :HIDDEN]) + bias[0]

        def strip(inner):
            for lane in lanes(HIDDEN):
                before = hidden[pl.ds(inner, STRIP), lane]
                cumulative = 0.5 + 0.5 * lax.erf(before * math.sqrt(0.5))
                bell = jnp.exp(-0.5 * before * before) * (1.0 / math.sqrt(2 * math.pi))
                activated[pl.ds(at + inner, STRIP), lane] = (before * cumulative).astype(bf16)
                slope[pl.ds(at + inner, STRIP), lane] = (cumulative + before * bell).astype(bf16)

        each_strip(chunk, STRIP, strip)
        result[pl.ds(at, chunk), :] += dot_rows(
            activated[pl.ds(at, chunk), :], weight[0, :, HIDDEN:]
        )

    each_strip(rows, chunk, product)

    @pl.when(pl.program_id(0) == pl.num_programs(0) - 1)
    def _():
        def strip(at):
            result_low[pl.ds(at, STRIP), :] = result[pl.ds(at, STRIP), :].astype(bf16)

        each_strip(rows, STRIP, strip, 2)


def row_order(split, mine, size):
    if not split:
        return [(0, D, 0)]
    runs = []
    for run in range(D // size):
        slot = (run % 2) ^ mine
        place = pl.multiple_of(slot * (D // 2) + run // 2 * size, 16)
        runs.append((run * size, size, place))
    return runs


def ff_backward_body(
    split, place, grad, second, middle, norm, activated, slope, weight, *refs
):
    middle_grad, middle_low, weight_grad, bias_grad, sums = refs[-10:-5]
    grad_low, grad_turned, second_turned, hidden, hidden_low = refs[-5:]
    rows = grad.shape[0]
    chunk = min(512, rows)
    order = row_order(split, place[0], 0 if not split else split)

    @pl.when(pl.program_id(0) == 0)
    def _():
        for at in range(0, rows, chunk):
            turn_into(grad_turned, grad[at : at + chunk, :], at, order)
            turn_into(second_turned, second[at : at + chunk, :], at, order)

        def strip(at):
            grad_low[pl.ds(at, 32), :] = grad[pl.ds(at, 32), :].astype(bf16)
            middle_grad[pl.ds(at, 32), :] = jnp.zeros((32, D), f32)

        each_strip(rows, 32, strip, 4)
        sums[...] = jnp.zeros_like(sums)
    bias_grad[...] = jnp.zeros_like(bias_grad)

    def product(at):
        hidden[...] = dot(grad_low[pl.ds(at, chunk), :], weight[0, :, HIDDEN:])

        def strip(inner):
            totals = []
            for lane in lanes(HIDDEN):
                part = hidden[pl.ds(inner, STRIP), lane] * slope[
                    pl.ds(at + inner, STRIP), lane
                ].astype(f32)
                hidden_low[pl.ds(at + inner, STRIP), lane] = part.astype(bf16)
                totals.append(fold(part))
            return totals

        zero = jnp.zeros((8, 128), f32)
        totals = sum_strips(chunk, STRIP, strip, (zero,) * (HIDDEN // 128))
        for lane, total in zip(lanes(HIDDEN), totals):
            bias_grad[0, :, lane] += jnp.sum(total, axis=0, keepdims=True)
        middle_grad[pl.ds(at, chunk), :] += dot_rows(
            hidden_low[pl.ds(at, chunk), :], weight[0, :, :HIDDEN]
        )

    each_strip(rows, chunk, product)

    def product_weight(at):
        weight_grad[0, pl.ds(at, 256), :HIDDEN] = dot(
            second_turned[pl.ds(at, 256), :], hidden_low[...]
        ).astype(bf16)
        weight_grad[0, pl.ds(at, 256), HIDDEN:] = dot(
            grad_turned[pl.ds(at, 256), :], activated[...]
        ).astype(bf16)

    each_strip(D, 256, product_weight)

    @pl.when(pl.program_id(0) == pl.num_programs(0) - 1)
    def _():
        def strip(at):
            above = grad[pl.ds(at, 128), :].astype(f32)
            inner = middle_grad[pl.ds(at, 128), :]
            scaled, rate = norm_rows(middle[pl.ds(at, 128), :])
            total = above + norm_rows_back(inner, scaled, rate, norm[0:1, :])
            middle_grad[pl.ds(at, 128), :] = total
            middle_low[pl.ds(at, 128), :] = total.astype(bf16)
            for k, part in enumerate((above, inner * scaled, inner, total)):
                sums[k] += fold(part)

        each_strip(rows, 128, strip)


def gates_backward_body(
    middle_low, weight, gate_out, carried, signal, carried_grad, gate_grad, bias_grad, product_ref
):
    rows = middle_low.shape[0]
    chunk = min(512, rows)
    bias_grad[...] = jnp.zeros_like(bias_grad)

    def product(at):
        product_ref[...] = dot(middle_low[pl.ds(at, chunk), :], weight[0])

        def strip(inner):
            totals = []
            for lane in lanes(LANES):
                part = product_ref[pl.ds(inner, STRIP), lane]
                where = (pl.ds(at + inner, STRIP), lane)
                grown = part * gate_out[where].astype(f32)
                carried_grad[where] = grown.astype(bf16)
                gate_grad[where] = (part * carried[where].astype(f32)).astype(bf16)
                totals.append(fold(grown * signal[where].astype(f32)))
            return totals

        zero = jnp.zeros((8, 128), f32)
        totals = sum_strips(chunk, STRIP, strip, (zero,) * (LANES // 128))
        for lane, total in zip(lanes(LANES), totals):
            bias_grad[0, :, lane] += jnp.sum(total, axis=0, keepdims=True)

    each_strip(rows, chunk, product)


def in_backward_body(
    split, place, first_grad, second_grad, third_grad, halo, age, projected, taps, normed,
    middle_low, mixer, weight, state, middle_grad, norm,
    grad, grad_out, bias_grad, taps_grad, sums, *refs
):
    normed_turned, middle_turned, spread, low = refs[-4:]
    weight_grads = refs[:-4]
    rows = normed.shape[0]
    chunk = min(512, rows)
    order = row_order(split, place[0], 0 if not split else split)

    @pl.when(pl.program_id(0) == 0)
    def _():
        for at in range(0, rows, chunk):
            turn_into(normed_turned, normed[at : at + chunk, :], at, order)
            turn_into(middle_turned, middle_low[at : at + chunk, :], at, order)
        sums[...] = jnp.zeros_like(sums)

        def strip(at):
            grad[pl.ds(at, 32), :] = jnp.zeros((32, D), f32)

        each_strip(rows, 32, strip, 4)

    for part, ref in enumerate((first_grad, second_grad, third_grad)):
        cols = slice(part * LANES, (part + 1) * LANES)

        def strip(at):
            spread[pl.ds(at, STRIP), cols] = ref[pl.ds(at, STRIP), :]

        each_strip(rows, STRIP, strip)
        spread[rows:, cols] = halo[part]

    for part in range(3):

        def strip(at):
            old = age[pl.ds(at, STRIP + HALO), :]
            mine, after_one, after_two = old[:STRIP], old[1 : STRIP + 1], old[2 : STRIP + 2]
            totals = []
            for lane in lanes(LANES):
                cols = slice(part * LANES + lane.start, part * LANES + lane.stop)
                block = spread[pl.ds(at, STRIP + HALO), cols].astype(f32)
                source = projected[part, pl.ds(at, STRIP + HALO), lane].astype(f32)
                now = block[:STRIP]
                total = (
                    taps[0, 0:1, cols] * now
                    + jnp.where(after_one >= 1, taps[0, 1:2, cols] * block[1 : STRIP + 1], 0.0)
                    + jnp.where(after_two >= 2, taps[0, 2:3, cols] * block[2 : STRIP + 2], 0.0)
                )
                low[pl.ds(at, STRIP), cols] = total.astype(bf16)
                totals += [
                    fold(now * source[HALO:]),
                    fold(jnp.where(mine >= 1, now * source[HALO - 1 : -1], 0.0)),
                    fold(jnp.where(mine >= 2, now * source[HALO - 2 : -2], 0.0)),
                    fold(total),
                ]
            return totals

        zero = jnp.zeros((8, 128), f32)
        totals = sum_strips(rows, STRIP, strip, (zero,) * (4 * LANES // 128))
        for q, lane in enumerate(lanes(LANES)):
            cols = slice(part * LANES + lane.start, part * LANES + lane.stop)
            for tap in range(3):
                taps_grad[0, tap : tap + 1, cols] = jnp.sum(
                    totals[4 * q + tap], axis=0, keepdims=True
                )
            bias_grad[0, :, cols] = jnp.sum(totals[4 * q + 3], axis=0, keepdims=True)

    def product(at):
        grad[pl.ds(at, chunk), :] += dot_rows(
            low[pl.ds(at, chunk), :], weight[0, :, : 3 * LANES]
        )

    each_strip(rows, chunk, product)

    size = D // len(weight_grads)
    for k, weight_grad in enumerate(weight_grads):

        def product_weight(at):
            source = pl.ds(k * size + at, 192)
            weight_grad[0, pl.ds(at, 192), : 3 * LANES] = dot(
                normed_turned[source, :], low[...]
            ).astype(bf16)
            weight_grad[0, pl.ds(at, 192), 3 * LANES :] = dot(
                middle_turned[source, :], mixer[...]
            ).astype(bf16)

        each_strip(size, 192, product_weight)

    @pl.when(pl.program_id(0) == pl.num_programs(0) - 1)
    def _():
        def strip(at):
            inner = grad[pl.ds(at, 128), :]
            scaled, rate = norm_rows(state[pl.ds(at, 128), :].astype(f32))
            total = middle_grad[pl.ds(at, 128), :] + norm_rows_back(
                inner, scaled, rate, norm[0:1, :]
            )
            grad[pl.ds(at, 128), :] = total
            grad_out[pl.ds(at, 128), :] = total.astype(bf16)
            for k, part in enumerate((inner * scaled, inner)):
                sums[k] += fold(part)

        each_strip(rows, 128, strip)


def whole(shape):
    return pl.BlockSpec(
        shape, lambda i, *_: (0,) * len(shape), pipeline_mode=pl.Buffered(1)
    )


def by_lane(shape):
    return pl.BlockSpec(shape, lambda i, *_: (0,) * (len(shape) - 1) + (i,))


def by_first(shape):
    return pl.BlockSpec(shape, lambda i, *_: (i,) + (0,) * (len(shape) - 1))


def weight_block(wide, per, first=0, stride=1, depth=D):
    return pl.BlockSpec(
        (1, depth, wide), lambda i, *_: (i // per, 0, first + stride * (i % per))
    )


def run(body, name, grid, scalars, ins, outs, scratch, flops, moved, limit=48, aliases={}):
    arrays, in_specs = zip(*ins)
    shapes, out_specs = zip(*outs)
    return pl.pallas_call(
        body,
        out_shape=shapes,
        grid_spec=pltpu.PrefetchScalarGridSpec(
            num_scalar_prefetch=len(scalars),
            grid=(grid,),
            in_specs=in_specs,
            out_specs=out_specs,
            scratch_shapes=scratch,
        ),
        compiler_params=pltpu.CompilerParams(vmem_limit_bytes=limit << 20),
        input_output_aliases=aliases,
        cost_estimate=pl.CostEstimate(flops=flops, bytes_accessed=moved, transcendentals=0),
        name=name,
    )(*scalars, *arrays)


def shape_of(dims, kind):
    return jax.ShapeDtypeStruct(dims, kind)


def in_forward(state, halo, norm, weights, first, per, bias, taps, age):
    rows = state.shape[0]
    blocks = D // LANES
    low = (shape_of((rows, D), bf16), by_lane((rows, LANES)))
    return run(
        in_forward_body, "in_forward", blocks, (),
        [
            (state, whole((rows, D))), (halo, whole((HALO, D))), (norm, whole((2, D))),
            (weights, weight_block(4 * LANES, per, first)),
            (bias, by_first((1, 1, 3 * LANES))), (taps, by_first((1, 3, 3 * LANES))),
            (age, whole(age.shape)),
        ],
        [
            (shape_of((rows, D), bf16), whole((rows, D))),
            (shape_of((3, rows + HALO, D), bf16), by_lane((3, rows + HALO, LANES))),
            low, low, low, low,
        ],
        [pltpu.VMEM((rows + HALO, D), bf16), pltpu.VMEM((rows + HALO, 3 * LANES), f32)],
        2 * rows * D * 3 * D, 20_000_000, 30,
    )


def ff_forward(mixer, state, norm, shifts, weights, per, hidden_per, bias, mix, first):
    rows = state.shape[0]
    hidden_blocks = FF // HIDDEN
    row = (rows, D)
    tall = (shape_of((rows, FF), bf16), by_lane((rows, HIDDEN)))
    out_specs = [
        pl.BlockSpec(
            (1, D, LANES), lambda i, *_, n=n: (n // per, 0, 4 * (first + n % per) + 3)
        )
        for n in range(D // LANES)
    ]
    return run(
        functools.partial(ff_forward_body, D // LANES), "ff_forward", hidden_blocks, (),
        [
            (mixer, whole(row)), (state, whole(row)), (norm, whole((2, D))),
            (shifts, whole((2, D))),
            (weights, weight_block(2 * HIDDEN, hidden_per)),
            (bias, by_first((1, 1, HIDDEN))),
        ]
        + [(mix, spec) for spec in out_specs],
        [
            (shape_of(row, f32), whole(row)), (shape_of(row, bf16), whole(row)), tall, tall,
            (shape_of(row, f32), whole(row)), (shape_of(row, bf16), whole(row)),
        ],
        [pltpu.VMEM((min(512, rows), HIDDEN), f32)],
        2 * rows * D * (2 * FF + D), 40_000_000, 32,
    )


def ff_backward(
    split, place, grad, second, middle, norm, activated, slope, weights, hidden_per, shared
):
    rows = grad.shape[0]
    row = (rows, D)
    hidden_blocks = FF // HIDDEN
    halves = weights.shape[0]
    grads = shape_of((halves, D, 2 * FF // halves) if shared is None else shared.shape, bf16)
    base = [] if shared is None else [(shared, pl.BlockSpec(memory_space=pl.ANY))]
    return run(
        functools.partial(ff_backward_body, split), "ff_backward", hidden_blocks, (place,),
        [
            (grad, whole(row)), (second, whole(row)), (middle, whole(row)), (norm, whole((2, D))),
            (activated, by_lane((rows, HIDDEN))), (slope, by_lane((rows, HIDDEN))),
            (weights, weight_block(2 * HIDDEN, hidden_per)),
        ]
        + base,
        [
            (shape_of(row, f32), whole(row)), (shape_of(row, bf16), whole(row)),
            (grads, weight_block(2 * HIDDEN, hidden_per)),
            (shape_of((hidden_blocks, 1, HIDDEN), f32), by_first((1, 1, HIDDEN))),
            (shape_of((4, 8, D), f32), whole((4, 8, D))),
        ],
        [
            pltpu.VMEM(row, bf16), pltpu.VMEM((D, rows), bf16), pltpu.VMEM((D, rows), bf16),
            pltpu.VMEM((min(512, rows), HIDDEN), f32), pltpu.VMEM((rows, HIDDEN), bf16),
        ],
        8 * rows * D * FF, 50_000_000, 40, {8: 2} if base else {},
    )


def gates_backward(middle_low, weights, first, per, gate_out, carried, signal):
    rows = middle_low.shape[0]
    block = (rows, LANES)
    low = (shape_of((rows, D), bf16), by_lane(block))
    return run(
        gates_backward_body, "gates_backward", D // LANES, (),
        [
            (middle_low, whole((rows, D))), (weights, weight_block(LANES, per, 4 * first + 3, 4)),
            (gate_out, by_lane(block)), (carried, by_lane(block)), (signal, by_lane(block)),
        ],
        [
            low, low,
            (shape_of((D // LANES, 1, LANES), f32), by_first((1, 1, LANES))),
        ],
        [pltpu.VMEM((min(512, rows), LANES), f32)],
        2 * rows * D * D, 10_000_000, 20,
    )


def in_backward(
    split, place, mixed_grads, halo, age, projected, taps, normed, middle_low, mixer, weights,
    first, per, state, middle_grad, norm, columns, grad_first,
):
    rows = normed.shape[0]
    row, block = (rows, D), (rows, LANES)
    blocks = D // LANES
    count = 2 if split else 1
    grads = (
        shape_of((weights.shape[0], D // count, columns), bf16),
        weight_block(4 * LANES, per, grad_first, depth=D // count),
    )
    return run(
        functools.partial(in_backward_body, split), "in_backward", blocks, (place,),
        [(part, by_lane(block)) for part in mixed_grads]
        + [
            (halo, by_lane((3, HALO, LANES))), (age, whole(age.shape)),
            (projected, by_lane((3, rows + HALO, LANES))), (taps, by_first((1, 3, 3 * LANES))),
            (normed, whole(row)), (middle_low, whole(row)), (mixer, by_lane(block)),
            (weights, weight_block(4 * LANES, per, first)), (state, whole(row)),
            (middle_grad, whole(row)), (norm, whole((2, D))),
        ],
        [
            (shape_of(row, f32), whole(row)), (shape_of(row, bf16), whole(row)),
            (shape_of((blocks, 1, 3 * LANES), f32), by_first((1, 1, 3 * LANES))),
            (shape_of((blocks, 3, 3 * LANES), f32), by_first((1, 3, 3 * LANES))),
            (shape_of((2, 8, D), f32), whole((2, 8, D))),
        ]
        + [grads] * count,
        [
            pltpu.VMEM((D, rows), bf16), pltpu.VMEM((D, rows), bf16),
            pltpu.VMEM((rows + HALO, 3 * LANES), bf16), pltpu.VMEM((rows, 3 * LANES), bf16),
        ],
        2 * rows * D * 7 * D, 40_000_000, 46,
    )


def conv_forward(table, window, kernel, gate_out, bias, rows, tables):
    causal, _, _, back = tables
    wide = window.shape[0]
    blocks = wide // BLK - 1
    own_block = (wide - BLK - rows) // BLK
    low = (shape_of((rows, D), bf16), by_lane((rows, CONV_LANES)))
    return run(
        functools.partial(conv_forward_body, own_block), "conv_forward", D // CONV_LANES, (table,),
        [
            (window, by_lane((wide, CONV_LANES))), (kernel, by_lane((TAPS, 2 * BLK, CONV_LANES))),
            (gate_out, by_lane((rows, CONV_LANES))), (bias, by_first((1, 1, CONV_LANES))),
            (causal, whole((2 * BLK, 2 * BLK))), (back, whole((BLK, 2 * BLK))),
        ],
        [low, low],
        [
            pltpu.VMEM((rows, CONV_LANES), f32),
            pltpu.VMEM((blocks + STEP - 1, 2 * BLK, CONV_LANES), f32),
            pltpu.VMEM((2 * BLK, CONV_LANES), bf16),
        ],
        20_000_000_000, 20_000_000, 28,
    )


def signal_backward(table, grads, kernel, values, gate_in, bias, rows, hops, tables):
    _, ahead, _, back = tables
    wide = grads.shape[0]
    low = (shape_of((rows, D), bf16), by_lane((rows, CONV_LANES)))
    return run(
        functools.partial(signal_backward_body, hops * rows // BLK), "signal_backward",
        D // CONV_LANES, (table,),
        [
            (grads, by_lane((wide, CONV_LANES))),
            (kernel, by_lane((TAPS, 2 * BLK, CONV_LANES))), (values, by_lane((rows, CONV_LANES))),
            (gate_in, by_lane((rows, CONV_LANES))), (bias, by_first((1, 1, CONV_LANES))),
            (ahead, whole((2 * BLK, 2 * BLK))), (back, whole((BLK, 2 * BLK))),
        ],
        [low, low],
        [
            pltpu.VMEM((rows, CONV_LANES), f32),
            pltpu.VMEM((wide // BLK + STEP - 2, 2 * BLK, CONV_LANES), f32),
            pltpu.VMEM((2 * BLK, CONV_LANES), bf16),
        ],
        20_000_000_000, 20_000_000, 32,
    )


def kernel_backward(table, window, grads, rows, tables):
    causal, _, single, back = tables
    wide = window.shape[0]
    blocks = wide // BLK - 1
    own_block = (wide - BLK - rows) // BLK
    return run(
        functools.partial(kernel_backward_body, own_block), "kernel_backward",
        D // CONV_LANES, (table,),
        [
            (window, by_lane((wide, CONV_LANES))), (grads, by_lane((rows, CONV_LANES))),
            (causal, whole((2 * BLK, 2 * BLK))), (single, whole((2 * BLK, BLK))),
            (back, whole((BLK, 2 * BLK))),
        ],
        [(shape_of((LMAX, D), f32), by_lane((LMAX, CONV_LANES)))],
        [
            pltpu.VMEM((blocks + STEP - 1, 2 * BLK, CONV_LANES), f32),
            pltpu.VMEM((rows // BLK + STEP - 1, 2 * BLK, CONV_LANES), f32),
            pltpu.VMEM((TAPS, 2 * BLK, CONV_LANES), f32),
        ],
        20_000_000_000, 20_000_000, 32,
    )[0]


def shards(
    tokens,
    out_grad,
    seq_lengths,
    deal_order,
    input_weight,
    output_weight,
    up_projection_weight,
    down_projection_weight,
    input_bias,
    short_taps,
    filter_first,
    filter_inner,
    filter_biases,
    filter_rates,
    filter_out,
    conv_bias,
    norm_gains,
    norm_biases,
    output_biases,
    up_projection_bias,
):
    tensor_count = lax.axis_size("tensor")
    chips = lax.axis_size("chip")
    cores = lax.axis_size("core")
    devices = tensor_count * chips * cores
    core = lax.axis_index("core")
    rank = (lax.axis_index("chip") * cores + core) * tensor_count + lax.axis_index("tensor")
    rows = tokens.shape[0]
    width = input_weight.shape[3]
    hidden = up_projection_weight.shape[2]
    depth = input_weight.shape[2]
    count = seq_lengths.shape[0]
    everyone = ("chip", "core", "tensor")
    owners = ("tensor", "chip", "core")
    hops = -(-(LMAX - 1) // rows)
    direct = width % LANES == 0 and hidden % HIDDEN == 0
    per, hidden_per = D // LANES, FF // HIDDEN
    paired = (
        direct and depth % 16 == 0 and cores == 2 and tensor_count == 2
        and chips > 1 and chips & (chips - 1) == 0
    )
    split = depth if paired else 0
    chip, side = lax.axis_index("chip"), lax.axis_index("tensor")
    plane, row, planes = chip // 2, chip % 2, chips // 2

    def swap(values, mask):
        pairs = [(i, i ^ mask) for i in range(chips * tensor_count)]
        return lax.ppermute(values, ("chip", "tensor"), pairs)

    def swap_core(values):
        return lax.ppermute(values, "core", [(0, 1), (1, 0)])

    def pick(values, index, axis=0):
        return lax.dynamic_index_in_dim(values, index, axis, False)

    def gather_pairs(values, beside):
        n = values.shape[-1]
        parts = jnp.stack([values] + [swap(values, k << 2) for k in range(1, planes)])
        values = jnp.stack([pick(parts, k ^ plane) for k in range(planes)])
        parts = jnp.stack([values] + [swap(values, k) for k in range(1, 4)])
        mine = row * 2 + side
        values = jnp.stack(
            [
                jnp.stack([pick(parts, (2 * r + s) ^ mine) for r in range(2)], axis=1)
                for s in range(2)
            ]
        )
        values, beside = lax.optimization_barrier((values, beside))
        other = swap_core(values)
        values = jnp.stack(
            [jnp.where(core == 0, values, other), jnp.where(core == 0, other, values)], axis=3
        )
        return values.reshape(2, D, n), beside

    def total_of(parts, mine):
        held = jnp.stack(parts)
        total = pick(held, mine).astype(f32)
        for k in range(1, len(parts)):
            total += pick(held, k ^ mine).astype(f32)
        return total

    def both_sides(values):
        other = swap(values, 1)
        first, second = jnp.where(side == 0, values, other), jnp.where(side == 0, other, values)
        return jnp.concatenate([first, second], axis=1)

    def gather_rows(values):
        return lax.all_gather(values, ("chip", "core"), axis=0, tiled=True)[None]

    def reduce_rows(values, sizes):
        values = lax.psum_scatter(
            values.reshape(D, -1), ("chip", "core"), scatter_dimension=0, tiled=True
        )
        kept, sent, at = [], [], 0
        for size in sizes:
            half = size // 2
            for held, which in ((kept, side), (sent, 1 - side)):
                held.append(lax.dynamic_slice_in_dim(values, at + which * half, half, axis=1))
            at += size
        other = swap(jnp.concatenate(sent, axis=1), 1).astype(f32)
        result, at = [], 0
        for part in kept:
            result.append(part.astype(f32) + other[:, at : at + part.shape[1]])
            at += part.shape[1]
        return result

    def reduce_plane(total, beside):
        total = total.reshape(2, planes, 2, depth, -1)

        def block(s, r):
            return pick(pick(total, s), r, 1)

        parts = [swap(block(side ^ (k % 2), row ^ (k // 2)), k) for k in range(1, 4)]
        total = block(side, row).astype(f32)
        for part in parts:
            total += part.astype(f32)
        total, beside = lax.optimization_barrier((total, beside))
        low = total.astype(bf16)
        parts = [swap(pick(low, plane ^ k), k << 2) for k in range(1, planes)]
        total = pick(total, plane)
        for part in parts:
            total += part.astype(f32)
        return total, beside

    def reduce_all(extra):
        def rounded(values):
            return lax.optimization_barrier(values.astype(bf16))

        if paired:
            low = rounded(extra)
            low = rounded(low.astype(f32) + swap_core(low).astype(f32))
            parts = [low] + [swap(low, k) for k in range(1, 4)]
            extra = total_of(parts, row * 2 + side)
            for k in range((planes - 1).bit_length()):
                low = rounded(extra)
                extra = low.astype(f32) + swap(low, 4 << k).astype(f32)
            return extra
        step = 1
        while step < devices:
            low = rounded(extra)
            other = lax.ppermute(low, everyone, [(i, i ^ step) for i in range(devices)])
            extra = low.astype(f32) + other.astype(f32)
            step *= 2
        return extra

    def from_before(values, hop=1):
        return lax.ppermute(values, everyone, [(i, i + hop) for i in range(devices - hop)])

    def from_after(values, hop=1):
        return lax.ppermute(values, everyone, [(i + hop, i) for i in range(devices - hop)])

    def join_columns(ins, out, up, down, mix_blocks, ff_blocks):
        lead = out.shape[:-1]
        mix = jnp.stack(
            [part.reshape(*lead, mix_blocks, -1) for part in (*ins, out)], axis=-2
        ).reshape(*lead, -1)
        ff = jnp.stack(
            [part.reshape(*lead, ff_blocks, -1) for part in (up, down)], axis=-2
        ).reshape(*lead, -1)
        return mix, ff

    def part_columns(mix, ff, mix_blocks, ff_blocks):
        def strided(values, blocks, kinds, k):
            size = values.shape[-1] // (blocks * kinds)
            starts = [(kinds * b + k) * size for b in range(blocks)]
            return jnp.concatenate([values[..., at : at + size] for at in starts], axis=-1)

        mixes = [strided(mix, mix_blocks, 4, k) for k in range(4)]
        return mixes[:3], mixes[3], *[strided(ff, ff_blocks, 2, k) for k in range(2)]

    local_mix = width // LANES if paired else 1
    local_ff = hidden // HIDDEN if paired else 1
    local = []
    for layer in range(LAYERS):
        local.append(
            join_columns(
                [input_weight[layer, k].astype(bf16) for k in range(3)],
                jnp.transpose(output_weight[layer].astype(bf16)),
                up_projection_weight[layer].astype(bf16),
                jnp.transpose(down_projection_weight[layer].astype(bf16)),
                local_mix,
                local_ff,
            )
        )

    def gather(part):
        return lax.all_gather(part, owners, axis=0, tiled=True).reshape(tensor_count, D, -1)

    tables = tuple(jnp.asarray(t, f32).astype(bf16) for t in wave_tables())
    positions = positions_table(LMAX)
    modulation = decay_table(LMAX)
    blank = jnp.zeros((BLK, D), bf16)

    filters = []
    for layer in range(LAYERS):
        inner, filter_back = jax.vjp(
            lambda a, b, c, d: filter_hidden(positions, a, b, c, d),
            filter_first[layer],
            filter_inner[layer],
            filter_biases[layer],
            filter_rates[layer],
        )
        kernel = jnp.dot(inner, filter_out[layer], precision=highest) * modulation
        kernel_spectra = jnp.einsum(
            "kr,brc->bkc",
            tables[2],
            kernel.reshape(TAPS, BLK, D).astype(bf16),
            preferred_element_type=f32,
        )
        filters.append((inner, filter_back, kernel_spectra))

    gathered = []
    if paired:
        shared = gather_rows(
            jnp.concatenate([both_sides(local[0][1]), both_sides(local[1][0])], axis=1)
        )
        last = gather_rows(both_sides(local[1][1]))
        inner, filter_back, kernel_spectra = filters[0]
        mix, kernel_spectra = gather_pairs(local[0][0], kernel_spectra)
        filters[0] = (inner, filter_back, kernel_spectra)
        gathered.append((mix, width // LANES, shared))
        gathered.append((shared[:, :, 2 * FF :], per, last))
    else:
        for mix, ff in local:
            mix, ff = gather(mix), gather(ff)
            ins, out, up, down = part_columns(mix, ff, local_mix, local_ff)

            def full(piece):
                return jnp.transpose(piece, (1, 0, 2)).reshape(1, D, -1)

            mix, ff = join_columns(
                [full(k) for k in ins], full(out), full(up), full(down), per, hidden_per
            )
            gathered.append((mix, per, ff))

    numbers = jnp.arange(count, dtype=jnp.int32)
    match = deal_order[:, None] == numbers[None, :]
    lengths = jnp.sum(jnp.where(match, seq_lengths[:, None], 0), axis=0)
    ends = jnp.sum(jnp.where(numbers[:, None] <= numbers[None, :], lengths[:, None], 0), axis=0)
    starts = ends - lengths
    base = rank * rows
    first_segment = jnp.sum((starts <= base).astype(jnp.int32)) - 1
    last_segment = jnp.sum((starts < base + rows).astype(jnp.int32)) - 1
    table = jnp.concatenate(
        [
            jnp.stack([first_segment, last_segment, base - hops * rows]),
            starts,
            ends[count - 1 :],
        ]
    ).astype(jnp.int32)

    def ages(places):
        begun = jnp.max(jnp.where(starts[None, :] <= places[:, None], starts[None, :], 0), axis=1)
        return jnp.broadcast_to((places - begun)[:, None], (places.shape[0], 128))

    age = ages(base + jnp.arange(rows + HALO, dtype=jnp.int32))
    place = core.astype(jnp.int32).reshape(1)

    def by_block(values):
        lead = values.shape[:-2]
        split_up = values.reshape(*lead, 3, D // LANES, LANES)
        return jnp.moveaxis(split_up, -2, 0).reshape(D // LANES, *lead, 3 * LANES)

    def from_block(values):
        lead = values.shape[1:-1]
        split_up = values.reshape(D // LANES, *lead, 3, LANES)
        return jnp.moveaxis(split_up, 0, -2).reshape(*lead, 3, D)

    state = tokens
    kept = []
    outputs = []
    for layer in range(LAYERS):
        mix_weights, mix_per, ff_weights = gathered[layer]
        first_norm = jnp.stack([norm_gains[layer, 0], norm_biases[layer, 0]])
        second_norm = jnp.stack([norm_gains[layer, 1], norm_biases[layer, 1]])
        taps = by_block(short_taps[layer])
        lane_bias = conv_bias[layer].reshape(D // CONV_LANES, 1, CONV_LANES)
        shared_in = (
            first_norm, mix_weights, 0, mix_per, by_block(input_bias[layer][None]), taps
        )
        near = from_before(state[rows - HALO :])
        normed, projected, gate_out, gate_in, values, signal = in_forward(
            state, near, *shared_in, age
        )
        before = [from_before(signal, hop) for hop in range(hops, 0, -1)]
        window = jnp.concatenate([blank, *before, signal])
        carried, mixer = conv_forward(
            table, window, filters[layer][2], gate_out, lane_bias, rows, tables
        )
        middle, second, activated, slope, result, result_low = ff_forward(
            mixer, state, second_norm, output_biases[layer], ff_weights, mix_per, hidden_per,
            up_projection_bias[layer].reshape(FF // HIDDEN, 1, HIDDEN), mix_weights, 0,
        )
        outputs.append(result_low)
        kept.append(
            (
                state, first_norm, second_norm, taps, lane_bias, normed, projected, gate_out,
                gate_in, values, signal, window, carried, mixer, middle, second, activated, slope,
            )
        )
        state = result

    grad = out_grad
    owned, owned_ff = {}, {}
    ff_columns = 2 * FF
    shared = None
    small = [None] * LAYERS

    def share(part):
        return lax.psum_scatter(
            part.reshape(tensor_count * D, -1), owners, scatter_dimension=0, tiled=True
        )

    for layer in reversed(range(LAYERS)):
        joint = paired and layer == LAYERS - 1
        mix_columns = 4 * LANES * gathered[layer][1] + (ff_columns if joint else 0)
        mix_first = ff_columns // (4 * LANES) if joint else 0
        (
            state, first_norm, second_norm, taps, lane_bias, normed, projected, gate_out,
            gate_in, values, signal, window, carried, mixer, middle, second, activated, slope,
        ) = kept[layer]
        mix_weights, mix_per, ff_weights = gathered[layer]
        inner, filter_back, kernel_spectra = filters[layer]
        middle_grad, middle_low, ff_grad, up_bias_grad, ff_sums = ff_backward(
            0, place, grad, second, middle, second_norm, activated, slope, ff_weights, hidden_per,
            shared,
        )
        carried_grad, gate_grad, conv_bias_grad = gates_backward(
            middle_low, mix_weights, 0, mix_per, gate_out, carried, signal
        )
        ahead = [from_after(carried_grad, hop) for hop in range(1, hops + 1)]
        kernel_grad = kernel_backward(table, window, carried_grad, rows, tables)
        shaped = kernel_grad * modulation
        filter_out_grad = jnp.dot(jnp.transpose(inner), shaped, precision=highest)
        inner_grad = jnp.dot(shaped, jnp.transpose(filter_out[layer]), precision=highest)
        filter_grads = filter_back(inner_grad)
        ahead, filter_grads, filter_out_grad, owned_ff = lax.optimization_barrier(
            (ahead, filter_grads, filter_out_grad, owned_ff)
        )
        grads_window = jnp.concatenate([carried_grad] + ahead + [blank])
        gate_in_grad, values_grad = signal_backward(
            table, grads_window, kernel_spectra, values, gate_in, lane_bias, rows, hops, tables
        )
        mixed_grads = (gate_grad, gate_in_grad, values_grad)
        after = from_after(jnp.stack([part[:HALO] for part in mixed_grads]))
        grad, grad_low, in_bias_grad, taps_grad, in_sums, *mix_grad = in_backward(
            0 if joint else split, place, mixed_grads, after, age, projected, taps, normed, middle_low, mixer,
            mix_weights, 0, mix_per, state, middle_grad, first_norm, mix_columns, mix_first,
        )

        if len(mix_grad) == 1:
            mix_grad = mix_grad[0]
        if not paired:
            ins, out, up, down = part_columns(mix_grad, ff_grad, per, hidden_per)

            def by_owner(piece):
                piece = piece.reshape(D, tensor_count, -1)
                return jnp.transpose(piece, (1, 0, 2))

            mix_grad, ff_grad = join_columns(
                [by_owner(k) for k in ins], by_owner(out), by_owner(up), by_owner(down), 1, 1
            )

        if not paired:
            owned[layer], owned_ff[layer] = share(mix_grad), share(ff_grad)
        elif layer == LAYERS - 1:
            owned_ff[layer] = reduce_rows(ff_grad, [ff_columns])[0]
            shared = mix_grad
        else:
            owned_ff[layer], owned[layer + 1] = reduce_rows(ff_grad, [ff_columns, 4 * D])
            last_grads = mix_grad

        ff_sums = jnp.sum(ff_sums, axis=1)
        in_sums = jnp.sum(in_sums, axis=1)
        small[layer] = (
            from_block(in_bias_grad)[0],
            from_block(taps_grad),
            *filter_grads,
            filter_out_grad,
            conv_bias_grad.reshape(D),
            jnp.stack([in_sums[0], ff_sums[1]]),
            jnp.stack([in_sums[1], ff_sums[2]]),
            jnp.stack([ff_sums[3], ff_sums[0]]),
            up_bias_grad.reshape(FF),
        )

    narrow = range(2, 6)
    filter_size = filter_first.shape[2]

    def as_rows(layer):
        thin = jnp.concatenate([small[layer][k].reshape(-1, filter_size) for k in narrow])
        thin = jnp.pad(thin, ((0, -thin.shape[0] % (D // filter_size)), (0, 0)))
        wide = [small[layer][k].reshape(-1, D) for k in range(12) if k not in narrow]
        return wide + [thin.reshape(-1, D)]

    blocks = [as_rows(layer) for layer in range(LAYERS)]
    flat = jnp.concatenate([block.astype(bf16) for part in blocks for block in part])
    filled = flat.shape[0]
    flat = jnp.pad(flat, ((0, -filled % 16), (0, 0)))
    if paired:
        keep, send = last_grads
        total = (keep.astype(f32) + swap_core(send).astype(f32)).astype(bf16)
        flat, _ = lax.optimization_barrier((flat, total))
        beside = (owned_ff[0], owned[1])
        owned[0], (owned_ff[0], owned[1]) = reduce_plane(total, beside)
    flat = reduce_all(flat)
    found = [[None] * 12 for _ in range(LAYERS)]
    offset = 0
    for layer in range(LAYERS):
        pieces = []
        for block in blocks[layer]:
            pieces.append(flat[offset : offset + block.shape[0]])
            offset += block.shape[0]
        thin = pieces[-1].reshape(-1, filter_size)
        at = 0
        for k in range(12):
            like = small[layer][k]
            if k in narrow:
                count = like.size // filter_size
                found[layer][k] = thin[at : at + count].reshape(like.shape)
                at += count
            else:
                found[layer][k] = pieces[k if k < 2 else k - 4].reshape(like.shape)
    summed = [jnp.stack([found[layer][k] for layer in range(LAYERS)]) for k in range(12)]

    in_owned, out_owned, up_owned, down_owned = [], [], [], []
    for layer in range(LAYERS):
        ins, out, up, down = part_columns(
            owned[layer].astype(f32), owned_ff[layer].astype(f32), local_mix, local_ff
        )
        in_owned.append(jnp.stack(ins))
        out_owned.append(jnp.transpose(out))
        up_owned.append(up)
        down_owned.append(jnp.transpose(down))
    return (
        outputs[0],
        outputs[1],
        grad_low,
        jnp.stack(in_owned),
        jnp.stack(out_owned),
        jnp.stack(up_owned),
        jnp.stack(down_owned),
        *summed,
    )


def solution(mesh):
    groups, tensors = mesh.shape["dp"], mesh.shape["tensor"]
    cores = 2 if groups % 2 == 0 else 1
    fine = jax.sharding.Mesh(
        mesh.devices.reshape(groups // cores, cores, tensors), ("chip", "core", "tensor")
    )
    dp = ("chip", "core")
    rows = P(("chip", "core", "tensor"), None)
    weights = (
        P(None, None, dp, "tensor"),
        P(None, "tensor", dp),
        P(None, dp, "tensor"),
        P(None, "tensor", dp),
    )
    return jax.shard_map(
        shards,
        mesh=fine,
        in_specs=(rows, rows, P(), P(), *weights) + (P(),) * 12,
        out_specs=(rows, rows, rows, *weights) + (P(),) * 12,
        check_vma=False,
    )
```
